32 devices in a mesh: grp: 8 (over z, x), tp: 4 (over y, core).
Axes of the slice: x: 2, y: 2, z: 4, core: 2. Of those that a mesh axis runs over, the one named last changes fastest.
Arguments:
- enc_in: bfloat16 [8, 1024, 1536], P('grp', 'tp'), may hold values from -36 to 36
- dec_in: bfloat16 [8, 576, 1536], P('grp', 'tp'), may hold values from -36 to 36
- dec_cot: bfloat16 [8, 576, 1536], P('grp', 'tp'), may hold values from -6 to 6
- enc_seg: int32 [8, 1, 1024], P('grp'), may hold values from 0 to 3, as said below
- dec_seg: int32 [8, 3, 192], P('grp'), may hold values from 0 to 3, as said below
- enc_norm1: bfloat16 [1536], P('grp'), may hold values from 0.25 to 1.75
- enc_wq: bfloat16 [1536, 768], P('grp', 'tp'), may hold values from -0.0625 to 0.0625
- enc_wk: bfloat16 [1536, 768], P('grp', 'tp'), may hold values from -0.0625 to 0.0625
- enc_wv: bfloat16 [1536, 768], P('grp', 'tp'), may hold values from -0.15625 to 0.15625
- enc_wo: bfloat16 [768, 1536], P('tp', 'grp'), may hold values from -1.75 to 1.75
- enc_table: bfloat16 [32, 12], P(None, 'tp'), may hold values from -4 to 4
- enc_norm2: bfloat16 [1536], P('grp'), may hold values from 0.25 to 1.75
- enc_wgate: bfloat16 [1536, 3968], P('grp', 'tp'), may hold values from -0.15625 to 0.15625
- enc_wup: bfloat16 [1536, 3968], P('grp', 'tp'), may hold values from -0.15625 to 0.15625
- enc_wdown: bfloat16 [3968, 1536], P('tp', 'grp'), may hold values from -0.09375 to 0.09375
- enc_normf: bfloat16 [1536], P('grp'), may hold values from 0.25 to 1.75
- dec_norm1: bfloat16 [1536], P('grp'), may hold values from 0.25 to 1.75
- dec_wq: bfloat16 [1536, 768], P('grp', 'tp'), may hold values from -0.0625 to 0.0625
- dec_wk: bfloat16 [1536, 768], P('grp', 'tp'), may hold values from -0.0625 to 0.0625
- dec_wv: bfloat16 [1536, 768], P('grp', 'tp'), may hold values from -0.15625 to 0.15625
- dec_wo: bfloat16 [768, 1536], P('tp', 'grp'), may hold values from -0.875 to 0.875
- dec_table: bfloat16 [32, 12], P(None, 'tp'), may hold values from -4 to 4
- dec_norm2: bfloat16 [1536], P('grp'), may hold values from 0.25 to 1.75
- cross_wq: bfloat16 [1536, 768], P('grp', 'tp'), may hold values from -0.0625 to 0.0625
- cross_wk: bfloat16 [1536, 768], P('grp', 'tp'), may hold values from -0.0625 to 0.0625
- cross_wv: bfloat16 [1536, 768], P('grp', 'tp'), may hold values from -0.15625 to 0.15625
- cross_wo: bfloat16 [768, 1536], P('tp', 'grp'), may hold values from -1.75 to 1.75
- dec_norm3: bfloat16 [1536], P('grp'), may hold values from 0.25 to 1.75
- dec_wgate: bfloat16 [1536, 3968], P('grp', 'tp'), may hold values from -0.15625 to 0.15625
- dec_wup: bfloat16 [1536, 3968], P('grp', 'tp'), may hold values from -0.15625 to 0.15625
- dec_wdown: bfloat16 [3968, 1536], P('tp', 'grp'), may hold values from -0.09375 to 0.09375
Outputs:
- dec_out: bfloat16 [8, 576, 1536], P('grp', 'tp')
- enc_grad: bfloat16 [8, 1024, 1536], P('grp', 'tp')
- dec_grad: bfloat16 [8, 576, 1536], P('grp', 'tp')
- grad_enc_norm1: float32 [1536], P('grp')
- grad_enc_wq: float32 [1536, 768], P('grp', 'tp')
- grad_enc_wk: float32 [1536, 768], P('grp', 'tp')
- grad_enc_wv: float32 [1536, 768], P('grp', 'tp')
- grad_enc_wo: float32 [768, 1536], P('tp', 'grp')
- grad_enc_table: float32 [32, 12], P(None, 'tp')
- grad_enc_norm2: float32 [1536], P('grp')
- grad_enc_wgate: float32 [1536, 3968], P('grp', 'tp')
- grad_enc_wup: float32 [1536, 3968], P('grp', 'tp')
- grad_enc_wdown: float32 [3968, 1536], P('tp', 'grp')
- grad_enc_normf: float32 [1536], P('grp')
- grad_dec_norm1: float32 [1536], P('grp')
- grad_dec_wq: float32 [1536, 768], P('grp', 'tp')
- grad_dec_wk: float32 [1536, 768], P('grp', 'tp')
- grad_dec_wv: float32 [1536, 768], P('grp', 'tp')
- grad_dec_wo: float32 [768, 1536], P('tp', 'grp')
- grad_dec_table: float32 [32, 12], P(None, 'tp')
- grad_dec_norm2: float32 [1536], P('grp')
- grad_cross_wq: float32 [1536, 768], P('grp', 'tp')
- grad_cross_wk: float32 [1536, 768], P('grp', 'tp')
- grad_cross_wv: float32 [1536, 768], P('grp', 'tp')
- grad_cross_wo: float32 [768, 1536], P('tp', 'grp')
- grad_dec_norm3: float32 [1536], P('grp')
- grad_dec_wgate: float32 [1536, 3968], P('grp', 'tp')
- grad_dec_wup: float32 [1536, 3968], P('grp', 'tp')
- grad_dec_wdown: float32 [3968, 1536], P('tp', 'grp')
The draws below stay inside these ranges and needn't reach their ends.
Inputs may be any that keep to these rules, and one draw needn't show every extreme that they name: `enc_seg`: in each row the ids never fall, and each of 0 to 3 occurs. `dec_seg`: in each row the ids never fall, and each of 0 to 3 occurs.
All inputs are finite; a program needn't handle non-finite values.
Results may differ from the reference program's by a relative error of at most 0.04.
Values may be sent and summed in bfloat16 or wider, within the bound.
No kernel may reach another device: no remote copies, remote signals or barrier semaphores. Data moves between devices by JAX's collectives and lax.ppermute only.
A program may use at most 640 MiB of HBM per device.

```python
import math
import jax
import jax.numpy as jnp
import numpy as np
from jax import lax

D = 1536
HEADS = 12
HEAD_DIM = 64
FF = 3968
BUCKETS = 32
MAX_DIST = 128
ENC_LEN = 1024
DEC_LEN = 192
NSEG = 4
ROWS = 1
INNER = 768
N_GRP = 8


def scaled_field(key, shape_dims):
    entry_key, row_key, col_key = jax.random.split(key, 3)
    entries = jnp.clip(jax.random.normal(entry_key, shape_dims, jnp.float32), -4.0, 4.0)
    row_scale = 0.3 * jnp.exp(jax.random.uniform(row_key, shape_dims[:-1] + (1,), jnp.float32, 0.0, math.log(10.0)))
    col_scale = 0.3 * jnp.exp(jax.random.uniform(col_key, (shape_dims[-1],), jnp.float32, 0.0, math.log(10.0)))
    return (entries * row_scale * col_scale).astype(jnp.bfloat16)


def segment_ids(key, rows_count, length):
    positions = jnp.arange(1, length)
    allowed = (positions < length // 4) | (positions > 3 * length // 4)
    noise = jax.random.randint(key, (rows_count, length - 1), 0, 2 ** 19)
    scores = noise * length + positions[None, :] + jnp.where(allowed, 0, 2 ** 30)[None, :]
    cuts = jnp.argsort(scores, axis=1)[:, :NSEG - 1] + 1
    segment = jnp.sum(jnp.arange(length)[None, :, None] >= cuts[:, None, :], axis=2)
    return segment.astype(jnp.int32)


def draw_enc_in(key, part):
    return scaled_field(key, (N_GRP, ROWS * ENC_LEN, D))


def draw_dec_in(key, part):
    return scaled_field(key, (N_GRP, 3 * ROWS * DEC_LEN, D))


def draw_enc_seg(key, part):
    return segment_ids(key, N_GRP * ROWS, ENC_LEN).reshape(N_GRP, ROWS, ENC_LEN)


def draw_dec_seg(key, part):
    return segment_ids(key, N_GRP * 3 * ROWS, DEC_LEN).reshape(N_GRP, 3 * ROWS, DEC_LEN)


def steps_of(key, dims, pieces, smallest, top_value):
    level = 1.0
    for position, parts in pieces:
        heights = jax.random.uniform(jax.random.fold_in(jax.random.fold_in(key, 6), position), (parts,), jnp.float32, smallest / len(pieces), top_value / len(pieces))
        level = level * jnp.repeat(jnp.exp(heights), dims[position] // parts).reshape((-1,) + (1,) * (len(dims) - 1 - position))
    return level


def centred(rng, shape, scale, bound, shards=(), kind=jnp.bfloat16):
    values = scale * jax.random.normal(rng, shape, jnp.float32)
    if shards:
        values = values * steps_of(rng, shape, shards, -0.22, 0.18)
    return jnp.clip(values, -bound, bound).astype(kind)


def setup_inputs(seed: int = 0) -> dict:
    keys = jax.random.split(jax.random.key(seed), 32)
    return {
        "enc_in": draw_enc_in(jax.random.fold_in(keys[31], 71), 0),
        "dec_in": draw_dec_in(jax.random.fold_in(keys[31], 71), 0),
        "dec_cot": centred(keys[2], (N_GRP, 3 * ROWS * DEC_LEN, D), 1.0, 6.0, ((0, 8), (1, 4))),
        "enc_seg": draw_enc_seg(jax.random.fold_in(keys[31], 71), 0),
        "dec_seg": draw_dec_seg(jax.random.fold_in(keys[31], 71), 0),
        "enc_norm1": jnp.clip(1.0 + 0.15 * jax.random.normal(keys[5], (D,), jnp.float32), 0.25, 1.75).astype(jnp.bfloat16),
        "enc_wq": centred(keys[6], (D, INNER), (6 * D) ** -0.5, 0.0625, ((0, 8), (1, 4))),
        "enc_wk": centred(keys[7], (D, INNER), (6 * D) ** -0.5, 0.0625, ((0, 8), (1, 4))),
        "enc_wv": centred(keys[8], (D, INNER), D ** -0.5, 0.15625, ((0, 8), (1, 4))),
        "enc_wo": centred(keys[9], (INNER, D), (max(INNER // 64, 1)) ** -0.5, 1.75, ((0, 4), (1, 8))),
        "enc_table": centred(keys[10], (BUCKETS, HEADS), 1.0, 4.0, ((1, 4),)),
        "enc_norm2": jnp.clip(1.0 + 0.15 * jax.random.normal(keys[11], (D,), jnp.float32), 0.25, 1.75).astype(jnp.bfloat16),
        "enc_wgate": centred(keys[12], (D, FF), D ** -0.5, 0.15625, ((0, 8), (1, 4))),
        "enc_wup": centred(keys[13], (D, FF), D ** -0.5, 0.15625, ((0, 8), (1, 4))),
        "enc_wdown": centred(keys[14], (FF, D), FF ** -0.5, 0.09375, ((0, 4), (1, 8))),
        "enc_normf": jnp.clip(1.0 + 0.15 * jax.random.normal(keys[15], (D,), jnp.float32), 0.25, 1.75).astype(jnp.bfloat16),
        "dec_norm1": jnp.clip(1.0 + 0.15 * jax.random.normal(keys[16], (D,), jnp.float32), 0.25, 1.75).astype(jnp.bfloat16),
        "dec_wq": centred(keys[17], (D, INNER), (6 * D) ** -0.5, 0.0625, ((0, 8), (1, 4))),
        "dec_wk": centred(keys[18], (D, INNER), (6 * D) ** -0.5, 0.0625, ((0, 8), (1, 4))),
        "dec_wv": centred(keys[19], (D, INNER), D ** -0.5, 0.15625, ((0, 8), (1, 4))),
        "dec_wo": centred(keys[20], (INNER, D), (max(INNER // 16, 1)) ** -0.5, 0.875, ((0, 4), (1, 8))),
        "dec_table": centred(keys[21], (BUCKETS, HEADS), 1.0, 4.0, ((1, 4),)),
        "dec_norm2": jnp.clip(1.0 + 0.15 * jax.random.normal(keys[22], (D,), jnp.float32), 0.25, 1.75).astype(jnp.bfloat16),
        "cross_wq": centred(keys[23], (D, INNER), (6 * D) ** -0.5, 0.0625, ((0, 8), (1, 4))),
        "cross_wk": centred(keys[24], (D, INNER), (6 * D) ** -0.5, 0.0625, ((0, 8), (1, 4))),
        "cross_wv": centred(keys[25], (D, INNER), D ** -0.5, 0.15625, ((0, 8), (1, 4))),
        "cross_wo": centred(keys[26], (INNER, D), (max(INNER // 64, 1)) ** -0.5, 1.75, ((0, 4), (1, 8))),
        "dec_norm3": jnp.clip(1.0 + 0.15 * jax.random.normal(keys[27], (D,), jnp.float32), 0.25, 1.75).astype(jnp.bfloat16),
        "dec_wgate": centred(keys[28], (D, FF), D ** -0.5, 0.15625, ((0, 8), (1, 4))),
        "dec_wup": centred(keys[29], (D, FF), D ** -0.5, 0.15625, ((0, 8), (1, 4))),
        "dec_wdown": centred(keys[30], (FF, D), FF ** -0.5, 0.09375, ((0, 4), (1, 8))),
    }


EPSILON = 1e-06
NEG_FILL = -1e+30
PRECISE = lax.Precision.HIGHEST

@jax.custom_vjp
def low(v):
    return lax.optimization_barrier(v.astype(jnp.bfloat16)).astype(jnp.float32)

@jax.custom_vjp
def low_back(v):
    return v

def low_keep(v):
    return (low(v), None)

def low_pass(kept, grad):
    return (grad,)

def back_keep(v):
    return (v, None)

def back_low(kept, grad):
    return (low(grad),)
low.defvjp(low_keep, low_pass)
low_back.defvjp(back_keep, back_low)

def bucket_of(relative, two_sided):
    bucket_count = BUCKETS
    shifted = relative * 0
    if two_sided:
        bucket_count = bucket_count // 2
        shifted = shifted + (relative > 0) * bucket_count
        distance = np.abs(relative)
    else:
        distance = np.maximum(-relative, 0)
    exact_span = bucket_count // 2
    log_ratio = np.log(np.maximum(distance, 1) / exact_span) / np.log(MAX_DIST / exact_span)
    farther = np.minimum(exact_span + np.floor(log_ratio * (bucket_count - exact_span) + 1e-09).astype(np.int32), bucket_count - 1)
    return (shifted + np.where(distance < exact_span, distance, farther)).astype(np.int32)

def rms_scale(hidden, gain_vec):
    return hidden * lax.rsqrt(lax.optimization_barrier(jnp.mean(hidden * hidden, axis=-1, keepdims=True)) + EPSILON) * gain_vec

def matmul(left, right):
    return jnp.dot(left, right, precision=PRECISE)

def heads_from(normed, weight):
    mixed = low_back(low(matmul(normed, weight)))
    return mixed.reshape(mixed.shape[0], -1, HEAD_DIM)

def attend(queries, key_rows, value_rows, pos_bias, allowed):
    scores = low_back(jnp.einsum('qhd,khd->hqk', queries, key_rows, precision=PRECISE))
    if pos_bias is not None:
        scores = scores + pos_bias
    scores = jnp.where(allowed[None], scores, NEG_FILL)
    row_peak = lax.optimization_barrier(jnp.max(scores, axis=-1, keepdims=True))
    exponent = jnp.exp(scores - row_peak)
    weights_bf = low(exponent / lax.optimization_barrier(jnp.sum(exponent, axis=-1, keepdims=True)))
    attended = jnp.einsum('hqk,khd->qhd', weights_bf, value_rows, precision=PRECISE)
    return low_back(low(attended)).reshape(queries.shape[0], -1)

def self_block(hidden, gain_vec, w_query, w_key, w_value, w_out, table, row_ids, two_sided):
    normed = low(rms_scale(hidden, gain_vec))
    length = hidden.shape[0]
    relative = np.arange(length)[None, :] - np.arange(length)[:, None]
    pos_bias = jnp.transpose(table[bucket_of(relative, two_sided)], (2, 0, 1))
    allowed = row_ids[:, None] == row_ids[None, :]
    if not two_sided:
        allowed = allowed & jnp.asarray(np.tril(np.ones((length, length), dtype=np.bool_)))
    attended = attend(heads_from(normed, w_query), heads_from(normed, w_key), heads_from(normed, w_value), pos_bias, allowed)
    return hidden + low_back(matmul(attended, w_out))

def cross_block(hidden, gain_vec, w_query, w_key, w_value, w_out, row_ids, memory, memory_ids):
    normed = low(rms_scale(hidden, gain_vec))
    allowed = row_ids[:, None] == memory_ids[None, :]
    attended = attend(heads_from(normed, w_query), heads_from(memory, w_key), heads_from(memory, w_value), None, allowed)
    return hidden + low_back(matmul(attended, w_out))

def ff_block(hidden, gain_vec, w_gate, w_up, w_down):
    normed = low(rms_scale(hidden, gain_vec))
    gate_val = low_back(matmul(normed, w_gate))
    up_val = low_back(matmul(normed, w_up))
    activated = low(jax.nn.gelu(gate_val, approximate=True) * up_val)
    return hidden + low_back(matmul(activated, w_down))

def encoder_row(params, row_data, row_ids):
    hidden = self_block(row_data, params[0], params[1], params[2], params[3], params[4], params[5], row_ids, True)
    hidden = ff_block(hidden, params[6], params[7], params[8], params[9])
    return low_back(low(rms_scale(hidden, params[10])))

def decoder_row(params, row_data, row_ids, memory, memory_ids):
    hidden = self_block(row_data, params[11], params[12], params[13], params[14], params[15], params[16], row_ids, False)
    hidden = cross_block(hidden, params[17], params[18], params[19], params[20], params[21], row_ids, memory, memory_ids)
    return ff_block(hidden, params[22], params[23], params[24], params[25])

def whole_forward(enc_all, dec_all, params, enc_ids_all, dec_ids_all):
    enc_slots = 3 * N_GRP // 4
    dec_slots = N_GRP // 4
    enc_rows = enc_all[:enc_slots].reshape(-1, ENC_LEN, D)
    enc_ids = enc_ids_all[:enc_slots].reshape(-1, ENC_LEN)

    def encode_one(operands):
        return encoder_row(params, operands[0], operands[1])
    memory = lax.map(jax.checkpoint(encode_one), (enc_rows, enc_ids))
    memory = memory.reshape(3, dec_slots, ROWS, ENC_LEN, D).transpose(1, 0, 2, 3, 4).reshape(-1, ENC_LEN, D)
    memory_ids = enc_ids.reshape(3, dec_slots, ROWS, ENC_LEN).transpose(1, 0, 2, 3).reshape(-1, ENC_LEN)
    dec_rows = dec_all[enc_slots:].reshape(-1, DEC_LEN, D)
    dec_ids = dec_ids_all[enc_slots:].reshape(-1, DEC_LEN)

    def decode_one(operands):
        return decoder_row(params, operands[0], operands[1], operands[2], operands[3])
    return lax.map(jax.checkpoint(decode_one), (dec_rows, dec_ids, memory, memory_ids))

def reference(enc_in, dec_in, dec_cot, enc_seg, dec_seg, enc_norm1, enc_wq, enc_wk, enc_wv, enc_wo, enc_table, enc_norm2, enc_wgate, enc_wup, enc_wdown, enc_normf, dec_norm1, dec_wq, dec_wk, dec_wv, dec_wo, dec_table, dec_norm2, cross_wq, cross_wk, cross_wv, cross_wo, dec_norm3, dec_wgate, dec_wup, dec_wdown):
    params = tuple((weight.astype(jnp.float32) for weight in (enc_norm1, enc_wq, enc_wk, enc_wv, enc_wo, enc_table, enc_norm2, enc_wgate, enc_wup, enc_wdown, enc_normf, dec_norm1, dec_wq, dec_wk, dec_wv, dec_wo, dec_table, dec_norm2, cross_wq, cross_wk, cross_wv, cross_wo, dec_norm3, dec_wgate, dec_wup, dec_wdown)))
    enc_slots = 3 * N_GRP // 4

    def forward_fn(enc_all, dec_all, weights_all):
        return whole_forward(enc_all, dec_all, weights_all, enc_seg, dec_seg)
    decoded, pullback = jax.vjp(forward_fn, enc_in.astype(jnp.float32), dec_in.astype(jnp.float32), params)
    cotangent = dec_cot[enc_slots:].astype(jnp.float32).reshape(decoded.shape)
    grad_enc, grad_dec, grad_params = pullback(cotangent)
    dec_out = jnp.concatenate([jnp.zeros((enc_slots,) + dec_in.shape[1:], jnp.float32), decoded.reshape((N_GRP - enc_slots,) + dec_in.shape[1:])], axis=0).astype(jnp.bfloat16)
    return (dec_out, grad_enc.astype(jnp.bfloat16), grad_dec.astype(jnp.bfloat16), grad_params[0], grad_params[1], grad_params[2], grad_params[3], grad_params[4], grad_params[5], grad_params[6], grad_params[7], grad_params[8], grad_params[9], grad_params[10], grad_params[11], grad_params[12], grad_params[13], grad_params[14], grad_params[15], grad_params[16], grad_params[17], grad_params[18], grad_params[19], grad_params[20], grad_params[21], grad_params[22], grad_params[23], grad_params[24], grad_params[25])
```

```python
from functools import partial

import jax
import jax.numpy as jnp
import numpy as np
from jax import lax
from jax.experimental import pallas as pl
from jax.experimental.pallas import tpu as pltpu
from jax.sharding import PartitionSpec as P

HEAD_DIM = 64
BUCKETS = 32
MAX_DIST = 128
DEC_LEN = 192
EPSILON = 1e-06
NEG_FILL = -1e30
QB = 128
F32 = jnp.float32
BF16 = jnp.bfloat16


def bucket_of(relative, two_sided):
    bucket_count = BUCKETS
    shifted = relative * 0
    if two_sided:
        bucket_count = bucket_count // 2
        shifted = shifted + (relative > 0) * bucket_count
        distance = np.abs(relative)
    else:
        distance = np.maximum(-relative, 0)
    exact_span = bucket_count // 2
    log_ratio = np.log(np.maximum(distance, 1) / exact_span) / np.log(MAX_DIST / exact_span)
    farther = np.minimum(
        exact_span + np.floor(log_ratio * (bucket_count - exact_span) + 1e-09).astype(np.int32),
        bucket_count - 1,
    )
    return (shifted + np.where(distance < exact_span, distance, farther)).astype(np.int32)


def one_hot_blocks(relative, two_sided):
    return np.eye(BUCKETS, dtype=np.float32)[:, bucket_of(relative, two_sided).reshape(-1)]


def enc_relative():
    return np.arange(-2 * QB, 3 * QB)[:, None] - np.arange(QB)[None, :]


def dec_relative():
    return np.arange(DEC_LEN)[:, None] - np.arange(DEC_LEN)[None, :]


def dot(left, right, dims):
    return lax.dot_general(left, right, (dims, ((), ())), preferred_element_type=F32)


NN = ((1,), (0,))
NT = ((1,), (1,))
TN = ((0,), (0,))


def block_of(place, tp):
    wide = place // 2
    swapped = (wide % 2) * 2 + wide // 2
    return (swapped ^ tp) * 2 + place % 2


def scores_t(head, cfg, keys, queries, bias_ref, same, place, tp):
    lanes = slice(head * HEAD_DIM, (head + 1) * HEAD_DIM)
    scores = dot(keys[:, lanes], queries[:, lanes], NT)
    if cfg["bias"] == "blocks":
        mine = block_of(place, tp)
        parts = []
        for kb in range(keys.shape[0] // QB):
            step = jnp.clip(block_of(kb, tp) - mine, -2, 2) + 2
            parts.append(bias_ref[head, step])
        scores = scores + jnp.concatenate(parts, axis=0)
    elif cfg["bias"] == "full":
        scores = scores + bias_ref[head]
    return jnp.where(same, scores, NEG_FILL)


def allowed_t(cfg, idk_ref, idq_ref):
    same = idk_ref[...] == idq_ref[0]
    if cfg["causal"]:
        key_pos = lax.broadcasted_iota(jnp.int32, same.shape, 0)
        query_pos = lax.broadcasted_iota(jnp.int32, same.shape, 1)
        same = same & (key_pos <= query_pos)
    return same


def forward_kernel(cfg, tp_ref, q_ref, kv_ref, idk_ref, idq_ref, *rest):
    if cfg["bias"]:
        bias_ref, out_ref, lse_ref, vt_ref = rest
    else:
        bias_ref, (out_ref, lse_ref, vt_ref) = None, rest
    heads = cfg["heads"]
    width = heads * HEAD_DIM
    place = pl.program_id(0)
    keys = kv_ref[:, cfg["k"] : cfg["k"] + width]

    def fill():
        vt_ref[...] = kv_ref[:, cfg["v"] : cfg["v"] + width].T

    if cfg["follow"]:
        fill()
    else:
        pl.when(place == 0)(fill)
    queries = q_ref[:, :width]
    same = allowed_t(cfg, idk_ref, idq_ref)
    outs = []
    for head in range(heads):
        scores = scores_t(head, cfg, keys, queries, bias_ref, same, place, tp_ref[0])
        peak = jnp.max(scores, axis=0, keepdims=True)
        exponent = jnp.exp(scores - peak)
        total = jnp.sum(exponent, axis=0, keepdims=True)
        weights = (exponent * (1.0 / total)).astype(BF16)
        outs.append(dot(vt_ref[head * HEAD_DIM : (head + 1) * HEAD_DIM, :], weights, NN))
        lse_ref[0, head : head + 1, :] = peak + jnp.log(total)
    out_ref[...] = jnp.concatenate(outs, axis=0).T.astype(BF16)


def backward_kernel(cfg, tp_ref, q_ref, kv_ref, idk_ref, idq_ref, *rest):
    if cfg["bias"]:
        bias_ref, lse_ref, go_ref, gq_ref, gkv_ref, gb_ref, kt_ref, acc_ref = rest
    else:
        bias_ref, gb_ref = None, None
        lse_ref, go_ref, gq_ref, gkv_ref, kt_ref, acc_ref = rest
    heads = cfg["heads"]
    width = heads * HEAD_DIM
    place = pl.program_id(0)
    keys = kv_ref[:, cfg["k"] : cfg["k"] + width]
    values = kv_ref[:, cfg["v"] : cfg["v"] + width]

    def clear():
        kt_ref[...] = kv_ref[:, cfg["k"] : cfg["k"] + width].T
        acc_ref[...] = jnp.zeros_like(acc_ref)

    def clear_bias():
        if gb_ref is not None:
            gb_ref[...] = jnp.zeros_like(gb_ref)

    pl.when(place == 0)(clear_bias)
    if cfg["follow"]:
        clear()
    else:
        pl.when(place == 0)(clear)
    queries = q_ref[:, :width]
    grad_out = go_ref[...]
    same = allowed_t(cfg, idk_ref, idq_ref)
    grads = []
    for head in range(heads):
        lanes = slice(head * HEAD_DIM, (head + 1) * HEAD_DIM)
        scores = scores_t(head, cfg, keys, queries, bias_ref, same, place, tp_ref[0])
        weights = jnp.exp(scores - lse_ref[0, head : head + 1, :])
        grad_weights = dot(values[:, lanes], grad_out[:, lanes], NT)
        delta = jnp.sum(grad_weights * weights, axis=0, keepdims=True)
        grad_scores = weights * (grad_weights - delta)
        if cfg["bias"] == "blocks":
            mine = block_of(place, tp_ref[0])
            for kb in range(keys.shape[0] // QB):
                step = jnp.clip(block_of(kb, tp_ref[0]) - mine, -2, 2) + 2
                gb_ref[head, step] += grad_scores[kb * QB : (kb + 1) * QB]
        elif cfg["bias"] == "full":
            gb_ref[head] += grad_scores
        scores_bf = grad_scores.astype(BF16)
        acc_ref[head] += dot(scores_bf, queries[:, lanes], NN)
        acc_ref[heads + head] += dot(weights.astype(BF16), grad_out[:, lanes], NN)
        grads.append(dot(kt_ref[lanes, :], scores_bf, NN))
    gq_ref[...] = jnp.concatenate(grads, axis=0).T.astype(BF16)

    def finish():
        gkv_ref[...] = jnp.concatenate(
            [acc_ref[k].astype(BF16) for k in range(2 * heads)], axis=1
        )

    if cfg["follow"]:
        finish()
    else:
        pl.when(place == pl.num_programs(0) - 1)(finish)


def attention_specs(cfg, q_cols, kv_cols, bias):
    bq, bk = cfg["bq"], cfg["bk"]
    follow = cfg["follow"]
    specs = [
        pl.BlockSpec((bq, q_cols), lambda i, s: (i, 0)),
        pl.BlockSpec((bk, kv_cols), (lambda i, s: (i, 0)) if follow else (lambda i, s: (0, 0))),
        pl.BlockSpec((bk, bq), (lambda i, s: (i, 0)) if follow else (lambda i, s: (0, 0))),
        pl.BlockSpec((1, 1, bq), lambda i, s: (i, 0, 0)),
    ]
    if bias is not None:
        rank = bias.ndim
        specs.append(pl.BlockSpec(bias.shape, lambda i, s: (0,) * rank))
    return specs


def attention_forward(cfg, tp, q, kv, idk, idq, bias=None):
    heads, bq, bk, steps = cfg["heads"], cfg["bq"], cfg["bk"], cfg["steps"]
    width = heads * HEAD_DIM
    extra = () if bias is None else (bias,)
    return pl.pallas_call(
        partial(forward_kernel, cfg),
        out_shape=(
            jax.ShapeDtypeStruct((steps * bq, width), BF16),
            jax.ShapeDtypeStruct((steps, heads, bq), F32),
        ),
        grid_spec=pltpu.PrefetchScalarGridSpec(
            num_scalar_prefetch=1,
            grid=(steps,),
            in_specs=attention_specs(cfg, q.shape[1], kv.shape[1], bias),
            out_specs=(
                pl.BlockSpec((bq, width), lambda i, s: (i, 0)),
                pl.BlockSpec((1, heads, bq), lambda i, s: (i, 0, 0)),
            ),
            scratch_shapes=[pltpu.VMEM((width, bk), BF16)],
        ),
        compiler_params=pltpu.CompilerParams(vmem_limit_bytes=40 << 20),
        name=cfg["name"] + "_forward",
    )(tp, q, kv, idk, idq, *extra)


def attention_backward(cfg, tp, q, kv, idk, idq, lse, grad_out, bias=None):
    heads, bq, bk, steps = cfg["heads"], cfg["bq"], cfg["bk"], cfg["steps"]
    width = heads * HEAD_DIM
    follow = cfg["follow"]
    extra = () if bias is None else (bias,)
    out_shape = [
        jax.ShapeDtypeStruct((steps * bq, width), BF16),
        jax.ShapeDtypeStruct((steps * bk if follow else bk, 2 * width), BF16),
    ]
    out_specs = [
        pl.BlockSpec((bq, width), lambda i, s: (i, 0)),
        pl.BlockSpec((bk, 2 * width), (lambda i, s: (i, 0)) if follow else (lambda i, s: (0, 0))),
    ]
    if bias is not None:
        rank = bias.ndim
        out_shape.append(jax.ShapeDtypeStruct(bias.shape, F32))
        out_specs.append(pl.BlockSpec(bias.shape, lambda i, s: (0,) * rank))
    return pl.pallas_call(
        partial(backward_kernel, cfg),
        out_shape=tuple(out_shape),
        grid_spec=pltpu.PrefetchScalarGridSpec(
            num_scalar_prefetch=1,
            grid=(steps,),
            in_specs=attention_specs(cfg, q.shape[1], kv.shape[1], bias)
            + [
                pl.BlockSpec((1, heads, bq), lambda i, s: (i, 0, 0)),
                pl.BlockSpec((bq, width), lambda i, s: (i, 0)),
            ],
            out_specs=tuple(out_specs),
            scratch_shapes=[pltpu.VMEM((width, bk), BF16), pltpu.VMEM((2 * heads, bk, HEAD_DIM), F32)],
        ),
        compiler_params=pltpu.CompilerParams(vmem_limit_bytes=48 << 20),
        name=cfg["name"] + "_backward",
    )(tp, q, kv, idk, idq, *extra, lse, grad_out)


def rms_scale(hidden, gain_vec):
    return (
        hidden * lax.rsqrt(jnp.mean(hidden * hidden, axis=-1, keepdims=True) + EPSILON) * gain_vec
    )


def norm_backward(hidden, gain_vec, grad_out):
    rate = lax.rsqrt(jnp.mean(hidden * hidden, axis=-1, keepdims=True) + EPSILON)
    scaled = gain_vec * grad_out
    inner = jnp.mean(hidden * scaled, axis=-1, keepdims=True)
    grad_in = rate * scaled - hidden * (rate * rate * rate * inner)
    return grad_in, jnp.sum(grad_out * hidden * rate, axis=0)


def gelu(value):
    return jax.nn.gelu(value, approximate=True)


def gated(gate_val, up_val):
    return (gelu(gate_val) * up_val).astype(BF16)


def gated_back(gate_val, up_val, grad_hidden):
    activated, gelu_back = jax.vjp(gelu, gate_val)
    hidden_bf = (activated * up_val).astype(BF16)
    grad_gate = gelu_back(grad_hidden * up_val)[0].astype(BF16)
    grad_up = (grad_hidden * activated).astype(BF16)
    return hidden_bf, grad_gate, grad_up


SWAP_CORE = [(0, 1), (1, 0), (2, 3), (3, 2)]
SWAP_PAIR = [(0, 2), (2, 0), (1, 3), (3, 1)]


def core_swap(value):
    return lax.ppermute(value, "tp", SWAP_CORE)


def pair_swap(value):
    return lax.ppermute(value, "tp", SWAP_PAIR)


def gather_tokens(own):
    far = pair_swap(own)
    return jnp.concatenate([own, far, core_swap(own), core_swap(far)], axis=0)


def reduce_tokens(partial_bf):
    count = partial_bf.shape[0] // 4
    other = core_swap(partial_bf[2 * count :])
    half = partial_bf[: 2 * count].astype(F32) + other.astype(F32)
    far = pair_swap(half[count:].astype(BF16))
    return half[:count] + far.astype(F32)


class Groups:
    def __init__(self):
        self.count = lax.axis_size("grp")
        self.quarter = self.count // 4
        where = lax.axis_index("grp")
        self.where = where
        self.role = where // self.quarter
        self.place = where % self.quarter
        self.is_enc = self.role < 3
        self.peers = [
            [a * self.quarter + j for j in range(self.quarter)] for a in range(4)
        ]
        self.swap = [(i, i ^ 1) for i in range(self.count)]

    def shift(self, value, steps):
        hop = steps * self.quarter
        return lax.ppermute(
            value, "grp", [(i, (i + hop) % self.count) for i in range(self.count)]
        )

    def send(self, value, source, target):
        q = self.quarter
        return lax.ppermute(
            value, "grp", [(source * q + j, target * q + j) for j in range(q)]
        )

    def gather(self, enc, dec):
        own = jnp.where(self.is_enc, enc, dec)
        held = [own]
        for step in (1, 2, 3):
            target = (self.role + step) % 4
            held.append(self.shift(jnp.where(target < 3, enc, dec), step))
        full = jnp.zeros((4, self.quarter) + own.shape, own.dtype)
        for step, shard in enumerate(held):
            source = (self.role - step) % 4
            if self.quarter == 2:
                other = lax.ppermute(shard, "grp", self.swap)
                full = lax.dynamic_update_slice(
                    full, shard[None, None], (source, self.place, 0, 0)
                )
                full = lax.dynamic_update_slice(
                    full, other[None, None], (source, 1 - self.place, 0, 0)
                )
            else:
                group = lax.all_gather(shard, "grp", axis_index_groups=self.peers)
                full = lax.dynamic_update_slice(full, group[None], (source, 0, 0, 0))
        return full.reshape(-1, own.shape[1])

    def peer_sum(self, value):
        if self.quarter == 2:
            return value + lax.ppermute(value, "grp", self.swap)
        return lax.psum(value, "grp", axis_index_groups=self.peers)

    def role_sums(self, mine):
        enc_total, dec_total = 0.0, 0.0
        for step in range(4):
            target = (self.role + step) % 4
            block = lax.dynamic_index_in_dim(mine, target, 0, keepdims=False)
            if step:
                block = self.shift(block, step)
            block = block.astype(F32)
            source_enc = (self.role - step) % 4 < 3
            enc_total = enc_total + jnp.where(source_enc, block, 0.0)
            dec_total = dec_total + jnp.where(source_enc, 0.0, block)
        return enc_total, dec_total

    def scatter(self, grad_bf):
        rows = grad_bf.shape[0] // self.count
        blocks = grad_bf.reshape(4, self.quarter, rows, grad_bf.shape[1])
        if self.quarter == 2:
            away = lax.dynamic_index_in_dim(blocks, 1 - self.place, 1, keepdims=False)
            home = lax.dynamic_index_in_dim(blocks, self.place, 1, keepdims=False)
            arrived = lax.ppermute(away, "grp", self.swap)
            mine = (home.astype(F32) + arrived.astype(F32)).astype(BF16)
        else:
            mine = lax.psum_scatter(
                blocks, "grp", scatter_dimension=1, axis_index_groups=self.peers
            )
        return self.role_sums(mine)

    def all_role_sums(self, value):
        value = self.peer_sum(value)
        return self.role_sums(jnp.broadcast_to(value[None], (4,) + value.shape))


def pad_rows(value, count):
    return jnp.pad(value, ((0, count - value.shape[0]), (0, 0)))


class DecoderRows:
    def __init__(self, tp, count, stride):
        self.count, self.stride, self.tp = count, stride, tp

    @staticmethod
    def flip(index):
        return (index % 2) * 2 + index // 2

    def to_rows(self, value, stride):
        return jnp.concatenate(
            [
                lax.dynamic_slice_in_dim(
                    value, self.flip(i ^ self.tp) * stride, self.count, axis=0
                )
                for i in range(4)
            ],
            axis=0,
        )

    def to_relative(self, value, stride):
        return jnp.concatenate(
            [
                pad_rows(
                    lax.dynamic_slice_in_dim(
                        value, (self.flip(b) ^ self.tp) * self.count, self.count, axis=0
                    ),
                    stride,
                )
                for b in range(4)
            ],
            axis=0,
        )


def body(
    enc_in,
    dec_in,
    dec_cot,
    enc_seg,
    dec_seg,
    enc_norm1,
    enc_wq,
    enc_wk,
    enc_wv,
    enc_wo,
    enc_table,
    enc_norm2,
    enc_wgate,
    enc_wup,
    enc_wdown,
    enc_normf,
    dec_norm1,
    dec_wq,
    dec_wk,
    dec_wv,
    dec_wo,
    dec_table,
    dec_norm2,
    cross_wq,
    cross_wk,
    cross_wv,
    cross_wo,
    dec_norm3,
    dec_wgate,
    dec_wup,
    dec_wdown,
):
    groups = Groups()
    is_enc = groups.is_enc
    tp = lax.axis_index("tp")
    tp_arg = tp.astype(jnp.int32)[None]
    heads = enc_table.shape[1]
    width = heads * HEAD_DIM
    enc_count = enc_in.shape[1]
    dec_count = dec_in.shape[1]
    enc_len = enc_seg.shape[-1]
    rows = DecoderRows(tp, dec_count, enc_count)

    def columns(parts):
        return jnp.concatenate(parts, axis=1)

    x_own = jnp.where(is_enc, enc_in[0], pad_rows(dec_in[0], enc_count))
    x_all = gather_tokens(x_own)
    w_qkv = groups.gather(
        columns([enc_wq, enc_wk, enc_wv, enc_norm1[:, None], enc_norm2[:, None], enc_normf[:, None]]),
        columns([dec_wq, dec_wk, dec_wv, dec_norm1[:, None], dec_norm2[:, None], dec_norm3[:, None]]),
    )
    gains = w_qkv[:, 3 * width :].astype(F32).T
    w_qkv = w_qkv[:, : 3 * width]
    gain1, gain2, gain3 = gains[0:1], gains[1:2], gains[2:3]
    w_out = groups.gather(enc_wo.T, dec_wo.T)
    w_gate = groups.gather(enc_wgate, dec_wgate)
    w_up = groups.gather(enc_wup, dec_wup)
    w_down = groups.gather(enc_wdown.T, dec_wdown.T)
    w_cross = groups.gather(columns([cross_wk, cross_wv]), columns([cross_wq, cross_wo.T]))
    w_cq, w_co = w_cross[:, :width], w_cross[:, width:]
    cot_own = dec_cot[0]
    cot_all = gather_tokens(cot_own)

    enc_ids = enc_seg[0, 0].astype(F32)
    ids_rel = jnp.concatenate(
        [
            lax.dynamic_slice_in_dim(enc_ids, (DecoderRows.flip(b) ^ tp) * enc_count, enc_count)
            for b in range(4)
        ]
    )
    dec_ids = dec_seg[0]
    cross_ids = sum(groups.send(dec_ids[r], 3, r) for r in range(3)).astype(F32)
    enc_hot = one_hot_blocks(enc_relative(), True)
    dec_hot = one_hot_blocks(dec_relative(), False)
    enc_bias = dot(enc_table, jnp.asarray(enc_hot, BF16), TN).reshape(heads, 5, QB, QB)
    dec_bias = dot(dec_table, jnp.asarray(dec_hot, BF16), TN).reshape(heads, DEC_LEN, DEC_LEN)

    enc_cfg = dict(
        name="enc", heads=heads, bq=QB, bk=enc_len, steps=enc_len // QB, follow=False,
        bias="blocks", causal=False, k=width, v=2 * width,
    )
    dec_cfg = dict(
        name="dec", heads=heads, bq=DEC_LEN, bk=DEC_LEN, steps=3, follow=True,
        bias="full", causal=True, k=width, v=2 * width,
    )
    cross_cfg = dict(
        name="cross", heads=heads, bq=DEC_LEN, bk=enc_len, steps=1, follow=False,
        bias=None, causal=False, k=0, v=width,
    )
    enc_idk = jnp.broadcast_to(ids_rel[:, None], (enc_len, QB))
    enc_idq = ids_rel.reshape(enc_len // QB, 1, QB)
    dec_idk = jnp.broadcast_to(dec_ids.astype(F32).reshape(-1, 1), (3 * DEC_LEN, DEC_LEN))
    dec_idq = dec_ids.astype(F32).reshape(3, 1, DEC_LEN)
    cross_idk = jnp.broadcast_to(ids_rel[:, None], (enc_len, DEC_LEN))
    cross_idq = cross_ids.reshape(1, 1, DEC_LEN)

    x_f32 = x_own.astype(F32)
    norm1_all = rms_scale(x_all.astype(F32), gain1).astype(BF16)
    qkv = dot(norm1_all, w_qkv, NN).astype(BF16)

    def enc_attend(qkv):
        return attention_forward(enc_cfg, tp_arg, qkv, qkv, enc_idk, enc_idq, enc_bias)

    def dec_attend(qkv):
        ordered = rows.to_rows(qkv, enc_count)
        out, lse = attention_forward(dec_cfg, tp_arg, ordered, ordered, dec_idk, dec_idq, dec_bias)
        return rows.to_relative(out, enc_count), jnp.pad(
            lse.reshape(-1), (0, heads * enc_len - lse.size)
        ).reshape(enc_len // QB, heads, QB)

    att, lse1 = lax.cond(is_enc, enc_attend, dec_attend, qkv)
    x1 = x_f32 + reduce_tokens(dot(att, w_out, NT).astype(BF16))

    norm2_all = gather_tokens(rms_scale(x1, gain2).astype(BF16))
    dec_q_rel = dot(norm2_all, w_cq, NN).astype(BF16)
    dec_q = rows.to_rows(dec_q_rel, enc_count).reshape(3, DEC_LEN, width)
    cross_q = sum(groups.send(dec_q[r], 3, r) for r in range(3))
    gate2 = dot(norm2_all, w_gate, NN)
    up2 = dot(norm2_all, w_up, NN)
    hidden2 = gated(gate2, up2)
    x2 = x1 + reduce_tokens(dot(hidden2, w_down, NT).astype(BF16))
    memory = gather_tokens(rms_scale(x2, gain3).astype(BF16))

    cross_kv = dot(memory, w_cross, NN).astype(BF16)
    cross_o, lse2 = attention_forward(cross_cfg, tp_arg, cross_q, cross_kv, cross_idk, cross_idq)
    dec_o = jnp.concatenate([groups.send(cross_o, r, 3) for r in range(3)], axis=0)
    dec_o_rel = rows.to_relative(dec_o, dec_count)

    x2d = x1[:dec_count] + reduce_tokens(dot(dec_o_rel, w_co, NT).astype(BF16))
    norm3_all = gather_tokens(rms_scale(x2d, gain3).astype(BF16))
    gate3 = dot(norm3_all, w_gate, NN)
    up3 = dot(norm3_all, w_up, NN)
    grad_hidden3 = dot(cot_all, w_down, NN)
    hidden3, grad_gate3, grad_up3 = gated_back(gate3, up3, grad_hidden3)
    grad_n3 = reduce_tokens((dot(grad_gate3, w_gate, NT) + dot(grad_up3, w_up, NT)).astype(BF16))
    grad_step, gain_d3 = norm_backward(x2d, gain3, grad_n3)
    grad_x2d = cot_own.astype(F32) + grad_step
    grad2_all = gather_tokens(grad_x2d.astype(BF16))
    grad_o_rel = dot(grad2_all, w_co, NN).astype(BF16)
    grad_o_rows = rows.to_rows(grad_o_rel, dec_count).reshape(3, DEC_LEN, width)
    cross_go = sum(groups.send(grad_o_rows[r], 3, r) for r in range(3))
    dec_out = x2d + reduce_tokens(dot(hidden3, w_down, NT).astype(BF16))

    cross_gq, cross_gkv = attention_backward(
        cross_cfg, tp_arg, cross_q, cross_kv, cross_idk, cross_idq, lse2, cross_go
    )
    dec_gq = jnp.concatenate([groups.send(cross_gq, r, 3) for r in range(3)], axis=0)
    dec_gq_rel = rows.to_relative(dec_gq, enc_count)
    grad_memory = reduce_tokens(dot(cross_gkv, w_cross, NT).astype(BF16)).astype(BF16).astype(F32)
    grad_e2, gain_ef = norm_backward(x2, gain3, grad_memory)

    grad_e2_all = gather_tokens(grad_e2.astype(BF16))
    grad_hidden2 = dot(grad_e2_all, w_down, NN)
    hidden2, grad_gate2, grad_up2 = gated_back(gate2, up2, grad_hidden2)
    zero = jnp.zeros((), BF16)
    grad_gate2 = jnp.where(is_enc, grad_gate2, zero)
    grad_up2 = jnp.where(is_enc, grad_up2, zero)
    grad_q_only = jnp.where(is_enc, zero, dec_gq_rel)
    grad_n2 = reduce_tokens(
        (
            dot(grad_gate2, w_gate, NT) + dot(grad_up2, w_up, NT) + dot(grad_q_only, w_cq, NT)
        ).astype(BF16)
    )
    grad_step, gain_2 = norm_backward(x1, gain2, grad_n2)
    grad_x1 = jnp.where(is_enc, grad_e2, pad_rows(grad_x2d, enc_count)) + grad_step

    def feed_grads(tokens, hidden, grad_gate, grad_up, grad_rows):
        return (
            dot(tokens, grad_gate, TN).astype(BF16),
            dot(tokens, grad_up, TN).astype(BF16),
            dot(grad_rows, hidden, TN).astype(BF16),
        )

    g_gate, g_up, g_down = lax.cond(
        is_enc,
        lambda enc, dec: feed_grads(*enc),
        lambda enc, dec: feed_grads(*dec),
        (norm2_all, hidden2, grad_gate2, grad_up2, grad_e2_all),
        (norm3_all, hidden3, grad_gate3, grad_up3, cot_all),
    )
    g_cross = jnp.where(
        is_enc,
        dot(memory, cross_gkv, TN),
        columns([dot(norm2_all, dec_gq_rel, TN), dot(grad2_all, dec_o_rel, TN)]),
    ).astype(BF16)

    grad_x1_all = gather_tokens(grad_x1.astype(BF16))
    grad_att = dot(grad_x1_all, w_out, NN).astype(BF16)
    g_out = dot(grad_x1_all, att, TN).astype(BF16)

    def enc_attend_back(qkv, lse, grad_att):
        gq, gkv, gb = attention_backward(
            enc_cfg, tp_arg, qkv, qkv, enc_idk, enc_idq, lse, grad_att, enc_bias
        )
        hot = jnp.asarray(enc_hot, F32)
        return columns([gq, gkv]), lax.dot_general(
            hot, gb.reshape(heads, -1), ((NT[0], NT[1]), ((), ())), precision=lax.Precision.HIGHEST
        )

    def dec_attend_back(qkv, lse, grad_att):
        ordered = rows.to_rows(qkv, enc_count)
        lse = lse.reshape(-1)[: 3 * heads * DEC_LEN].reshape(3, heads, DEC_LEN)
        gq, gkv, gb = attention_backward(
            dec_cfg, tp_arg, ordered, ordered, dec_idk, dec_idq, lse,
            rows.to_rows(grad_att, enc_count), dec_bias,
        )
        hot = jnp.asarray(dec_hot, F32)
        return rows.to_relative(columns([gq, gkv]), enc_count), lax.dot_general(
            hot, gb.reshape(heads, -1), ((NT[0], NT[1]), ((), ())), precision=lax.Precision.HIGHEST
        )

    grad_qkv, grad_table = lax.cond(is_enc, enc_attend_back, dec_attend_back, qkv, lse1, grad_att)
    grad_n1 = reduce_tokens(dot(grad_qkv, w_qkv, NT).astype(BF16))
    grad_step, gain_1 = norm_backward(x_f32, gain1, grad_n1)
    grad_x = grad_x1 + grad_step
    g_qkv = dot(norm1_all, grad_qkv, TN).astype(BF16)

    enc_gate, dec_gate = groups.scatter(g_gate)
    enc_up, dec_up = groups.scatter(g_up)
    enc_down, dec_down = groups.scatter(g_down)
    enc_cross, dec_cross = groups.scatter(g_cross)
    enc_out, dec_wout = groups.scatter(g_out)
    enc_qkv, dec_qkv = groups.scatter(g_qkv)

    gain_rows = jnp.stack([gain_1, gain_2, jnp.where(is_enc, gain_ef, gain_d3)])
    gain_rows = gain_rows + core_swap(gain_rows)
    gain_rows = gain_rows + pair_swap(gain_rows)
    small = jnp.concatenate([gain_rows.reshape(-1), grad_table.reshape(-1)])
    length = small.shape[0]
    small = jnp.pad(small, (0, -length % 1024)).reshape(-1, 128)
    enc_small, dec_small = groups.all_role_sums(small)

    def unpack(total):
        flat = total.reshape(-1)
        gain = flat[: gain_rows.size].reshape(gain_rows.shape)
        share = gain.shape[1] // groups.count
        mine = lax.dynamic_slice_in_dim(gain, groups.where * share, share, axis=1)
        return mine, flat[gain_rows.size : length].reshape(BUCKETS, heads)

    enc_gains, enc_table_grad = unpack(enc_small)
    dec_gains, dec_table_grad = unpack(dec_small)

    def part(value, index):
        return value[:, index * width : (index + 1) * width]

    zero_bf = jnp.zeros((), BF16)
    return (
        jnp.where(is_enc, zero_bf, dec_out.astype(BF16))[None],
        jnp.where(is_enc, grad_x.astype(BF16), zero_bf)[None],
        jnp.where(is_enc, zero_bf, grad_x[:dec_count].astype(BF16))[None],
        enc_gains[0],
        part(enc_qkv, 0),
        part(enc_qkv, 1),
        part(enc_qkv, 2),
        enc_out.T,
        enc_table_grad,
        enc_gains[1],
        enc_gate,
        enc_up,
        enc_down.T,
        enc_gains[2],
        dec_gains[0],
        part(dec_qkv, 0),
        part(dec_qkv, 1),
        part(dec_qkv, 2),
        dec_wout.T,
        dec_table_grad,
        dec_gains[1],
        part(dec_cross, 0),
        part(enc_cross, 0),
        part(enc_cross, 1),
        part(dec_cross, 1).T,
        dec_gains[2],
        dec_gate,
        dec_up,
        dec_down.T,
    )


def solution(mesh):
    vector, matrix, turned = P("grp"), P("grp", "tp"), P("tp", "grp")
    tokens, ids, table = P("grp", "tp", None), P("grp", None, None), P(None, "tp")
    enc = (vector, matrix, matrix, matrix, turned, table, vector, matrix, matrix, turned, vector)
    dec = (vector, matrix, matrix, matrix, turned, table, vector, matrix, matrix, matrix, turned)
    dec = dec + (vector, matrix, matrix, turned)
    return jax.shard_map(
        body,
        mesh=mesh,
        in_specs=(tokens, tokens, tokens, ids, ids) + enc + dec,
        out_specs=(tokens, tokens, tokens) + enc + dec,
        check_vma=False,
    )
```

```python
import math
from functools import partial

import jax
import jax.numpy as jnp
import numpy as np
from jax import lax
from jax.experimental import pallas as pl
from jax.experimental.pallas import tpu as pltpu
from jax.sharding import PartitionSpec as P

HEAD_DIM = 64
BUCKETS = 32
MAX_DIST = 128
DEC_LEN = 192
EPSILON = 1e-06
NEG_FILL = -1e30
QB = 128
F32 = jnp.float32
BF16 = jnp.bfloat16


def bucket_of(relative, two_sided):
    bucket_count = BUCKETS
    shifted = relative * 0
    if two_sided:
        bucket_count = bucket_count // 2
        shifted = shifted + (relative > 0) * bucket_count
        distance = np.abs(relative)
    else:
        distance = np.maximum(-relative, 0)
    exact_span = bucket_count // 2
    log_ratio = np.log(np.maximum(distance, 1) / exact_span) / np.log(MAX_DIST / exact_span)
    farther = np.minimum(
        exact_span + np.floor(log_ratio * (bucket_count - exact_span) + 1e-09).astype(np.int32),
        bucket_count - 1,
    )
    return (shifted + np.where(distance < exact_span, distance, farther)).astype(np.int32)


def one_hot_blocks(relative, two_sided):
    return np.eye(BUCKETS, dtype=np.float32)[:, bucket_of(relative, two_sided).reshape(-1)]


def enc_relative():
    return np.arange(-2 * QB, 3 * QB)[:, None] - np.arange(QB)[None, :]


def dec_relative():
    return np.arange(DEC_LEN)[:, None] - np.arange(DEC_LEN)[None, :]


def after(value, *others):
    return lax.optimization_barrier((value,) + others)[0]


def dot(left, right, dims):
    return lax.dot_general(left, right, (dims, ((), ())), preferred_element_type=F32)


NN = ((1,), (0,))
NT = ((1,), (1,))
TN = ((0,), (0,))


def block_of(place, tp):
    wide = place // 2
    swapped = (wide % 2) * 2 + wide // 2
    return (swapped ^ tp) * 2 + place % 2


def scores_t(head, cfg, keys, queries, bias_ref, same, place, tp):
    lanes = slice(head * HEAD_DIM, (head + 1) * HEAD_DIM)
    scores = dot(keys[:, lanes], queries[:, lanes], NT)
    if cfg["bias"] == "blocks":
        mine = block_of(place, tp)
        parts = []
        for kb in range(keys.shape[0] // QB):
            step = jnp.clip(block_of(kb, tp) - mine, -2, 2) + 2
            parts.append(bias_ref[head, step])
        scores = scores + jnp.concatenate(parts, axis=0)
    elif cfg["bias"] == "full":
        scores = scores + bias_ref[head]
    return jnp.where(same, scores, NEG_FILL)


def allowed_t(cfg, idk_ref, idq_ref):
    same = idk_ref[...] == idq_ref[0]
    if cfg["causal"]:
        key_pos = lax.broadcasted_iota(jnp.int32, same.shape, 0)
        query_pos = lax.broadcasted_iota(jnp.int32, same.shape, 1)
        same = same & (key_pos <= query_pos)
    return same


def forward_kernel(cfg, tp_ref, q_ref, kv_ref, idk_ref, idq_ref, *rest):
    if cfg["bias"]:
        bias_ref, out_ref, lse_ref, vt_ref = rest
    else:
        bias_ref, (out_ref, lse_ref, vt_ref) = None, rest
    heads = cfg["heads"]
    width = heads * HEAD_DIM
    place = pl.program_id(0)
    keys = kv_ref[:, cfg["k"] : cfg["k"] + width]

    def fill():
        vt_ref[...] = kv_ref[:, cfg["v"] : cfg["v"] + width].T

    if cfg["follow"]:
        fill()
    else:
        pl.when(place == 0)(fill)
    queries = q_ref[:, :width]
    same = allowed_t(cfg, idk_ref, idq_ref)
    outs = []
    for head in range(heads):
        scores = scores_t(head, cfg, keys, queries, bias_ref, same, place, tp_ref[0])
        peak = jnp.max(scores, axis=0, keepdims=True)
        exponent = jnp.exp(scores - peak)
        total = jnp.sum(exponent, axis=0, keepdims=True)
        weights = (exponent * (1.0 / total)).astype(BF16)
        outs.append(dot(vt_ref[head * HEAD_DIM : (head + 1) * HEAD_DIM, :], weights, NN))
        lse_ref[0, head : head + 1, :] = peak + jnp.log(total)
    out_ref[...] = jnp.concatenate(outs, axis=0).T.astype(BF16)


def backward_kernel(cfg, tp_ref, q_ref, kv_ref, idk_ref, idq_ref, *rest):
    if cfg["bias"]:
        bias_ref, lse_ref, go_ref, gq_ref, gkv_ref, gb_ref, kt_ref, acc_ref = rest
    else:
        bias_ref, gb_ref = None, None
        lse_ref, go_ref, gq_ref, gkv_ref, kt_ref, acc_ref = rest
    heads = cfg["heads"]
    width = heads * HEAD_DIM
    place = pl.program_id(0)
    keys = kv_ref[:, cfg["k"] : cfg["k"] + width]
    values = kv_ref[:, cfg["v"] : cfg["v"] + width]

    def clear():
        kt_ref[...] = kv_ref[:, cfg["k"] : cfg["k"] + width].T
        acc_ref[...] = jnp.zeros_like(acc_ref)

    def clear_bias():
        if gb_ref is not None:
            gb_ref[...] = jnp.zeros_like(gb_ref)

    pl.when(place == 0)(clear_bias)
    if cfg["follow"]:
        clear()
    else:
        pl.when(place == 0)(clear)
    queries = q_ref[:, :width]
    grad_out = go_ref[...]
    same = allowed_t(cfg, idk_ref, idq_ref)
    grads = []
    for head in range(heads):
        lanes = slice(head * HEAD_DIM, (head + 1) * HEAD_DIM)
        scores = scores_t(head, cfg, keys, queries, bias_ref, same, place, tp_ref[0])
        weights = jnp.exp(scores - lse_ref[0, head : head + 1, :])
        grad_weights = dot(values[:, lanes], grad_out[:, lanes], NT)
        delta = jnp.sum(grad_weights * weights, axis=0, keepdims=True)
        grad_scores = weights * (grad_weights - delta)
        if cfg["bias"] == "blocks":
            mine = block_of(place, tp_ref[0])
            for kb in range(keys.shape[0] // QB):
                step = jnp.clip(block_of(kb, tp_ref[0]) - mine, -2, 2) + 2
                gb_ref[head, step] += grad_scores[kb * QB : (kb + 1) * QB]
        elif cfg["bias"] == "full":
            gb_ref[head] += grad_scores
        scores_bf = grad_scores.astype(BF16)
        acc_ref[head] += dot(scores_bf, queries[:, lanes], NN)
        acc_ref[heads + head] += dot(weights.astype(BF16), grad_out[:, lanes], NN)
        grads.append(dot(kt_ref[lanes, :], scores_bf, NN))
    gq_ref[...] = jnp.concatenate(grads, axis=0).T.astype(BF16)

    def finish():
        gkv_ref[...] = jnp.concatenate(
            [acc_ref[k].astype(BF16) for k in range(2 * heads)], axis=1
        )

    if cfg["follow"]:
        finish()
    else:
        pl.when(place == pl.num_programs(0) - 1)(finish)


def attention_specs(cfg, q_cols, kv_cols, bias):
    bq, bk = cfg["bq"], cfg["bk"]
    follow = cfg["follow"]
    specs = [
        pl.BlockSpec((bq, q_cols), lambda i, s: (i, 0)),
        pl.BlockSpec((bk, kv_cols), (lambda i, s: (i, 0)) if follow else (lambda i, s: (0, 0))),
        pl.BlockSpec((bk, bq), (lambda i, s: (i, 0)) if follow else (lambda i, s: (0, 0))),
        pl.BlockSpec((1, 1, bq), lambda i, s: (i, 0, 0)),
    ]
    if bias is not None:
        rank = bias.ndim
        specs.append(pl.BlockSpec(bias.shape, lambda i, s: (0,) * rank))
    return specs


def attention_forward(cfg, tp, q, kv, idk, idq, bias=None):
    heads, bq, bk, steps = cfg["heads"], cfg["bq"], cfg["bk"], cfg["steps"]
    width = heads * HEAD_DIM
    extra = () if bias is None else (bias,)
    return pl.pallas_call(
        partial(forward_kernel, cfg),
        out_shape=(
            jax.ShapeDtypeStruct((steps * bq, width), BF16),
            jax.ShapeDtypeStruct((steps, heads, bq), F32),
        ),
        grid_spec=pltpu.PrefetchScalarGridSpec(
            num_scalar_prefetch=1,
            grid=(steps,),
            in_specs=attention_specs(cfg, q.shape[1], kv.shape[1], bias),
            out_specs=(
                pl.BlockSpec((bq, width), lambda i, s: (i, 0)),
                pl.BlockSpec((1, heads, bq), lambda i, s: (i, 0, 0)),
            ),
            scratch_shapes=[pltpu.VMEM((width, bk), BF16)],
        ),
        compiler_params=pltpu.CompilerParams(vmem_limit_bytes=40 << 20),
        name=cfg["name"] + "_forward",
    )(tp, q, kv, idk, idq, *extra)


def attention_backward(cfg, tp, q, kv, idk, idq, lse, grad_out, bias=None):
    heads, bq, bk, steps = cfg["heads"], cfg["bq"], cfg["bk"], cfg["steps"]
    width = heads * HEAD_DIM
    follow = cfg["follow"]
    extra = () if bias is None else (bias,)
    out_shape = [
        jax.ShapeDtypeStruct((steps * bq, width), BF16),
        jax.ShapeDtypeStruct((steps * bk if follow else bk, 2 * width), BF16),
    ]
    out_specs = [
        pl.BlockSpec((bq, width), lambda i, s: (i, 0)),
        pl.BlockSpec((bk, 2 * width), (lambda i, s: (i, 0)) if follow else (lambda i, s: (0, 0))),
    ]
    if bias is not None:
        rank = bias.ndim
        out_shape.append(jax.ShapeDtypeStruct(bias.shape, F32))
        out_specs.append(pl.BlockSpec(bias.shape, lambda i, s: (0,) * rank))
    return pl.pallas_call(
        partial(backward_kernel, cfg),
        out_shape=tuple(out_shape),
        grid_spec=pltpu.PrefetchScalarGridSpec(
            num_scalar_prefetch=1,
            grid=(steps,),
            in_specs=attention_specs(cfg, q.shape[1], kv.shape[1], bias)
            + [
                pl.BlockSpec((1, heads, bq), lambda i, s: (i, 0, 0)),
                pl.BlockSpec((bq, width), lambda i, s: (i, 0)),
            ],
            out_specs=tuple(out_specs),
            scratch_shapes=[pltpu.VMEM((width, bk), BF16), pltpu.VMEM((2 * heads, bk, HEAD_DIM), F32)],
        ),
        compiler_params=pltpu.CompilerParams(vmem_limit_bytes=48 << 20),
        name=cfg["name"] + "_backward",
    )(tp, q, kv, idk, idq, *extra, lse, grad_out)


def product_kernel(quarter, share, step, jobs, widths, role_ref, *refs):
    operands, out_refs = refs[: 2 * len(jobs)], refs[2 * len(jobs) :]
    starts = [sum(widths[:k]) for k in range(len(widths))]
    for index, (on_role, column) in enumerate(jobs):
        left_ref, right_ref = operands[2 * index], operands[2 * index + 1]

        @pl.when(role_ref[0] == on_role)
        def _():
            result = dot(left_ref[...], right_ref[...], TN).astype(BF16)
            rows_here, cols_here = result.shape
            first = pl.program_id(0) * (rows_here // step)
            for unit in range(rows_here // step):
                row = (first + unit) * step
                owner, offset = row // share, pl.multiple_of(row % share, step)
                for out_ref, start, cols in zip(out_refs, starts, widths):
                    low, high = max(start, column), min(start + cols, column + cols_here)
                    if low < high:
                        out_ref[
                            owner % quarter,
                            owner // quarter,
                            pl.ds(offset, step),
                            low - start : high - start,
                        ] = result[unit * step : (unit + 1) * step, low - column : high - column]


def token_product(groups, widths, *jobs):
    rows_count = jobs[0][1].shape[1]
    tile = 256
    share = rows_count // groups.count
    step = math.gcd(share, 64)
    offsets, described, operands, specs = {}, [], [], []
    for role, left, right in jobs:
        count, cols = right.shape
        described.append((role, offsets.get(role, 0)))
        offsets[role] = offsets.get(role, 0) + cols

        def left_map(i, s, role=role):
            return (0, jnp.where(s[0] == role, i, 0))

        operands += [left, right]
        specs += [
            pl.BlockSpec((count, tile), left_map),
            pl.BlockSpec((count, cols), lambda i, s: (0, 0), pipeline_mode=pl.Buffered(1)),
        ]
    shapes = [(groups.quarter, 4, share, cols) for cols in widths]
    role = jnp.where(groups.is_enc, 0, 1).astype(jnp.int32)[None]
    return pl.pallas_call(
        partial(product_kernel, groups.quarter, share, step, described, widths),
        out_shape=tuple(jax.ShapeDtypeStruct(dims, BF16) for dims in shapes),
        grid_spec=pltpu.PrefetchScalarGridSpec(
            num_scalar_prefetch=1,
            grid=(rows_count // tile,),
            in_specs=specs,
            out_specs=tuple(pl.BlockSpec(dims, lambda i, s: (0, 0, 0, 0)) for dims in shapes),
        ),
        compiler_params=pltpu.CompilerParams(vmem_limit_bytes=56 << 20),
        name="token_product",
    )(role, *operands)


def bucket_sums(hot, values):
    high = values.astype(BF16)
    low = (values - high.astype(F32)).astype(BF16)
    sums = dot(jnp.asarray(hot, BF16), jnp.concatenate([high, low], axis=0), NT)
    return sums[:, : values.shape[0]] + sums[:, values.shape[0] :]


def rms_scale(hidden, gain_vec):
    return (
        hidden * lax.rsqrt(jnp.mean(hidden * hidden, axis=-1, keepdims=True) + EPSILON) * gain_vec
    )


def norm_backward(hidden, gain_vec, grad_out):
    rate = lax.rsqrt(jnp.mean(hidden * hidden, axis=-1, keepdims=True) + EPSILON)
    scaled = gain_vec * grad_out
    inner = jnp.mean(hidden * scaled, axis=-1, keepdims=True)
    grad_in = rate * scaled - hidden * (rate * rate * rate * inner)
    return grad_in, jnp.sum(grad_out * hidden * rate, axis=0)


GELU_SCALE = float(np.sqrt(2.0 / np.pi))
GELU_CUBIC = 0.044715


def gelu_parts(value):
    square = value * value
    tanh = jnp.tanh(GELU_SCALE * (value + GELU_CUBIC * (value * square)))
    half = 0.5 * (1.0 + tanh)
    slope = half + 0.5 * value * (1.0 - tanh * tanh) * (
        GELU_SCALE * (1.0 + 3.0 * GELU_CUBIC * square)
    )
    return value * half, slope


def gelu(value):
    cubic = value + GELU_CUBIC * (value * value * value)
    return value * (0.5 * (1.0 + jnp.tanh(GELU_SCALE * cubic)))


def feed_kernel(tok_ref, wg_ref, wu_ref, wd_ref, out_ref, gate_ref, up_ref):
    tokens = tok_ref[...]
    gate = dot(tokens, wg_ref[...], NN)
    up = dot(tokens, wu_ref[...], NN)
    gate_ref[...] = gate
    up_ref[...] = up
    hidden = (gelu(gate) * up).astype(BF16)
    out_ref[...] = dot(hidden, wd_ref[...], NT).astype(BF16)


def feed_grads(gate, up, grads, wg_ref, wu_ref, wd_ref, gn_ref, both_ref, hid_ref):
    units = gate.shape[1]
    grad_hidden = dot(grads, wd_ref[...], NN)
    activated, slope = gelu_parts(gate)
    hid_ref[...] = (activated * up).astype(BF16)
    grad_gate = (grad_hidden * up * slope).astype(BF16)
    grad_up = (grad_hidden * activated).astype(BF16)
    both_ref[:, :units] = grad_gate
    both_ref[:, units:] = grad_up
    gn_ref[...] = (dot(grad_gate, wg_ref[...], NT) + dot(grad_up, wu_ref[...], NT)).astype(BF16)


def feed_back_kernel(gate_ref, up_ref, ga_ref, wg_ref, wu_ref, wd_ref, gn_ref, both_ref, hid_ref):
    feed_grads(
        gate_ref[...], up_ref[...], ga_ref[...], wg_ref, wu_ref, wd_ref, gn_ref, both_ref, hid_ref
    )


def feed_both_kernel(
    tok_ref, ga_ref, wg_ref, wu_ref, wd_ref, gn_ref, both_ref, hid_ref, out_ref
):
    tokens = tok_ref[...]
    gate = dot(tokens, wg_ref[...], NN)
    up = dot(tokens, wu_ref[...], NN)
    feed_grads(gate, up, ga_ref[...], wg_ref, wu_ref, wd_ref, gn_ref, both_ref, hid_ref)
    out_ref[...] = dot(hid_ref[...], wd_ref[...], NT).astype(BF16)


def feed_call(name, kernel, tile, streamed, weights, outs):
    count = streamed[0].shape[0]
    return pl.pallas_call(
        kernel,
        out_shape=tuple(jax.ShapeDtypeStruct((count, cols), kind) for cols, kind in outs),
        grid=(count // tile,),
        in_specs=[pl.BlockSpec((tile, a.shape[1]), lambda i: (i, 0)) for a in streamed]
        + [
            pl.BlockSpec(w.shape, lambda i: (0, 0), pipeline_mode=pl.Buffered(1)) for w in weights
        ],
        out_specs=tuple(pl.BlockSpec((tile, cols), lambda i: (i, 0)) for cols, _ in outs),
        compiler_params=pltpu.CompilerParams(vmem_limit_bytes=50 << 20),
        name=name,
    )(*streamed, *weights)


SWAP_CORE = [(0, 1), (1, 0), (2, 3), (3, 2)]
SWAP_PAIR = [(0, 2), (2, 0), (1, 3), (3, 1)]


def core_swap(value):
    return lax.ppermute(value, "tp", SWAP_CORE)


def pair_swap(value):
    return lax.ppermute(value, "tp", SWAP_PAIR)


def gather_tokens(own, meanwhile=None):
    far = pair_swap(own)
    if meanwhile is not None:
        far = after(far, meanwhile(own))
    return jnp.concatenate([own, far, core_swap(own), core_swap(far)], axis=0)


def reduce_tokens(partial_bf, meanwhile=None, first=None):
    count = partial_bf.shape[0] // 4
    other = core_swap(partial_bf[2 * count :])
    if first is not None:
        other = after(other, first(partial_bf))
    half = partial_bf[: 2 * count].astype(F32) + other.astype(F32)
    away = half[count:].astype(BF16)
    far = pair_swap(away)
    if meanwhile is not None:
        far = after(far, meanwhile(away))
    return half[:count] + far.astype(F32)


class Groups:
    def __init__(self):
        self.count = lax.axis_size("grp")
        self.quarter = self.count // 4
        where = lax.axis_index("grp")
        self.where = where
        self.role = where // self.quarter
        self.place = where % self.quarter
        self.is_enc = self.role < 3
        self.peers = [
            [a * self.quarter + j for j in range(self.quarter)] for a in range(4)
        ]
        self.swap = [(i, i ^ 1) for i in range(self.count)]
        self.roles = [
            [a * self.quarter + j for a in range(4)] for j in range(self.quarter)
        ]

    def shift(self, value, steps):
        hop = steps * self.quarter
        return lax.ppermute(
            value, "grp", [(i, (i + hop) % self.count) for i in range(self.count)]
        )

    def send(self, value, source, target):
        q = self.quarter
        return lax.ppermute(
            value, "grp", [(source * q + j, target * q + j) for j in range(q)]
        )

    def gather(self, chunks, eager):
        fulls, last, brought = [], {}, []
        for (enc, dec), one_by_one in zip(chunks, eager):
            rows, cols = enc.shape
            shards = [jnp.where(self.is_enc, enc, dec)]
            for step in (1, 2, 3):
                payload = jnp.where((self.role + step) % 4 < 3, enc, dec)
                if step in last:
                    payload = after(payload, last[step])
                last[step] = self.shift(payload, step)
                shards.append(last[step])
            brought.append(tuple(shards[1:]))
            sources = [(self.role - step) % 4 for step in range(4)]
            full = jnp.zeros((4, self.quarter, rows, cols), enc.dtype)
            if one_by_one and self.quarter == 2:
                for source, shard in zip(sources, shards):
                    other = lax.ppermute(shard, "grp", self.swap)
                    full = lax.dynamic_update_slice(
                        full, shard[None, None], (source, self.place, 0, 0)
                    )
                    full = lax.dynamic_update_slice(
                        full, other[None, None], (source, 1 - self.place, 0, 0)
                    )
            else:
                held = jnp.zeros((4, rows, cols), enc.dtype)
                for source, shard in zip(sources, shards):
                    held = lax.dynamic_update_slice(held, shard[None], (source, 0, 0))
                if self.quarter == 2:
                    other = lax.ppermute(held, "grp", self.swap)
                    full = lax.dynamic_update_slice(full, held[:, None], (0, self.place, 0, 0))
                    full = lax.dynamic_update_slice(
                        full, other[:, None], (0, 1 - self.place, 0, 0)
                    )
                else:
                    full = lax.all_gather(held, "grp", axis=1, axis_index_groups=self.peers)
            fulls.append(full.reshape(-1, cols))
        return fulls, brought

    def to_quarters(self, blocks):
        return lax.all_to_all(
            blocks, "grp", 0, 0, tiled=True, axis_index_groups=self.roles
        )

    def peer_sum(self, value):
        if self.quarter == 2:
            return value + lax.ppermute(value, "grp", self.swap)
        return lax.psum(value, "grp", axis_index_groups=self.peers)

    def role_sums(self, mine):
        enc_total, dec_total = 0.0, 0.0
        for step in range(4):
            target = (self.role + step) % 4
            block = lax.dynamic_index_in_dim(mine, target, 0, keepdims=False)
            if step:
                block = self.shift(block, step)
            block = block.astype(F32)
            source_enc = (self.role - step) % 4 < 3
            enc_total = enc_total + jnp.where(source_enc, block, 0.0)
            dec_total = dec_total + jnp.where(source_enc, 0.0, block)
        return enc_total, dec_total

    def to_place(self, product):
        return lax.psum_scatter(
            product, "grp", scatter_dimension=0, axis_index_groups=self.peers
        )

    def to_owner(self, mine):
        parts = self.to_quarters(mine).astype(F32)
        return parts[0] + parts[1] + parts[2], parts[3]

    def all_role_sums(self, value):
        value = self.peer_sum(value)
        return self.role_sums(jnp.broadcast_to(value[None], (4,) + value.shape))


def pad_rows(value, count):
    return jnp.pad(value, ((0, count - value.shape[0]), (0, 0)))


class DecoderRows:
    def __init__(self, tp, count, stride):
        self.count, self.stride, self.tp = count, stride, tp

    @staticmethod
    def flip(index):
        return (index % 2) * 2 + index // 2

    def to_rows(self, value, stride):
        return jnp.concatenate(
            [
                lax.dynamic_slice_in_dim(
                    value, self.flip(i ^ self.tp) * stride, self.count, axis=0
                )
                for i in range(4)
            ],
            axis=0,
        )

    def to_relative(self, value, stride):
        return jnp.concatenate(
            [
                pad_rows(
                    lax.dynamic_slice_in_dim(
                        value, (self.flip(b) ^ self.tp) * self.count, self.count, axis=0
                    ),
                    stride,
                )
                for b in range(4)
            ],
            axis=0,
        )


def body(
    enc_in,
    dec_in,
    dec_cot,
    enc_seg,
    dec_seg,
    enc_norm1,
    enc_wq,
    enc_wk,
    enc_wv,
    enc_wo,
    enc_table,
    enc_norm2,
    enc_wgate,
    enc_wup,
    enc_wdown,
    enc_normf,
    dec_norm1,
    dec_wq,
    dec_wk,
    dec_wv,
    dec_wo,
    dec_table,
    dec_norm2,
    cross_wq,
    cross_wk,
    cross_wv,
    cross_wo,
    dec_norm3,
    dec_wgate,
    dec_wup,
    dec_wdown,
):
    groups = Groups()
    is_enc = groups.is_enc
    tp = lax.axis_index("tp")
    tp_arg = tp.astype(jnp.int32)[None]
    heads = enc_table.shape[1]
    width = heads * HEAD_DIM
    enc_count = enc_in.shape[1]
    dec_count = dec_in.shape[1]
    enc_len = enc_seg.shape[-1]
    rows = DecoderRows(tp, dec_count, enc_count)

    def columns(parts):
        return jnp.concatenate(parts, axis=1)

    x_own = jnp.where(is_enc, enc_in[0], pad_rows(dec_in[0], enc_count))
    x_all = gather_tokens(x_own)
    units = enc_wgate.shape[1]
    padded = -units % 128

    def first_chunk(weights, gains):
        gains = jnp.pad(jnp.stack(gains, axis=1), ((0, 0), (0, -len(gains) % 64)))
        return columns(list(weights) + [gains])

    def second_chunk(weights):
        return jnp.pad(columns(weights), ((0, 0), (0, -3 * width % 128)))

    def wide(weight):
        return jnp.pad(weight, ((0, 0), (0, padded)))

    (first, second, w_gate, w_up, w_down), brought = groups.gather(
        [
            (
                first_chunk([enc_wq, enc_wk, enc_wv], [enc_norm1, enc_norm2, enc_normf]),
                first_chunk([dec_wq, dec_wk, dec_wv], [dec_norm1, dec_norm2, dec_norm3]),
            ),
            (
                second_chunk([enc_wo.T, cross_wk, cross_wv]),
                second_chunk([dec_wo.T, cross_wq, cross_wo.T]),
            ),
            (wide(enc_wgate), wide(dec_wgate)),
            (wide(enc_wup), wide(dec_wup)),
            (wide(enc_wdown.T), wide(dec_wdown.T)),
        ],
        (True, True, False, False, False),
    )
    w_qkv = first[:, : 3 * width]
    gains = first[:, 3 * width : 3 * width + 3].astype(F32).T
    gain1, gain2, gain3 = gains[0:1], gains[1:2], gains[2:3]
    w_out, w_cross = second[:, :width], second[:, width : 3 * width]
    w_cq, w_co = w_cross[:, :width], w_cross[:, width:]
    cot_own = dec_cot[0]
    enc_table, dec_table = after((enc_table, dec_table), brought[0])

    enc_ids = enc_seg[0, 0].astype(F32)
    ids_rel = jnp.concatenate(
        [
            lax.dynamic_slice_in_dim(enc_ids, (DecoderRows.flip(b) ^ tp) * enc_count, enc_count)
            for b in range(4)
        ]
    )
    dec_ids = dec_seg[0]
    cross_ids = sum(groups.send(dec_ids[r], 3, r) for r in range(3)).astype(F32)
    enc_hot = one_hot_blocks(enc_relative(), True)
    dec_hot = one_hot_blocks(dec_relative(), False)
    enc_bias = dot(enc_table, jnp.asarray(enc_hot, BF16), TN).reshape(heads, 5, QB, QB)
    dec_bias = dot(dec_table, jnp.asarray(dec_hot, BF16), TN).reshape(heads, DEC_LEN, DEC_LEN)

    enc_cfg = dict(
        name="enc", heads=heads, bq=QB, bk=enc_len, steps=enc_len // QB, follow=False,
        bias="blocks", causal=False, k=width, v=2 * width,
    )
    dec_cfg = dict(
        name="dec", heads=heads, bq=DEC_LEN, bk=DEC_LEN, steps=3, follow=True,
        bias="full", causal=True, k=width, v=2 * width,
    )
    cross_cfg = dict(
        name="cross", heads=heads, bq=DEC_LEN, bk=enc_len, steps=1, follow=False,
        bias=None, causal=False, k=0, v=width,
    )
    enc_idk = jnp.broadcast_to(ids_rel[:, None], (enc_len, QB))
    enc_idq = ids_rel.reshape(enc_len // QB, 1, QB)
    dec_idk = jnp.broadcast_to(dec_ids.astype(F32).reshape(-1, 1), (3 * DEC_LEN, DEC_LEN))
    dec_idq = dec_ids.astype(F32).reshape(3, 1, DEC_LEN)
    cross_idk = jnp.broadcast_to(ids_rel[:, None], (enc_len, DEC_LEN))
    cross_idq = cross_ids.reshape(1, 1, DEC_LEN)

    x_f32 = x_own.astype(F32)
    norm1_all = rms_scale(x_all.astype(F32), gain1).astype(BF16)
    qkv = dot(norm1_all, w_qkv, NN).astype(BF16)

    def enc_attend(qkv):
        return attention_forward(enc_cfg, tp_arg, qkv, qkv, enc_idk, enc_idq, enc_bias)

    def dec_attend(qkv):
        ordered = rows.to_rows(qkv, enc_count)
        out, lse = attention_forward(dec_cfg, tp_arg, ordered, ordered, dec_idk, dec_idq, dec_bias)
        return rows.to_relative(out, enc_count), jnp.pad(
            lse.reshape(-1), (0, heads * enc_len - lse.size)
        ).reshape(enc_len // QB, heads, QB)

    att, lse1 = lax.cond(is_enc, enc_attend, dec_attend, after(qkv, brought[2]))
    x1 = x_f32 + reduce_tokens(dot(after(att, brought[3]), w_out, NT).astype(BF16))

    norm2_all = gather_tokens(rms_scale(x1, gain2).astype(BF16))
    cot_all = gather_tokens(after(cot_own, norm2_all))
    dec_q_rel = dot(norm2_all, w_cq, NN).astype(BF16)
    dec_q = rows.to_rows(dec_q_rel, enc_count).reshape(3, DEC_LEN, width)
    cross_q = sum(groups.send(dec_q[r], 3, r) for r in range(3))
    feed_weights = (w_gate, w_up, after(w_down, cross_q, cross_ids))
    wide_units = w_gate.shape[1]
    width_all = x_own.shape[1]
    feed_out2, gate2, up2 = feed_call(
        "feed_forward", feed_kernel, 256, (norm2_all,), feed_weights,
        ((width_all, BF16), (wide_units, F32), (wide_units, F32)),
    )
    x2 = x1 + reduce_tokens(feed_out2)
    memory = gather_tokens(rms_scale(x2, gain3).astype(BF16))

    cross_kv = dot(memory, w_cross, NN).astype(BF16)
    cross_o, lse2 = attention_forward(cross_cfg, tp_arg, cross_q, cross_kv, cross_idk, cross_idq)
    dec_o = jnp.concatenate([groups.send(cross_o, r, 3) for r in range(3)], axis=0)
    dec_o_rel = rows.to_relative(dec_o, dec_count)

    x2d = x1[:dec_count] + reduce_tokens(dot(dec_o_rel, w_co, NT).astype(BF16))
    norm3_all = gather_tokens(rms_scale(x2d, gain3).astype(BF16))
    grad_outs = ((width_all, BF16), (2 * wide_units, BF16), (wide_units, BF16))
    partial_n3, both3, hidden3, feed_out3 = feed_call(
        "feed_both", feed_both_kernel, 192, (norm3_all, cot_all), feed_weights,
        grad_outs + ((width_all, BF16),),
    )
    grad_n3 = reduce_tokens(partial_n3)
    grad_step, gain_d3 = norm_backward(x2d, gain3, grad_n3)
    grad_x2d = cot_own.astype(F32) + grad_step
    grad2_all = gather_tokens(grad_x2d.astype(BF16))
    grad_o_rel = dot(grad2_all, w_co, NN).astype(BF16)
    grad_o_rows = rows.to_rows(grad_o_rel, dec_count).reshape(3, DEC_LEN, width)
    cross_go = sum(groups.send(grad_o_rows[r], 3, r) for r in range(3))
    dec_out = x2d + reduce_tokens(after(feed_out3, grad_o_rel))

    cross_go = after(cross_go, dec_out)
    cross_gq, cross_gkv = attention_backward(
        cross_cfg, tp_arg, cross_q, cross_kv, cross_idk, cross_idq, lse2, cross_go
    )
    dec_gq = jnp.concatenate([groups.send(cross_gq, r, 3) for r in range(3)], axis=0)
    dec_gq_rel = rows.to_relative(dec_gq, enc_count)
    placed = {}

    def while_memory(anchor):
        left, right = after((memory, norm2_all), anchor)
        (product,) = token_product(
            groups,
            (2 * width,),
            (0, left, cross_gkv),
            (1, right, dec_gq_rel),
            (1, grad2_all, dec_o_rel),
        )
        placed["cross"] = groups.to_place(product)
        return product

    grad_memory = reduce_tokens(dot(cross_gkv, w_cross, NT).astype(BF16), while_memory)
    grad_memory = grad_memory.astype(BF16).astype(F32)
    grad_e2, gain_ef = norm_backward(x2, gain3, grad_memory)

    grad_e2_all = gather_tokens(grad_e2.astype(BF16))
    partial_n2, both2, hidden2 = feed_call(
        "feed_back", feed_back_kernel, 256, (gate2, up2, grad_e2_all), feed_weights, grad_outs
    )

    products = token_product(
        groups,
        (wide_units, wide_units),
        (0, after(norm2_all, partial_n2), both2),
        (1, norm3_all, both3),
    )
    for index, product in enumerate(products):
        placed[index] = groups.to_place(product)
    dec_partial = dot(after(dec_gq_rel, products), w_cq, NT).astype(BF16)
    partial_n2 = jnp.where(is_enc, partial_n2, dec_partial)

    def while_n2(anchor):
        grads, others = after((grad_e2_all, cot_all), anchor)
        (product,) = token_product(
            groups, (wide_units,), (0, grads, hidden2), (1, others, hidden3)
        )
        placed[2] = groups.to_place(product)
        sums["cross"] = groups.to_owner(after(placed["cross"], product))
        return product, sums["cross"]

    sums = {}
    grad_n2 = reduce_tokens(partial_n2, while_n2)
    grad_step, gain_2 = norm_backward(x1, gain2, grad_n2)
    grad_x1 = jnp.where(is_enc, grad_e2, pad_rows(grad_x2d, enc_count)) + grad_step
    sums[0] = groups.to_owner(after(placed[0], grad_x1))

    grad_x1_all = gather_tokens(grad_x1.astype(BF16))
    grad_att = dot(grad_x1_all, w_out, NN).astype(BF16)
    def enc_attend_back(qkv, lse, grad_att):
        gq, gkv, gb = attention_backward(
            enc_cfg, tp_arg, qkv, qkv, enc_idk, enc_idq, lse, grad_att, enc_bias
        )
        return columns([gq, gkv]), gb.reshape(heads, -1)

    def dec_attend_back(qkv, lse, grad_att):
        ordered = rows.to_rows(qkv, enc_count)
        lse = lse.reshape(-1)[: 3 * heads * DEC_LEN].reshape(3, heads, DEC_LEN)
        gq, gkv, gb = attention_backward(
            dec_cfg, tp_arg, ordered, ordered, dec_idk, dec_idq, lse,
            rows.to_rows(grad_att, enc_count), dec_bias,
        )
        gb = gb.reshape(heads, -1)
        return (
            rows.to_relative(columns([gq, gkv]), enc_count),
            jnp.pad(gb, ((0, 0), (0, enc_hot.shape[1] - gb.shape[1]))),
        )

    grad_qkv, grad_bias = lax.cond(is_enc, enc_attend_back, dec_attend_back, qkv, lse1, grad_att)
    partial_n1 = dot(grad_qkv, w_qkv, NT).astype(BF16)

    def while_n1(anchor):
        left, right = after((norm1_all, grad_x1_all), anchor)
        (product,) = token_product(
            groups,
            (4 * width,),
            (0, left, grad_qkv),
            (0, right, att),
            (1, left, grad_qkv),
            (1, right, att),
        )
        placed["first"] = groups.to_place(product)
        tables["grad"] = lax.cond(
            is_enc,
            lambda gb: bucket_sums(enc_hot, gb),
            lambda gb: bucket_sums(dec_hot, gb[:, : dec_hot.shape[1]]),
            after(grad_bias, product),
        )
        return product, tables["grad"]

    tables = {}

    sums[1] = groups.to_owner(after(placed[1], partial_n1, sums[0]))
    grad_n1 = reduce_tokens(partial_n1, while_n1)
    grad_step, gain_1 = norm_backward(x_f32, gain1, grad_n1)
    grad_x = grad_x1 + grad_step
    sums[2] = groups.to_owner(after(placed[2], gain_1, sums[1]))
    enc_first, dec_first = groups.to_owner(after(placed["first"], sums[2]))
    enc_cross, dec_cross = sums["cross"]
    (enc_gate, dec_gate), (enc_up, dec_up), (enc_down, dec_down) = sums[0], sums[1], sums[2]

    gain_rows = jnp.stack([gain_1, gain_2, jnp.where(is_enc, gain_ef, gain_d3)])
    gain_rows = gain_rows + core_swap(gain_rows)
    gain_rows = gain_rows + pair_swap(gain_rows)
    small = jnp.concatenate([gain_rows.reshape(-1), tables["grad"].reshape(-1)])
    length = small.shape[0]
    small = jnp.pad(small, (0, -length % 1024)).reshape(-1, 128)
    enc_small, dec_small = groups.all_role_sums(small)

    def unpack(total):
        flat = total.reshape(-1)
        gain = flat[: gain_rows.size].reshape(gain_rows.shape)
        share = gain.shape[1] // groups.count
        mine = lax.dynamic_slice_in_dim(gain, groups.where * share, share, axis=1)
        return mine, flat[gain_rows.size : length].reshape(BUCKETS, heads)

    enc_gains, enc_table_grad = unpack(enc_small)
    dec_gains, dec_table_grad = unpack(dec_small)

    def part(value, index):
        return value[:, index * width : (index + 1) * width]

    zero_bf = jnp.zeros((), BF16)
    return (
        jnp.where(is_enc, zero_bf, dec_out.astype(BF16))[None],
        jnp.where(is_enc, grad_x.astype(BF16), zero_bf)[None],
        jnp.where(is_enc, zero_bf, grad_x[:dec_count].astype(BF16))[None],
        enc_gains[0],
        part(enc_first, 0),
        part(enc_first, 1),
        part(enc_first, 2),
        part(enc_first, 3).T,
        enc_table_grad,
        enc_gains[1],
        enc_gate[:, :units],
        enc_up[:, :units],
        enc_down[:, :units].T,
        enc_gains[2],
        dec_gains[0],
        part(dec_first, 0),
        part(dec_first, 1),
        part(dec_first, 2),
        part(dec_first, 3).T,
        dec_table_grad,
        dec_gains[1],
        part(dec_cross, 0),
        part(enc_cross, 0),
        part(enc_cross, 1),
        part(dec_cross, 1).T,
        dec_gains[2],
        dec_gate[:, :units],
        dec_up[:, :units],
        dec_down[:, :units].T,
    )


def solution(mesh):
    vector, matrix, turned = P("grp"), P("grp", "tp"), P("tp", "grp")
    tokens, ids, table = P("grp", "tp", None), P("grp", None, None), P(None, "tp")
    enc = (vector, matrix, matrix, matrix, turned, table, vector, matrix, matrix, turned, vector)
    dec = (vector, matrix, matrix, matrix, turned, table, vector, matrix, matrix, matrix, turned)
    dec = dec + (vector, matrix, matrix, turned)
    return jax.shard_map(
        body,
        mesh=mesh,
        in_specs=(tokens, tokens, tokens, ids, ids) + enc + dec,
        out_specs=(tokens, tokens, tokens) + enc + dec,
        check_vma=False,
    )
```

```python
import math
from functools import partial

import jax
import jax.numpy as jnp
import numpy as np
from jax import lax
from jax.experimental import pallas as pl
from jax.experimental.pallas import tpu as pltpu
from jax.sharding import PartitionSpec as P

HEAD_DIM = 64
BUCKETS = 32
MAX_DIST = 128
DEC_LEN = 192
EPSILON = 1e-06
NEG_FILL = -1e30
QB = 128
F32 = jnp.float32
BF16 = jnp.bfloat16


def bucket_of(relative, two_sided):
    bucket_count = BUCKETS
    shifted = relative * 0
    if two_sided:
        bucket_count = bucket_count // 2
        shifted = shifted + (relative > 0) * bucket_count
        distance = np.abs(relative)
    else:
        distance = np.maximum(-relative, 0)
    exact_span = bucket_count // 2
    log_ratio = np.log(np.maximum(distance, 1) / exact_span) / np.log(MAX_DIST / exact_span)
    farther = np.minimum(
        exact_span + np.floor(log_ratio * (bucket_count - exact_span) + 1e-09).astype(np.int32),
        bucket_count - 1,
    )
    return (shifted + np.where(distance < exact_span, distance, farther)).astype(np.int32)


def one_hot_blocks(relative, two_sided):
    return np.eye(BUCKETS, dtype=np.float32)[:, bucket_of(relative, two_sided).reshape(-1)]


def enc_relative():
    return np.arange(-2 * QB, 3 * QB)[:, None] - np.arange(QB)[None, :]


def dec_relative():
    return np.arange(DEC_LEN)[:, None] - np.arange(DEC_LEN)[None, :]


def after(value, *others):
    return lax.optimization_barrier((value,) + others)[0]


def dot(left, right, dims):
    return lax.dot_general(left, right, (dims, ((), ())), preferred_element_type=F32)


NN = ((1,), (0,))
NT = ((1,), (1,))
TN = ((0,), (0,))


def block_of(place, tp):
    wide = place // 2
    swapped = (wide % 2) * 2 + wide // 2
    return (swapped ^ tp) * 2 + place % 2


def scores_t(head, cfg, keys, queries, bias_ref, same, place, tp):
    lanes = slice(head * HEAD_DIM, (head + 1) * HEAD_DIM)
    scores = dot(keys[:, lanes], queries[:, lanes], NT)
    if cfg["bias"] == "blocks":
        mine = block_of(place, tp)
        parts = []
        for kb in range(keys.shape[0] // QB):
            step = jnp.clip(block_of(kb, tp) - mine, -2, 2) + 2
            parts.append(bias_ref[head, step])
        scores = scores + jnp.concatenate(parts, axis=0)
    elif cfg["bias"] == "full":
        scores = scores + bias_ref[head]
    return jnp.where(same, scores, NEG_FILL)


def allowed_t(cfg, idk_ref, idq_ref):
    same = idk_ref[...] == idq_ref[0]
    if cfg["causal"]:
        key_pos = lax.broadcasted_iota(jnp.int32, same.shape, 0)
        query_pos = lax.broadcasted_iota(jnp.int32, same.shape, 1)
        same = same & (key_pos <= query_pos)
    return same


def forward_kernel(cfg, tp_ref, q_ref, kv_ref, idk_ref, idq_ref, *rest):
    if cfg["bias"]:
        bias_ref, out_ref, lse_ref, vt_ref = rest
    else:
        bias_ref, (out_ref, lse_ref, vt_ref) = None, rest
    heads = cfg["heads"]
    width = heads * HEAD_DIM
    place = pl.program_id(0)
    keys = kv_ref[:, cfg["k"] : cfg["k"] + width]

    def fill():
        vt_ref[...] = kv_ref[:, cfg["v"] : cfg["v"] + width].T

    if cfg["follow"]:
        fill()
    else:
        pl.when(place == 0)(fill)
    queries = q_ref[:, :width]
    same = allowed_t(cfg, idk_ref, idq_ref)
    outs = []
    for head in range(heads):
        scores = scores_t(head, cfg, keys, queries, bias_ref, same, place, tp_ref[0])
        peak = jnp.max(scores, axis=0, keepdims=True)
        exponent = jnp.exp(scores - peak)
        total = jnp.sum(exponent, axis=0, keepdims=True)
        weights = (exponent * (1.0 / total)).astype(BF16)
        outs.append(dot(vt_ref[head * HEAD_DIM : (head + 1) * HEAD_DIM, :], weights, NN))
        lse_ref[0, head : head + 1, :] = peak + jnp.log(total)
    out_ref[...] = jnp.concatenate(outs, axis=0).T.astype(BF16)


def backward_kernel(cfg, tp_ref, q_ref, kv_ref, idk_ref, idq_ref, *rest):
    if cfg["bias"]:
        bias_ref, lse_ref, go_ref, gq_ref, gkv_ref, gb_ref, kt_ref, acc_ref = rest
    else:
        bias_ref, gb_ref = None, None
        lse_ref, go_ref, gq_ref, gkv_ref, kt_ref, acc_ref = rest
    heads = cfg["heads"]
    width = heads * HEAD_DIM
    place = pl.program_id(0)
    keys = kv_ref[:, cfg["k"] : cfg["k"] + width]
    values = kv_ref[:, cfg["v"] : cfg["v"] + width]

    def clear():
        kt_ref[...] = kv_ref[:, cfg["k"] : cfg["k"] + width].T
        acc_ref[...] = jnp.zeros_like(acc_ref)

    def clear_bias():
        if gb_ref is not None:
            gb_ref[...] = jnp.zeros_like(gb_ref)

    pl.when(place == 0)(clear_bias)
    if cfg["follow"]:
        clear()
    else:
        pl.when(place == 0)(clear)
    queries = q_ref[:, :width]
    grad_out = go_ref[...]
    same = allowed_t(cfg, idk_ref, idq_ref)
    grads = []
    for head in range(heads):
        lanes = slice(head * HEAD_DIM, (head + 1) * HEAD_DIM)
        scores = scores_t(head, cfg, keys, queries, bias_ref, same, place, tp_ref[0])
        weights = jnp.exp(scores - lse_ref[0, head : head + 1, :])
        grad_weights = dot(values[:, lanes], grad_out[:, lanes], NT)
        delta = jnp.sum(grad_weights * weights, axis=0, keepdims=True)
        grad_scores = weights * (grad_weights - delta)
        if cfg["bias"] == "blocks":
            mine = block_of(place, tp_ref[0])
            for kb in range(keys.shape[0] // QB):
                step = jnp.clip(block_of(kb, tp_ref[0]) - mine, -2, 2) + 2
                gb_ref[head, step] += grad_scores[kb * QB : (kb + 1) * QB]
        elif cfg["bias"] == "full":
            gb_ref[head] += grad_scores
        scores_bf = grad_scores.astype(BF16)
        acc_ref[head] += dot(scores_bf, queries[:, lanes], NN)
        acc_ref[heads + head] += dot(weights.astype(BF16), grad_out[:, lanes], NN)
        grads.append(dot(kt_ref[lanes, :], scores_bf, NN))
    gq_ref[...] = jnp.concatenate(grads, axis=0).T.astype(BF16)

    def finish():
        gkv_ref[...] = jnp.concatenate(
            [acc_ref[k].astype(BF16) for k in range(2 * heads)], axis=1
        )

    if cfg["follow"]:
        finish()
    else:
        pl.when(place == pl.num_programs(0) - 1)(finish)


def attention_specs(cfg, q_cols, kv_cols, bias):
    bq, bk = cfg["bq"], cfg["bk"]
    follow = cfg["follow"]
    specs = [
        pl.BlockSpec((bq, q_cols), lambda i, s: (i, 0)),
        pl.BlockSpec((bk, kv_cols), (lambda i, s: (i, 0)) if follow else (lambda i, s: (0, 0))),
        pl.BlockSpec((bk, bq), (lambda i, s: (i, 0)) if follow else (lambda i, s: (0, 0))),
        pl.BlockSpec((1, 1, bq), lambda i, s: (i, 0, 0)),
    ]
    if bias is not None:
        rank = bias.ndim
        specs.append(pl.BlockSpec(bias.shape, lambda i, s: (0,) * rank))
    return specs


def attention_forward(cfg, tp, q, kv, idk, idq, bias=None):
    heads, bq, bk, steps = cfg["heads"], cfg["bq"], cfg["bk"], cfg["steps"]
    width = heads * HEAD_DIM
    extra = () if bias is None else (bias,)
    return pl.pallas_call(
        partial(forward_kernel, cfg),
        out_shape=(
            jax.ShapeDtypeStruct((steps * bq, width), BF16),
            jax.ShapeDtypeStruct((steps, heads, bq), F32),
        ),
        grid_spec=pltpu.PrefetchScalarGridSpec(
            num_scalar_prefetch=1,
            grid=(steps,),
            in_specs=attention_specs(cfg, q.shape[1], kv.shape[1], bias),
            out_specs=(
                pl.BlockSpec((bq, width), lambda i, s: (i, 0)),
                pl.BlockSpec((1, heads, bq), lambda i, s: (i, 0, 0)),
            ),
            scratch_shapes=[pltpu.VMEM((width, bk), BF16)],
        ),
        compiler_params=pltpu.CompilerParams(vmem_limit_bytes=40 << 20),
        name=cfg["name"] + "_forward",
    )(tp, q, kv, idk, idq, *extra)


def attention_backward(cfg, tp, q, kv, idk, idq, lse, grad_out, bias=None):
    heads, bq, bk, steps = cfg["heads"], cfg["bq"], cfg["bk"], cfg["steps"]
    width = heads * HEAD_DIM
    follow = cfg["follow"]
    extra = () if bias is None else (bias,)
    out_shape = [
        jax.ShapeDtypeStruct((steps * bq, width), BF16),
        jax.ShapeDtypeStruct((steps * bk if follow else bk, 2 * width), BF16),
    ]
    out_specs = [
        pl.BlockSpec((bq, width), lambda i, s: (i, 0)),
        pl.BlockSpec((bk, 2 * width), (lambda i, s: (i, 0)) if follow else (lambda i, s: (0, 0))),
    ]
    if bias is not None:
        rank = bias.ndim
        out_shape.append(jax.ShapeDtypeStruct(bias.shape, F32))
        out_specs.append(pl.BlockSpec(bias.shape, lambda i, s: (0,) * rank))
    return pl.pallas_call(
        partial(backward_kernel, cfg),
        out_shape=tuple(out_shape),
        grid_spec=pltpu.PrefetchScalarGridSpec(
            num_scalar_prefetch=1,
            grid=(steps,),
            in_specs=attention_specs(cfg, q.shape[1], kv.shape[1], bias)
            + [
                pl.BlockSpec((1, heads, bq), lambda i, s: (i, 0, 0)),
                pl.BlockSpec((bq, width), lambda i, s: (i, 0)),
            ],
            out_specs=tuple(out_specs),
            scratch_shapes=[pltpu.VMEM((width, bk), BF16), pltpu.VMEM((2 * heads, bk, HEAD_DIM), F32)],
        ),
        compiler_params=pltpu.CompilerParams(vmem_limit_bytes=48 << 20),
        name=cfg["name"] + "_backward",
    )(tp, q, kv, idk, idq, *extra, lse, grad_out)


def product_kernel(quarter, share, step, jobs, widths, role_ref, *refs):
    operands, out_refs = refs[: 2 * len(jobs)], refs[2 * len(jobs) :]
    starts = [sum(widths[:k]) for k in range(len(widths))]
    for index, (on_role, column) in enumerate(jobs):
        left_ref, right_ref = operands[2 * index], operands[2 * index + 1]

        @pl.when(role_ref[0] == on_role)
        def _():
            result = dot(left_ref[...], right_ref[...], TN).astype(BF16)
            rows_here, cols_here = result.shape
            first = pl.program_id(0) * (rows_here // step)
            for unit in range(rows_here // step):
                row = (first + unit) * step
                owner, offset = row // share, pl.multiple_of(row % share, step)
                for out_ref, start, cols in zip(out_refs, starts, widths):
                    low, high = max(start, column), min(start + cols, column + cols_here)
                    if low < high:
                        out_ref[
                            owner % quarter,
                            owner // quarter,
                            pl.ds(offset, step),
                            low - start : high - start,
                        ] = result[unit * step : (unit + 1) * step, low - column : high - column]


def token_product(groups, widths, *jobs):
    rows_count = jobs[0][1].shape[1]
    tile = 256
    share = rows_count // groups.count
    step = math.gcd(share, 64)
    offsets, described, operands, specs = {}, [], [], []
    for role, left, right, *block in jobs:
        count, cols = right.shape
        cols = sum(widths) if block else cols
        described.append((role, offsets.get(role, 0)))
        offsets[role] = offsets.get(role, 0) + cols

        def left_map(i, s, role=role):
            return (0, jnp.where(s[0] == role, i, 0))

        operands += [left, right]
        specs += [
            pl.BlockSpec((count, tile), left_map),
            pl.BlockSpec(
                (count, cols),
                lambda i, s, block=(block or [0])[0]: (0, block),
                pipeline_mode=pl.Buffered(1),
            ),
        ]
    shapes = [(groups.quarter, 4, share, cols) for cols in widths]
    role = jnp.where(groups.is_enc, 0, 1).astype(jnp.int32)[None]
    return pl.pallas_call(
        partial(product_kernel, groups.quarter, share, step, described, widths),
        out_shape=tuple(jax.ShapeDtypeStruct(dims, BF16) for dims in shapes),
        grid_spec=pltpu.PrefetchScalarGridSpec(
            num_scalar_prefetch=1,
            grid=(rows_count // tile,),
            in_specs=specs,
            out_specs=tuple(pl.BlockSpec(dims, lambda i, s: (0, 0, 0, 0)) for dims in shapes),
        ),
        compiler_params=pltpu.CompilerParams(vmem_limit_bytes=56 << 20),
        name="token_product",
    )(role, *operands)


def bucket_sums(hot, values):
    high = values.astype(BF16)
    low = (values - high.astype(F32)).astype(BF16)
    sums = dot(jnp.asarray(hot, BF16), jnp.concatenate([high, low], axis=0), NT)
    return sums[:, : values.shape[0]] + sums[:, values.shape[0] :]


def rms_scale(hidden, gain_vec):
    return (
        hidden * lax.rsqrt(jnp.mean(hidden * hidden, axis=-1, keepdims=True) + EPSILON) * gain_vec
    )


def norm_backward(hidden, gain_vec, grad_out):
    rate = lax.rsqrt(jnp.mean(hidden * hidden, axis=-1, keepdims=True) + EPSILON)
    scaled = gain_vec * grad_out
    inner = jnp.mean(hidden * scaled, axis=-1, keepdims=True)
    grad_in = rate * scaled - hidden * (rate * rate * rate * inner)
    return grad_in, jnp.sum(grad_out * hidden * rate, axis=0)


GELU_SCALE = float(np.sqrt(2.0 / np.pi))
GELU_CUBIC = 0.044715


def gelu_parts(value):
    square = value * value
    tanh = jnp.tanh(GELU_SCALE * (value + GELU_CUBIC * (value * square)))
    half = 0.5 * (1.0 + tanh)
    slope = half + 0.5 * value * (1.0 - tanh * tanh) * (
        GELU_SCALE * (1.0 + 3.0 * GELU_CUBIC * square)
    )
    return value * half, slope


def gelu(value):
    cubic = value + GELU_CUBIC * (value * value * value)
    return value * (0.5 * (1.0 + jnp.tanh(GELU_SCALE * cubic)))


def feed_kernel(tok_ref, wg_ref, wu_ref, wd_ref, out_ref, gate_ref, up_ref):
    tokens = tok_ref[...]
    gate = dot(tokens, wg_ref[...], NN)
    up = dot(tokens, wu_ref[...], NN)
    gate_ref[...] = gate
    up_ref[...] = up
    hidden = (gelu(gate) * up).astype(BF16)
    out_ref[...] = dot(hidden, wd_ref[...], NT).astype(BF16)


def feed_grads(gate, up, grads, wg_ref, wu_ref, wd_ref, gn_ref, both_ref, hid_ref):
    units = gate.shape[1]
    grad_hidden = dot(grads, wd_ref[...], NN)
    activated, slope = gelu_parts(gate)
    hid_ref[...] = (activated * up).astype(BF16)
    grad_gate = (grad_hidden * up * slope).astype(BF16)
    grad_up = (grad_hidden * activated).astype(BF16)
    both_ref[:, :units] = grad_gate
    both_ref[:, units:] = grad_up
    gn_ref[...] = (dot(grad_gate, wg_ref[...], NT) + dot(grad_up, wu_ref[...], NT)).astype(BF16)


def feed_back_kernel(gate_ref, up_ref, ga_ref, wg_ref, wu_ref, wd_ref, gn_ref, both_ref, hid_ref):
    feed_grads(
        gate_ref[...], up_ref[...], ga_ref[...], wg_ref, wu_ref, wd_ref, gn_ref, both_ref, hid_ref
    )


def feed_both_kernel(
    tok_ref, ga_ref, wg_ref, wu_ref, wd_ref, gn_ref, both_ref, hid_ref, out_ref
):
    tokens = tok_ref[...]
    gate = dot(tokens, wg_ref[...], NN)
    up = dot(tokens, wu_ref[...], NN)
    feed_grads(gate, up, ga_ref[...], wg_ref, wu_ref, wd_ref, gn_ref, both_ref, hid_ref)
    out_ref[...] = dot(hid_ref[...], wd_ref[...], NT).astype(BF16)


def feed_call(name, kernel, tile, streamed, weights, outs):
    count = streamed[0].shape[0]
    return pl.pallas_call(
        kernel,
        out_shape=tuple(jax.ShapeDtypeStruct((count, cols), kind) for cols, kind in outs),
        grid=(count // tile,),
        in_specs=[pl.BlockSpec((tile, a.shape[1]), lambda i: (i, 0)) for a in streamed]
        + [
            pl.BlockSpec(w.shape, lambda i: (0, 0), pipeline_mode=pl.Buffered(1)) for w in weights
        ],
        out_specs=tuple(pl.BlockSpec((tile, cols), lambda i: (i, 0)) for cols, _ in outs),
        compiler_params=pltpu.CompilerParams(vmem_limit_bytes=50 << 20),
        name=name,
    )(*streamed, *weights)


SWAP_CORE = [(0, 1), (1, 0), (2, 3), (3, 2)]
SWAP_PAIR = [(0, 2), (2, 0), (1, 3), (3, 1)]


def tp_swap(value, pairs, groups=None):
    if groups is None:
        return lax.ppermute(value, "tp", pairs)
    size = lax.axis_size("tp")
    flat = [(g * size + source, g * size + target) for g in groups for source, target in pairs]
    return lax.ppermute(value, ("grp", "tp"), flat)


def core_swap(value, groups=None):
    return tp_swap(value, SWAP_CORE, groups)


def pair_swap(value, groups=None):
    return tp_swap(value, SWAP_PAIR, groups)


def gather_tokens(own, meanwhile=None):
    far = pair_swap(own)
    if meanwhile is not None:
        far = after(far, meanwhile(own))
    return jnp.concatenate([own, far, core_swap(own), core_swap(far)], axis=0)


def reduce_tokens(partial_bf, meanwhile=None, groups=None):
    count = partial_bf.shape[0] // 4
    other = core_swap(partial_bf[2 * count :], groups)
    half = partial_bf[: 2 * count].astype(F32) + other.astype(F32)
    away = half[count:].astype(BF16)
    far = pair_swap(away, groups)
    if meanwhile is not None:
        far = after(far, meanwhile(away))
    return half[:count] + far.astype(F32)


class Groups:
    def __init__(self):
        self.count = lax.axis_size("grp")
        self.quarter = self.count // 4
        where = lax.axis_index("grp")
        self.where = where
        self.role = where // self.quarter
        self.place = where % self.quarter
        self.is_enc = self.role < 3
        self.peers = [
            [a * self.quarter + j for j in range(self.quarter)] for a in range(4)
        ]
        self.swap = [(i, i ^ 1) for i in range(self.count)]
        self.swapped = None
        self.roles = [
            [a * self.quarter + j for a in range(4)] for j in range(self.quarter)
        ]

    def shift(self, value, steps):
        hop = steps * self.quarter
        return lax.ppermute(
            value, "grp", [(i, (i + hop) % self.count) for i in range(self.count)]
        )

    def send(self, value, source, target):
        q = self.quarter
        return lax.ppermute(
            value, "grp", [(source * q + j, target * q + j) for j in range(q)]
        )

    def gather(self, chunks):
        fulls, last, brought = [], {}, []
        for enc, dec in chunks:
            rows, cols = enc.shape
            shards = [jnp.where(self.is_enc, enc, dec)]
            for step in (1, 2, 3):
                payload = jnp.where((self.role + step) % 4 < 3, enc, dec)
                if step in last:
                    payload = after(payload, last[step])
                last[step] = self.shift(payload, step)
                shards.append(last[step])
            brought.append(tuple(shards[1:]))
            full = jnp.zeros((4, self.quarter, rows, cols), enc.dtype)
            for step, shard in enumerate(shards):
                source = (self.role - step) % 4
                if self.quarter == 2:
                    other = lax.ppermute(shard, "grp", self.swap)
                    full = lax.dynamic_update_slice(
                        full, shard[None, None], (source, self.place, 0, 0)
                    )
                    full = lax.dynamic_update_slice(
                        full, other[None, None], (source, 1 - self.place, 0, 0)
                    )
                else:
                    group = lax.all_gather(shard, "grp", axis_index_groups=self.peers)
                    full = lax.dynamic_update_slice(full, group[None], (source, 0, 0, 0))
            fulls.append(full.reshape(-1, cols))
        return fulls, brought

    def gather_whole(self, enc, dec, pieces, *anchors):
        rows, cols = enc.shape
        payload = jnp.stack([enc, enc, enc, dec])
        held = self.to_quarters(after(payload, *anchors) if anchors else payload)
        if self.quarter == 2:
            full = jnp.zeros((4, 2, rows, cols), enc.dtype)
            full = lax.dynamic_update_slice(full, held[:, None], (0, self.place, 0, 0))
            for low in range(0, 4, 4 // pieces):
                piece = held[low : low + 4 // pieces]
                if self.swapped is not None:
                    piece = after(piece, self.swapped)
                self.swapped = lax.ppermute(piece, "grp", self.swap)
                full = lax.dynamic_update_slice(
                    full, self.swapped[:, None], (low, 1 - self.place, 0, 0)
                )
        else:
            full = lax.all_gather(held, "grp", axis=1, axis_index_groups=self.peers)
        return full.reshape(-1, cols), held

    def to_quarters(self, blocks):
        return lax.all_to_all(
            blocks, "grp", 0, 0, tiled=True, axis_index_groups=self.roles
        )

    def peer_sum(self, value):
        if self.quarter == 2:
            return value + lax.ppermute(value, "grp", self.swap)
        return lax.psum(value, "grp", axis_index_groups=self.peers)

    def role_sums(self, mine):
        enc_total, dec_total = 0.0, 0.0
        for step in range(4):
            target = (self.role + step) % 4
            block = lax.dynamic_index_in_dim(mine, target, 0, keepdims=False)
            if step:
                block = self.shift(block, step)
            block = block.astype(F32)
            source_enc = (self.role - step) % 4 < 3
            enc_total = enc_total + jnp.where(source_enc, block, 0.0)
            dec_total = dec_total + jnp.where(source_enc, 0.0, block)
        return enc_total, dec_total

    def to_place(self, product):
        return lax.psum_scatter(
            product, "grp", scatter_dimension=0, axis_index_groups=self.peers
        )

    def to_owner(self, mine):
        parts = self.to_quarters(mine).astype(F32)
        return parts[0] + parts[1] + parts[2], parts[3]

    def all_role_sums(self, value):
        value = self.peer_sum(value)
        return self.role_sums(jnp.broadcast_to(value[None], (4,) + value.shape))


def pad_rows(value, count):
    return jnp.pad(value, ((0, count - value.shape[0]), (0, 0)))


class DecoderRows:
    def __init__(self, tp, count, stride):
        self.count, self.stride, self.tp = count, stride, tp

    @staticmethod
    def flip(index):
        return (index % 2) * 2 + index // 2

    def to_rows(self, value, stride):
        return jnp.concatenate(
            [
                lax.dynamic_slice_in_dim(
                    value, self.flip(i ^ self.tp) * stride, self.count, axis=0
                )
                for i in range(4)
            ],
            axis=0,
        )

    def to_relative(self, value, stride):
        return jnp.concatenate(
            [
                pad_rows(
                    lax.dynamic_slice_in_dim(
                        value, (self.flip(b) ^ self.tp) * self.count, self.count, axis=0
                    ),
                    stride,
                )
                for b in range(4)
            ],
            axis=0,
        )


def body(
    enc_in,
    dec_in,
    dec_cot,
    enc_seg,
    dec_seg,
    enc_norm1,
    enc_wq,
    enc_wk,
    enc_wv,
    enc_wo,
    enc_table,
    enc_norm2,
    enc_wgate,
    enc_wup,
    enc_wdown,
    enc_normf,
    dec_norm1,
    dec_wq,
    dec_wk,
    dec_wv,
    dec_wo,
    dec_table,
    dec_norm2,
    cross_wq,
    cross_wk,
    cross_wv,
    cross_wo,
    dec_norm3,
    dec_wgate,
    dec_wup,
    dec_wdown,
):
    groups = Groups()
    is_enc = groups.is_enc
    tp = lax.axis_index("tp")
    tp_arg = tp.astype(jnp.int32)[None]
    heads = enc_table.shape[1]
    width = heads * HEAD_DIM
    enc_count = enc_in.shape[1]
    dec_count = dec_in.shape[1]
    enc_len = enc_seg.shape[-1]
    rows = DecoderRows(tp, dec_count, enc_count)

    def columns(parts):
        return jnp.concatenate(parts, axis=1)

    x_own = jnp.where(is_enc, enc_in[0], pad_rows(dec_in[0], enc_count))
    x_all = gather_tokens(x_own)
    units = enc_wgate.shape[1]
    padded = -units % 128

    def first_chunk(weights, gains, w_out):
        gains = jnp.pad(jnp.stack(gains, axis=1), ((0, 0), (0, -len(gains) % 64)))
        parts = columns(list(weights) + [gains, w_out])
        return jnp.pad(parts, ((0, 0), (0, -parts.shape[1] % 128)))

    def wide(weight):
        return jnp.pad(weight, ((0, 0), (0, padded)))

    (first,), brought = groups.gather(
        [
            (
                first_chunk(
                    [enc_wq, enc_wk, enc_wv], [enc_norm1, enc_norm2, enc_normf], enc_wo.T
                ),
                first_chunk(
                    [dec_wq, dec_wk, dec_wv], [dec_norm1, dec_norm2, dec_norm3], dec_wo.T
                ),
            ),
        ]
    )
    w_gate, held_gate = groups.gather_whole(
        wide(enc_wgate), wide(dec_wgate), 2, brought[0][0]
    )
    w_up, held_up = groups.gather_whole(wide(enc_wup), wide(dec_wup), 2, held_gate)
    w_down, held_down = groups.gather_whole(wide(enc_wdown.T), wide(dec_wdown.T), 2, held_up)
    w_cross, held_cross = groups.gather_whole(
        columns([cross_wk, cross_wv]), columns([cross_wq, cross_wo.T]), 1, held_down
    )
    w_qkv = first[:, : 3 * width]
    gains = first[:, 3 * width : 3 * width + 3].astype(F32).T
    gains = after(gains, held_gate)
    gain1, gain2, gain3 = gains[0:1], gains[1:2], gains[2:3]
    w_out = first[:, 3 * width + 64 : 4 * width + 64]
    w_cq, w_co = w_cross[:, :width], w_cross[:, width:]
    cot_own = dec_cot[0]
    enc_table, dec_table = after((enc_table, dec_table), brought[0])

    enc_ids = enc_seg[0, 0].astype(F32)
    ids_rel = jnp.concatenate(
        [
            lax.dynamic_slice_in_dim(enc_ids, (DecoderRows.flip(b) ^ tp) * enc_count, enc_count)
            for b in range(4)
        ]
    )
    dec_ids = dec_seg[0]
    enc_hot = one_hot_blocks(enc_relative(), True)
    dec_hot = one_hot_blocks(dec_relative(), False)
    enc_bias = dot(enc_table, jnp.asarray(enc_hot, BF16), TN).reshape(heads, 5, QB, QB)
    dec_bias = dot(dec_table, jnp.asarray(dec_hot, BF16), TN).reshape(heads, DEC_LEN, DEC_LEN)

    enc_cfg = dict(
        name="enc", heads=heads, bq=QB, bk=enc_len, steps=enc_len // QB, follow=False,
        bias="blocks", causal=False, k=width, v=2 * width,
    )
    dec_cfg = dict(
        name="dec", heads=heads, bq=DEC_LEN, bk=DEC_LEN, steps=3, follow=True,
        bias="full", causal=True, k=width, v=2 * width,
    )
    cross_cfg = dict(
        name="cross", heads=heads, bq=DEC_LEN, bk=enc_len, steps=1, follow=False,
        bias=None, causal=False, k=0, v=width,
    )
    enc_idk = jnp.broadcast_to(ids_rel[:, None], (enc_len, QB))
    enc_idq = ids_rel.reshape(enc_len // QB, 1, QB)
    dec_idk = jnp.broadcast_to(dec_ids.astype(F32).reshape(-1, 1), (3 * DEC_LEN, DEC_LEN))
    dec_idq = dec_ids.astype(F32).reshape(3, 1, DEC_LEN)
    cross_idk = jnp.broadcast_to(ids_rel[:, None], (enc_len, DEC_LEN))

    x_f32 = x_own.astype(F32)
    norm1_all = rms_scale(x_all.astype(F32), gain1).astype(BF16)
    qkv = dot(norm1_all, w_qkv, NN).astype(BF16)

    def enc_attend(qkv):
        return attention_forward(enc_cfg, tp_arg, qkv, qkv, enc_idk, enc_idq, enc_bias)

    def dec_attend(qkv):
        ordered = rows.to_rows(qkv, enc_count)
        out, lse = attention_forward(dec_cfg, tp_arg, ordered, ordered, dec_idk, dec_idq, dec_bias)
        return rows.to_relative(out, enc_count), jnp.pad(
            lse.reshape(-1), (0, heads * enc_len - lse.size)
        ).reshape(enc_len // QB, heads, QB)

    att, lse1 = lax.cond(is_enc, enc_attend, dec_attend, after(qkv, held_gate))
    x1 = x_f32 + reduce_tokens(dot(after(att, held_up), w_out, NT).astype(BF16))

    norm2_all = gather_tokens(after(rms_scale(x1, gain2).astype(BF16), held_down))
    cot_all = gather_tokens(after(cot_own, norm2_all))
    feed_weights = (w_gate, w_up, after(w_down, held_cross))
    wide_units = w_gate.shape[1]
    width_all = x_own.shape[1]
    feed_out2, gate2, up2 = feed_call(
        "feed_forward", feed_kernel, 256, (norm2_all,), feed_weights,
        ((width_all, BF16), (wide_units, F32), (wide_units, F32)),
    )
    queries = {}

    def while_feed(anchor):
        dec_q_rel = dot(after(norm2_all, anchor), w_cq, NN).astype(BF16)
        dec_q = rows.to_rows(dec_q_rel, enc_count).reshape(3, DEC_LEN, width)
        dec_q = jnp.concatenate([dec_q, dec_ids.astype(BF16)[:, :, None]], axis=2)
        queries["sent"] = sum(groups.send(dec_q[r], 3, r) for r in range(3))
        return queries["sent"]

    x2 = x1 + reduce_tokens(feed_out2)
    memory = gather_tokens(rms_scale(x2, gain3).astype(BF16), while_feed)
    cross_idq = queries["sent"][:, width].astype(F32).reshape(1, 1, DEC_LEN)
    cross_q = queries["sent"][:, :width]

    cross_kv = dot(memory, w_cross, NN).astype(BF16)
    cross_o, lse2 = attention_forward(cross_cfg, tp_arg, cross_q, cross_kv, cross_idk, cross_idq)
    dec_o = jnp.concatenate([groups.send(cross_o, r, 3) for r in range(3)], axis=0)
    dec_o_rel = rows.to_relative(dec_o, dec_count)

    x2d = x1[:dec_count] + reduce_tokens(dot(dec_o_rel, w_co, NT).astype(BF16))
    norm3_all = gather_tokens(rms_scale(x2d, gain3).astype(BF16))
    grad_outs = ((width_all, BF16), (2 * wide_units, BF16), (wide_units, BF16))
    partial_n3, both3, hidden3, feed_out3 = feed_call(
        "feed_both", feed_both_kernel, 288, (norm3_all, cot_all), feed_weights,
        grad_outs + ((width_all, BF16),),
    )
    grad_n3 = reduce_tokens(partial_n3)
    grad_step, gain_d3 = norm_backward(x2d, gain3, grad_n3)
    grad_x2d = cot_own.astype(F32) + grad_step
    grad2_all = gather_tokens(grad_x2d.astype(BF16))
    grad_o_rel = dot(grad2_all, w_co, NN).astype(BF16)
    grad_o_rows = rows.to_rows(grad_o_rel, dec_count).reshape(3, DEC_LEN, width)
    cross_go = sum(groups.send(grad_o_rows[r], 3, r) for r in range(3))
    dec_groups = range(3 * groups.quarter, groups.count)
    dec_out = x2d + reduce_tokens(after(feed_out3, cross_go), None, dec_groups)

    cross_gq, cross_gkv = attention_backward(
        cross_cfg, tp_arg, cross_q, cross_kv, cross_idk, cross_idq, lse2, cross_go
    )
    dec_gq = jnp.concatenate([groups.send(cross_gq, r, 3) for r in range(3)], axis=0)
    dec_gq_rel = rows.to_relative(dec_gq, enc_count)
    placed = {}

    def while_memory(anchor):
        left, right = after((memory, norm2_all), anchor)
        (product,) = token_product(
            groups,
            (2 * width,),
            (0, left, cross_gkv),
            (1, right, dec_gq_rel),
            (1, grad2_all, dec_o_rel),
        )
        placed["cross"] = groups.to_place(product)
        return product

    grad_memory = reduce_tokens(dot(cross_gkv, w_cross, NT).astype(BF16), while_memory)
    grad_memory = grad_memory.astype(BF16).astype(F32)
    grad_e2, gain_ef = norm_backward(x2, gain3, grad_memory)

    grad_e2_all = gather_tokens(grad_e2.astype(BF16))
    partial_n2, both2, hidden2 = feed_call(
        "feed_back", feed_back_kernel, 256, (gate2, up2, grad_e2_all), feed_weights, grad_outs
    )

    def input_product(index, anchor):
        tokens, others = after((norm2_all, norm3_all), anchor)
        (product,) = token_product(
            groups, (wide_units,), (0, tokens, both2, index), (1, others, both3, index)
        )
        placed[index] = groups.to_place(product)
        return product

    product = input_product(0, partial_n2)
    dec_partial = dot(after(dec_gq_rel, product), w_cq, NT).astype(BF16)
    partial_n2 = jnp.where(is_enc, partial_n2, dec_partial)

    def while_n2(anchor):
        grads, others = after((grad_e2_all, cot_all), input_product(1, anchor))
        (product,) = token_product(
            groups, (wide_units,), (0, grads, hidden2), (1, others, hidden3)
        )
        placed[2] = groups.to_place(product)
        return product

    sums = {}
    grad_n2 = reduce_tokens(partial_n2, while_n2)
    grad_step, gain_2 = norm_backward(x1, gain2, grad_n2)
    grad_x1 = jnp.where(is_enc, grad_e2, pad_rows(grad_x2d, enc_count)) + grad_step
    sums["cross"] = groups.to_owner(after(placed["cross"], product))
    sums[0] = groups.to_owner(after(placed[0], sums["cross"]))

    grad_x1_all = gather_tokens(after(grad_x1.astype(BF16), placed[0]))
    grad_att = dot(grad_x1_all, w_out, NN).astype(BF16)
    grad_att, sums[0] = lax.optimization_barrier((grad_att, sums[0]))
    def enc_attend_back(qkv, lse, grad_att):
        gq, gkv, gb = attention_backward(
            enc_cfg, tp_arg, qkv, qkv, enc_idk, enc_idq, lse, grad_att, enc_bias
        )
        return columns([gq, gkv]), gb.reshape(heads, -1)

    def dec_attend_back(qkv, lse, grad_att):
        ordered = rows.to_rows(qkv, enc_count)
        lse = lse.reshape(-1)[: 3 * heads * DEC_LEN].reshape(3, heads, DEC_LEN)
        gq, gkv, gb = attention_backward(
            dec_cfg, tp_arg, ordered, ordered, dec_idk, dec_idq, lse,
            rows.to_rows(grad_att, enc_count), dec_bias,
        )
        gb = gb.reshape(heads, -1)
        return (
            rows.to_relative(columns([gq, gkv]), enc_count),
            jnp.pad(gb, ((0, 0), (0, enc_hot.shape[1] - gb.shape[1]))),
        )

    grad_qkv, grad_bias = lax.cond(is_enc, enc_attend_back, dec_attend_back, qkv, lse1, grad_att)
    sums[1] = groups.to_owner(after(placed[1], sums[0]))
    partial_n1 = dot(grad_qkv, w_qkv, NT).astype(BF16)
    partial_n1, sums[1] = lax.optimization_barrier((partial_n1, sums[1]))

    def while_n1(anchor):
        left, right = after((norm1_all, grad_x1_all), anchor)
        (product,) = token_product(
            groups,
            (4 * width,),
            (0, left, grad_qkv),
            (0, right, att),
            (1, left, grad_qkv),
            (1, right, att),
        )
        placed["first"] = groups.to_place(product)
        tables["grad"] = lax.cond(
            is_enc,
            lambda gb: bucket_sums(enc_hot, gb),
            lambda gb: bucket_sums(dec_hot, gb[:, : dec_hot.shape[1]]),
            after(grad_bias, product),
        )
        return product, tables["grad"]

    tables = {}

    sums[2] = groups.to_owner(after(placed[2], sums[1]))
    grad_n1 = reduce_tokens(partial_n1, while_n1)
    grad_n1, sums[2] = lax.optimization_barrier((grad_n1, sums[2]))
    grad_step, gain_1 = norm_backward(x_f32, gain1, grad_n1)
    grad_x = grad_x1 + grad_step
    enc_first, dec_first = groups.to_owner(after(placed["first"], sums[2]))
    enc_cross, dec_cross = sums["cross"]
    (enc_gate, dec_gate), (enc_up, dec_up), (enc_down, dec_down) = sums[0], sums[1], sums[2]

    gain_rows = jnp.stack([gain_1, gain_2, jnp.where(is_enc, gain_ef, gain_d3)])
    gain_rows = gain_rows + core_swap(gain_rows)
    gain_rows = gain_rows + pair_swap(gain_rows)
    small = jnp.concatenate([gain_rows.reshape(-1), tables["grad"].reshape(-1)])
    length = small.shape[0]
    small = jnp.pad(small, (0, -length % 1024)).reshape(-1, 128)
    enc_small, dec_small = groups.all_role_sums(small)

    def unpack(total):
        flat = total.reshape(-1)
        gain = flat[: gain_rows.size].reshape(gain_rows.shape)
        share = gain.shape[1] // groups.count
        mine = lax.dynamic_slice_in_dim(gain, groups.where * share, share, axis=1)
        return mine, flat[gain_rows.size : length].reshape(BUCKETS, heads)

    enc_gains, enc_table_grad = unpack(enc_small)
    dec_gains, dec_table_grad = unpack(dec_small)

    def part(value, index):
        return value[:, index * width : (index + 1) * width]

    zero_bf = jnp.zeros((), BF16)
    return (
        jnp.where(is_enc, zero_bf, dec_out.astype(BF16))[None],
        jnp.where(is_enc, grad_x.astype(BF16), zero_bf)[None],
        jnp.where(is_enc, zero_bf, grad_x[:dec_count].astype(BF16))[None],
        enc_gains[0],
        part(enc_first, 0),
        part(enc_first, 1),
        part(enc_first, 2),
        part(enc_first, 3).T,
        enc_table_grad,
        enc_gains[1],
        enc_gate[:, :units],
        enc_up[:, :units],
        enc_down[:, :units].T,
        enc_gains[2],
        dec_gains[0],
        part(dec_first, 0),
        part(dec_first, 1),
        part(dec_first, 2),
        part(dec_first, 3).T,
        dec_table_grad,
        dec_gains[1],
        part(dec_cross, 0),
        part(enc_cross, 0),
        part(enc_cross, 1),
        part(dec_cross, 1).T,
        dec_gains[2],
        dec_gate[:, :units],
        dec_up[:, :units],
        dec_down[:, :units].T,
    )


def solution(mesh):
    vector, matrix, turned = P("grp"), P("grp", "tp"), P("tp", "grp")
    tokens, ids, table = P("grp", "tp", None), P("grp", None, None), P(None, "tp")
    enc = (vector, matrix, matrix, matrix, turned, table, vector, matrix, matrix, turned, vector)
    dec = (vector, matrix, matrix, matrix, turned, table, vector, matrix, matrix, matrix, turned)
    dec = dec + (vector, matrix, matrix, turned)
    return jax.shard_map(
        body,
        mesh=mesh,
        in_specs=(tokens, tokens, tokens, ids, ids) + enc + dec,
        out_specs=(tokens, tokens, tokens) + enc + dec,
        check_vma=False,
    )
```

```python
import math
from functools import partial

import jax
import jax.numpy as jnp
import numpy as np
from jax import lax
from jax.experimental import pallas as pl
from jax.experimental.pallas import tpu as pltpu
from jax.sharding import PartitionSpec as P

HEAD_DIM = 64
BUCKETS = 32
MAX_DIST = 128
DEC_LEN = 192
EPSILON = 1e-06
NEG_FILL = -1e30
QB = 128
F32 = jnp.float32
BF16 = jnp.bfloat16


def bucket_of(relative, two_sided):
    bucket_count = BUCKETS
    shifted = relative * 0
    if two_sided:
        bucket_count = bucket_count // 2
        shifted = shifted + (relative > 0) * bucket_count
        distance = np.abs(relative)
    else:
        distance = np.maximum(-relative, 0)
    exact_span = bucket_count // 2
    log_ratio = np.log(np.maximum(distance, 1) / exact_span) / np.log(MAX_DIST / exact_span)
    farther = np.minimum(
        exact_span + np.floor(log_ratio * (bucket_count - exact_span) + 1e-09).astype(np.int32),
        bucket_count - 1,
    )
    return (shifted + np.where(distance < exact_span, distance, farther)).astype(np.int32)


def one_hot_blocks(relative, two_sided):
    return np.eye(BUCKETS, dtype=np.float32)[:, bucket_of(relative, two_sided).reshape(-1)]


def enc_relative():
    return np.arange(-2 * QB, 3 * QB)[:, None] - np.arange(QB)[None, :]


def dec_relative():
    return np.arange(DEC_LEN)[:, None] - np.arange(DEC_LEN)[None, :]


def after(value, *others):
    return lax.optimization_barrier((value,) + others)[0]


def dot(left, right, dims):
    return lax.dot_general(left, right, (dims, ((), ())), preferred_element_type=F32)


NN = ((1,), (0,))
NT = ((1,), (1,))
TN = ((0,), (0,))


def block_of(place, tp):
    wide = place // 2
    swapped = (wide % 2) * 2 + wide // 2
    return (swapped ^ tp) * 2 + place % 2


def scores_t(head, cfg, keys, queries, bias_ref, same, place, tp):
    lanes = slice(head * HEAD_DIM, (head + 1) * HEAD_DIM)
    scores = dot(keys[:, lanes], queries[:, lanes], NT)
    if cfg["bias"] == "blocks":
        mine = block_of(place, tp)
        parts = []
        for kb in range(keys.shape[0] // QB):
            step = jnp.clip(block_of(kb, tp) - mine, -2, 2) + 2
            parts.append(bias_ref[head, step])
        scores = scores + jnp.concatenate(parts, axis=0)
    elif cfg["bias"] == "full":
        scores = scores + bias_ref[head]
    return jnp.where(same, scores, NEG_FILL)


def allowed_t(cfg, idk_ref, idq_ref):
    same = idk_ref[...] == idq_ref[0]
    if cfg["causal"]:
        key_pos = lax.broadcasted_iota(jnp.int32, same.shape, 0)
        query_pos = lax.broadcasted_iota(jnp.int32, same.shape, 1)
        same = same & (key_pos <= query_pos)
    return same


def forward_kernel(cfg, tp_ref, q_ref, kv_ref, idk_ref, idq_ref, *rest):
    if cfg["bias"]:
        bias_ref, out_ref, lse_ref, vt_ref = rest
    else:
        bias_ref, (out_ref, lse_ref, vt_ref) = None, rest
    heads = cfg["heads"]
    width = heads * HEAD_DIM
    place = pl.program_id(0)
    keys = kv_ref[:, cfg["k"] : cfg["k"] + width]

    def fill():
        vt_ref[...] = kv_ref[:, cfg["v"] : cfg["v"] + width].T

    if cfg["follow"]:
        fill()
    else:
        pl.when(place == 0)(fill)
    queries = q_ref[:, :width]
    same = allowed_t(cfg, idk_ref, idq_ref)
    outs = []
    for head in range(heads):
        scores = scores_t(head, cfg, keys, queries, bias_ref, same, place, tp_ref[0])
        peak = jnp.max(scores, axis=0, keepdims=True)
        exponent = jnp.exp(scores - peak)
        total = jnp.sum(exponent, axis=0, keepdims=True)
        weights = (exponent * (1.0 / total)).astype(BF16)
        outs.append(dot(vt_ref[head * HEAD_DIM : (head + 1) * HEAD_DIM, :], weights, NN))
        lse_ref[0, head : head + 1, :] = peak + jnp.log(total)
    out_ref[...] = jnp.concatenate(outs, axis=0).T.astype(BF16)


def backward_kernel(cfg, tp_ref, q_ref, kv_ref, idk_ref, idq_ref, *rest):
    if cfg["bias"]:
        bias_ref, lse_ref, go_ref, gq_ref, gkv_ref, gb_ref, kt_ref, acc_ref = rest
    else:
        bias_ref, gb_ref = None, None
        lse_ref, go_ref, gq_ref, gkv_ref, kt_ref, acc_ref = rest
    heads = cfg["heads"]
    width = heads * HEAD_DIM
    place = pl.program_id(0)
    keys = kv_ref[:, cfg["k"] : cfg["k"] + width]
    values = kv_ref[:, cfg["v"] : cfg["v"] + width]

    def clear():
        kt_ref[...] = kv_ref[:, cfg["k"] : cfg["k"] + width].T
        acc_ref[...] = jnp.zeros_like(acc_ref)

    def clear_bias():
        if gb_ref is not None:
            gb_ref[...] = jnp.zeros_like(gb_ref)

    pl.when(place == 0)(clear_bias)
    if cfg["follow"]:
        clear()
    else:
        pl.when(place == 0)(clear)
    queries = q_ref[:, :width]
    grad_out = go_ref[...]
    same = allowed_t(cfg, idk_ref, idq_ref)
    grads = []
    for head in range(heads):
        lanes = slice(head * HEAD_DIM, (head + 1) * HEAD_DIM)
        scores = scores_t(head, cfg, keys, queries, bias_ref, same, place, tp_ref[0])
        weights = jnp.exp(scores - lse_ref[0, head : head + 1, :])
        grad_weights = dot(values[:, lanes], grad_out[:, lanes], NT)
        delta = jnp.sum(grad_weights * weights, axis=0, keepdims=True)
        grad_scores = weights * (grad_weights - delta)
        if cfg["bias"] == "blocks":
            mine = block_of(place, tp_ref[0])
            for kb in range(keys.shape[0] // QB):
                step = jnp.clip(block_of(kb, tp_ref[0]) - mine, -2, 2) + 2
                gb_ref[head, step] += grad_scores[kb * QB : (kb + 1) * QB]
        elif cfg["bias"] == "full":
            gb_ref[head] += grad_scores
        scores_bf = grad_scores.astype(BF16)
        acc_ref[head] += dot(scores_bf, queries[:, lanes], NN)
        acc_ref[heads + head] += dot(weights.astype(BF16), grad_out[:, lanes], NN)
        grads.append(dot(kt_ref[lanes, :], scores_bf, NN))
    gq_ref[...] = jnp.concatenate(grads, axis=0).T.astype(BF16)

    def finish():
        gkv_ref[...] = jnp.concatenate(
            [acc_ref[k].astype(BF16) for k in range(2 * heads)], axis=1
        )

    if cfg["follow"]:
        finish()
    else:
        pl.when(place == pl.num_programs(0) - 1)(finish)


def attention_specs(cfg, q_cols, kv_cols, bias):
    bq, bk = cfg["bq"], cfg["bk"]
    follow = cfg["follow"]
    specs = [
        pl.BlockSpec((bq, q_cols), lambda i, s: (i, 0)),
        pl.BlockSpec((bk, kv_cols), (lambda i, s: (i, 0)) if follow else (lambda i, s: (0, 0))),
        pl.BlockSpec((bk, bq), (lambda i, s: (i, 0)) if follow else (lambda i, s: (0, 0))),
        pl.BlockSpec((1, 1, bq), lambda i, s: (i, 0, 0)),
    ]
    if bias is not None:
        rank = bias.ndim
        specs.append(pl.BlockSpec(bias.shape, lambda i, s: (0,) * rank))
    return specs


def attention_forward(cfg, tp, q, kv, idk, idq, bias=None):
    heads, bq, bk, steps = cfg["heads"], cfg["bq"], cfg["bk"], cfg["steps"]
    width = heads * HEAD_DIM
    extra = () if bias is None else (bias,)
    return pl.pallas_call(
        partial(forward_kernel, cfg),
        out_shape=(
            jax.ShapeDtypeStruct((steps * bq, width), BF16),
            jax.ShapeDtypeStruct((steps, heads, bq), F32),
        ),
        grid_spec=pltpu.PrefetchScalarGridSpec(
            num_scalar_prefetch=1,
            grid=(steps,),
            in_specs=attention_specs(cfg, q.shape[1], kv.shape[1], bias),
            out_specs=(
                pl.BlockSpec((bq, width), lambda i, s: (i, 0)),
                pl.BlockSpec((1, heads, bq), lambda i, s: (i, 0, 0)),
            ),
            scratch_shapes=[pltpu.VMEM((width, bk), BF16)],
        ),
        compiler_params=pltpu.CompilerParams(vmem_limit_bytes=40 << 20),
        name=cfg["name"] + "_forward",
    )(tp, q, kv, idk, idq, *extra)


def attention_backward(cfg, tp, q, kv, idk, idq, lse, grad_out, bias=None):
    heads, bq, bk, steps = cfg["heads"], cfg["bq"], cfg["bk"], cfg["steps"]
    width = heads * HEAD_DIM
    follow = cfg["follow"]
    extra = () if bias is None else (bias,)
    out_shape = [
        jax.ShapeDtypeStruct((steps * bq, width), BF16),
        jax.ShapeDtypeStruct((steps * bk if follow else bk, 2 * width), BF16),
    ]
    out_specs = [
        pl.BlockSpec((bq, width), lambda i, s: (i, 0)),
        pl.BlockSpec((bk, 2 * width), (lambda i, s: (i, 0)) if follow else (lambda i, s: (0, 0))),
    ]
    if bias is not None:
        rank = bias.ndim
        out_shape.append(jax.ShapeDtypeStruct(bias.shape, F32))
        out_specs.append(pl.BlockSpec(bias.shape, lambda i, s: (0,) * rank))
    return pl.pallas_call(
        partial(backward_kernel, cfg),
        out_shape=tuple(out_shape),
        grid_spec=pltpu.PrefetchScalarGridSpec(
            num_scalar_prefetch=1,
            grid=(steps,),
            in_specs=attention_specs(cfg, q.shape[1], kv.shape[1], bias)
            + [
                pl.BlockSpec((1, heads, bq), lambda i, s: (i, 0, 0)),
                pl.BlockSpec((bq, width), lambda i, s: (i, 0)),
            ],
            out_specs=tuple(out_specs),
            scratch_shapes=[pltpu.VMEM((width, bk), BF16), pltpu.VMEM((2 * heads, bk, HEAD_DIM), F32)],
        ),
        compiler_params=pltpu.CompilerParams(vmem_limit_bytes=48 << 20),
        name=cfg["name"] + "_backward",
    )(tp, q, kv, idk, idq, *extra, lse, grad_out)


def product_kernel(quarter, share, step, jobs, widths, role_ref, *refs):
    operands, out_refs = refs[: 2 * len(jobs)], refs[2 * len(jobs) :]
    starts = [sum(widths[:k]) for k in range(len(widths))]
    for index, (on_role, column) in enumerate(jobs):
        left_ref, right_ref = operands[2 * index], operands[2 * index + 1]

        @pl.when(role_ref[0] == on_role)
        def _():
            result = dot(left_ref[...], right_ref[...], TN).astype(BF16)
            rows_here, cols_here = result.shape
            first = pl.program_id(0) * (rows_here // step)
            for unit in range(rows_here // step):
                row = (first + unit) * step
                owner, offset = row // share, pl.multiple_of(row % share, step)
                for out_ref, start, cols in zip(out_refs, starts, widths):
                    low, high = max(start, column), min(start + cols, column + cols_here)
                    if low < high:
                        out_ref[
                            owner % quarter,
                            owner // quarter,
                            pl.ds(offset, step),
                            low - start : high - start,
                        ] = result[unit * step : (unit + 1) * step, low - column : high - column]


def token_product(groups, widths, *jobs):
    rows_count = jobs[0][1].shape[1]
    tile = 256
    share = rows_count // groups.count
    step = math.gcd(share, 64)
    offsets, described, operands, specs = {}, [], [], []
    for role, left, right, *block in jobs:
        count, cols = right.shape
        cols = sum(widths) if block else cols
        described.append((role, offsets.get(role, 0)))
        offsets[role] = offsets.get(role, 0) + cols

        def left_map(i, s, role=role):
            return (0, jnp.where(s[0] == role, i, 0))

        operands += [left, right]
        specs += [
            pl.BlockSpec((count, tile), left_map),
            pl.BlockSpec(
                (count, cols),
                lambda i, s, block=(block or [0])[0]: (0, block),
                pipeline_mode=pl.Buffered(1),
            ),
        ]
    shapes = [(groups.quarter, 4, share, cols) for cols in widths]
    role = jnp.where(groups.is_enc, 0, 1).astype(jnp.int32)[None]
    return pl.pallas_call(
        partial(product_kernel, groups.quarter, share, step, described, widths),
        out_shape=tuple(jax.ShapeDtypeStruct(dims, BF16) for dims in shapes),
        grid_spec=pltpu.PrefetchScalarGridSpec(
            num_scalar_prefetch=1,
            grid=(rows_count // tile,),
            in_specs=specs,
            out_specs=tuple(pl.BlockSpec(dims, lambda i, s: (0, 0, 0, 0)) for dims in shapes),
        ),
        compiler_params=pltpu.CompilerParams(vmem_limit_bytes=56 << 20),
        name="token_product",
    )(role, *operands)


def bucket_sums(hot, values):
    high = values.astype(BF16)
    low = (values - high.astype(F32)).astype(BF16)
    sums = dot(jnp.asarray(hot, BF16), jnp.concatenate([high, low], axis=0), NT)
    return sums[:, : values.shape[0]] + sums[:, values.shape[0] :]


def rms_scale(hidden, gain_vec):
    return (
        hidden * lax.rsqrt(jnp.mean(hidden * hidden, axis=-1, keepdims=True) + EPSILON) * gain_vec
    )


def norm_backward(hidden, gain_vec, grad_out):
    rate = lax.rsqrt(jnp.mean(hidden * hidden, axis=-1, keepdims=True) + EPSILON)
    scaled = gain_vec * grad_out
    inner = jnp.mean(hidden * scaled, axis=-1, keepdims=True)
    grad_in = rate * scaled - hidden * (rate * rate * rate * inner)
    return grad_in, jnp.sum(grad_out * hidden * rate, axis=0)


GELU_SCALE = float(np.sqrt(2.0 / np.pi))
GELU_CUBIC = 0.044715


def gelu_parts(value):
    square = value * value
    tanh = jnp.tanh(GELU_SCALE * (value + GELU_CUBIC * (value * square)))
    half = 0.5 * (1.0 + tanh)
    slope = half + 0.5 * value * (1.0 - tanh * tanh) * (
        GELU_SCALE * (1.0 + 3.0 * GELU_CUBIC * square)
    )
    return value * half, slope


def gelu(value):
    cubic = value + GELU_CUBIC * (value * value * value)
    return value * (0.5 * (1.0 + jnp.tanh(GELU_SCALE * cubic)))


def feed_kernel(tok_ref, wg_ref, wu_ref, wd_ref, out_ref, gate_ref, up_ref):
    tokens = tok_ref[...]
    gate = dot(tokens, wg_ref[...], NN)
    up = dot(tokens, wu_ref[...], NN)
    gate_ref[...] = gate
    up_ref[...] = up
    hidden = (gelu(gate) * up).astype(BF16)
    out_ref[...] = dot(hidden, wd_ref[...], NT).astype(BF16)


def feed_grads(gate, up, grad_hidden, wg_ref, wu_ref, gn_ref, both_ref, hid_ref):
    units = gate.shape[1]
    activated, slope = gelu_parts(gate)
    hid_ref[...] = (activated * up).astype(BF16)
    grad_gate = (grad_hidden * up * slope).astype(BF16)
    grad_up = (grad_hidden * activated).astype(BF16)
    both_ref[:, :units] = grad_gate
    both_ref[:, units:] = grad_up
    gn_ref[...] = (dot(grad_gate, wg_ref[...], NT) + dot(grad_up, wu_ref[...], NT)).astype(BF16)


def feed_back_kernel(gate_ref, up_ref, ga_ref, wg_ref, wu_ref, wd_ref, *outs):
    grad_hidden = dot(ga_ref[...], wd_ref[...], NN)
    feed_grads(gate_ref[...], up_ref[...], grad_hidden, wg_ref, wu_ref, *outs)


def feed_both_kernel(tok_ref, gh_ref, wg_ref, wu_ref, *outs):
    tokens = tok_ref[...]
    gate = dot(tokens, wg_ref[...], NN)
    up = dot(tokens, wu_ref[...], NN)
    feed_grads(gate, up, gh_ref[...], wg_ref, wu_ref, *outs)


def feed_call(name, kernel, tile, streamed, weights, outs):
    count = streamed[0].shape[0]
    return pl.pallas_call(
        kernel,
        out_shape=tuple(jax.ShapeDtypeStruct((count, cols), kind) for cols, kind in outs),
        grid=(count // tile,),
        in_specs=[pl.BlockSpec((tile, a.shape[1]), lambda i: (i, 0)) for a in streamed]
        + [
            pl.BlockSpec(w.shape, lambda i: (0, 0), pipeline_mode=pl.Buffered(1)) for w in weights
        ],
        out_specs=tuple(pl.BlockSpec((tile, cols), lambda i: (i, 0)) for cols, _ in outs),
        compiler_params=pltpu.CompilerParams(vmem_limit_bytes=50 << 20),
        name=name,
    )(*streamed, *weights)


SWAP_CORE = [(0, 1), (1, 0), (2, 3), (3, 2)]
SWAP_PAIR = [(0, 2), (2, 0), (1, 3), (3, 1)]


def tp_swap(value, pairs, groups=None):
    if groups is None:
        return lax.ppermute(value, "tp", pairs)
    size = lax.axis_size("tp")
    flat = [(g * size + source, g * size + target) for g in groups for source, target in pairs]
    return lax.ppermute(value, ("grp", "tp"), flat)


def core_swap(value, groups=None):
    return tp_swap(value, SWAP_CORE, groups)


def pair_swap(value, groups=None):
    return tp_swap(value, SWAP_PAIR, groups)


def gather_tokens(own, meanwhile=None, groups=None):
    far = pair_swap(own, groups)
    if meanwhile is not None:
        far = after(far, meanwhile(own))
    return jnp.concatenate([own, far, core_swap(own, groups), core_swap(far, groups)], axis=0)


def reduce_tokens(partial_bf, meanwhile=None, groups=None):
    count = partial_bf.shape[0] // 4
    other = core_swap(partial_bf[2 * count :], groups)
    half = partial_bf[: 2 * count].astype(F32) + other.astype(F32)
    away = half[count:].astype(BF16)
    far = pair_swap(away, groups)
    if meanwhile is not None:
        far = after(far, meanwhile(away))
    return half[:count] + far.astype(F32)


class Groups:
    def __init__(self):
        self.count = lax.axis_size("grp")
        self.quarter = self.count // 4
        where = lax.axis_index("grp")
        self.where = where
        self.role = where // self.quarter
        self.place = where % self.quarter
        self.is_enc = self.role < 3
        self.peers = [
            [a * self.quarter + j for j in range(self.quarter)] for a in range(4)
        ]
        self.swap = [(i, i ^ 1) for i in range(self.count)]
        self.swapped = None
        self.roles = [
            [a * self.quarter + j for a in range(4)] for j in range(self.quarter)
        ]

    def shift(self, value, steps):
        hop = steps * self.quarter
        return lax.ppermute(
            value, "grp", [(i, (i + hop) % self.count) for i in range(self.count)]
        )

    def send(self, value, source, target):
        q = self.quarter
        return lax.ppermute(
            value, "grp", [(source * q + j, target * q + j) for j in range(q)]
        )

    def gather(self, chunks):
        fulls, last, brought = [], {}, []
        for enc, dec in chunks:
            rows, cols = enc.shape
            shards = [jnp.where(self.is_enc, enc, dec)]
            for step in (1, 2, 3):
                payload = jnp.where((self.role + step) % 4 < 3, enc, dec)
                if step in last:
                    payload = after(payload, last[step])
                last[step] = self.shift(payload, step)
                shards.append(last[step])
            brought.append(tuple(shards[1:]))
            full = jnp.zeros((4, self.quarter, rows, cols), enc.dtype)
            for step, shard in enumerate(shards):
                source = (self.role - step) % 4
                if self.quarter == 2:
                    other = lax.ppermute(shard, "grp", self.swap)
                    full = lax.dynamic_update_slice(
                        full, shard[None, None], (source, self.place, 0, 0)
                    )
                    full = lax.dynamic_update_slice(
                        full, other[None, None], (source, 1 - self.place, 0, 0)
                    )
                else:
                    group = lax.all_gather(shard, "grp", axis_index_groups=self.peers)
                    full = lax.dynamic_update_slice(full, group[None], (source, 0, 0, 0))
            fulls.append(full.reshape(-1, cols))
        return fulls, brought

    def gather_whole(self, enc, dec, pieces, *anchors):
        rows, cols = enc.shape
        payload = jnp.stack([enc, enc, enc, dec])
        held = self.to_quarters(after(payload, *anchors) if anchors else payload)
        if self.quarter == 2:
            full = jnp.zeros((4, 2, rows, cols), enc.dtype)
            full = lax.dynamic_update_slice(full, held[:, None], (0, self.place, 0, 0))
            for low in range(0, 4, 4 // pieces):
                piece = held[low : low + 4 // pieces]
                if self.swapped is not None:
                    piece = after(piece, self.swapped)
                self.swapped = lax.ppermute(piece, "grp", self.swap)
                full = lax.dynamic_update_slice(
                    full, self.swapped[:, None], (low, 1 - self.place, 0, 0)
                )
        else:
            full = lax.all_gather(held, "grp", axis=1, axis_index_groups=self.peers)
        return full.reshape(-1, cols), held

    def to_quarters(self, blocks):
        return lax.all_to_all(
            blocks, "grp", 0, 0, tiled=True, axis_index_groups=self.roles
        )

    def peer_sum(self, value):
        if self.quarter == 2:
            return value + lax.ppermute(value, "grp", self.swap)
        return lax.psum(value, "grp", axis_index_groups=self.peers)

    def role_sums(self, mine):
        enc_total, dec_total = 0.0, 0.0
        for step in range(4):
            target = (self.role + step) % 4
            block = lax.dynamic_index_in_dim(mine, target, 0, keepdims=False)
            if step:
                block = self.shift(block, step)
            block = block.astype(F32)
            source_enc = (self.role - step) % 4 < 3
            enc_total = enc_total + jnp.where(source_enc, block, 0.0)
            dec_total = dec_total + jnp.where(source_enc, 0.0, block)
        return enc_total, dec_total

    def to_place(self, product):
        return lax.psum_scatter(
            product, "grp", scatter_dimension=0, axis_index_groups=self.peers
        )

    def to_owner(self, mine):
        parts = self.to_quarters(mine).astype(F32)
        return parts[0] + parts[1] + parts[2], parts[3]

    def all_role_sums(self, value):
        value = self.peer_sum(value)
        return self.role_sums(jnp.broadcast_to(value[None], (4,) + value.shape))


def pad_rows(value, count):
    return jnp.pad(value, ((0, count - value.shape[0]), (0, 0)))


class DecoderRows:
    def __init__(self, tp, count, stride):
        self.count, self.stride, self.tp = count, stride, tp

    @staticmethod
    def flip(index):
        return (index % 2) * 2 + index // 2

    def to_rows(self, value, stride):
        return jnp.concatenate(
            [
                lax.dynamic_slice_in_dim(
                    value, self.flip(i ^ self.tp) * stride, self.count, axis=0
                )
                for i in range(4)
            ],
            axis=0,
        )

    def to_relative(self, value, stride):
        return jnp.concatenate(
            [
                pad_rows(
                    lax.dynamic_slice_in_dim(
                        value, (self.flip(b) ^ self.tp) * self.count, self.count, axis=0
                    ),
                    stride,
                )
                for b in range(4)
            ],
            axis=0,
        )


def body(
    enc_in,
    dec_in,
    dec_cot,
    enc_seg,
    dec_seg,
    enc_norm1,
    enc_wq,
    enc_wk,
    enc_wv,
    enc_wo,
    enc_table,
    enc_norm2,
    enc_wgate,
    enc_wup,
    enc_wdown,
    enc_normf,
    dec_norm1,
    dec_wq,
    dec_wk,
    dec_wv,
    dec_wo,
    dec_table,
    dec_norm2,
    cross_wq,
    cross_wk,
    cross_wv,
    cross_wo,
    dec_norm3,
    dec_wgate,
    dec_wup,
    dec_wdown,
):
    groups = Groups()
    is_enc = groups.is_enc
    tp = lax.axis_index("tp")
    tp_arg = tp.astype(jnp.int32)[None]
    heads = enc_table.shape[1]
    width = heads * HEAD_DIM
    enc_count = enc_in.shape[1]
    dec_count = dec_in.shape[1]
    enc_len = enc_seg.shape[-1]
    rows = DecoderRows(tp, dec_count, enc_count)

    def columns(parts):
        return jnp.concatenate(parts, axis=1)

    x_own = jnp.where(is_enc, enc_in[0], pad_rows(dec_in[0], enc_count))
    x_all = gather_tokens(x_own)
    units = enc_wgate.shape[1]
    padded = -units % 128

    def first_chunk(weights, gains, w_out):
        gains = jnp.pad(jnp.stack(gains, axis=1), ((0, 0), (0, -len(gains) % 64)))
        parts = columns(list(weights) + [gains, w_out])
        return jnp.pad(parts, ((0, 0), (0, -parts.shape[1] % 128)))

    def wide(weight):
        return jnp.pad(weight, ((0, 0), (0, padded)))

    (first,), brought = groups.gather(
        [
            (
                first_chunk(
                    [enc_wq, enc_wk, enc_wv], [enc_norm1, enc_norm2, enc_normf], enc_wo.T
                ),
                first_chunk(
                    [dec_wq, dec_wk, dec_wv], [dec_norm1, dec_norm2, dec_norm3], dec_wo.T
                ),
            ),
        ]
    )
    w_gate, held_gate = groups.gather_whole(
        wide(enc_wgate), wide(dec_wgate), 1, brought[0][0]
    )
    w_up, held_up = groups.gather_whole(wide(enc_wup), wide(dec_wup), 2, held_gate)
    w_down, held_down = groups.gather_whole(wide(enc_wdown.T), wide(dec_wdown.T), 1, held_up)
    w_cross, held_cross = groups.gather_whole(
        columns([cross_wk, cross_wv]), columns([cross_wq, cross_wo.T]), 1, held_down
    )
    w_qkv = first[:, : 3 * width]
    gains = first[:, 3 * width : 3 * width + 3].astype(F32).T
    gains = after(gains, held_gate)
    gain1, gain2, gain3 = gains[0:1], gains[1:2], gains[2:3]
    w_out = first[:, 3 * width + 64 : 4 * width + 64]
    w_cq, w_co = w_cross[:, :width], w_cross[:, width:]
    cot_own = dec_cot[0]
    dec_groups = range(3 * groups.quarter, groups.count)
    cot_all = gather_tokens(cot_own, None, dec_groups)
    enc_table, dec_table = after((enc_table, dec_table), brought[0])

    enc_ids = enc_seg[0, 0].astype(F32)
    ids_rel = jnp.concatenate(
        [
            lax.dynamic_slice_in_dim(enc_ids, (DecoderRows.flip(b) ^ tp) * enc_count, enc_count)
            for b in range(4)
        ]
    )
    dec_ids = dec_seg[0]
    enc_hot = one_hot_blocks(enc_relative(), True)
    dec_hot = one_hot_blocks(dec_relative(), False)
    enc_bias = dot(enc_table, jnp.asarray(enc_hot, BF16), TN).reshape(heads, 5, QB, QB)
    dec_bias = dot(dec_table, jnp.asarray(dec_hot, BF16), TN).reshape(heads, DEC_LEN, DEC_LEN)

    enc_cfg = dict(
        name="enc", heads=heads, bq=QB, bk=enc_len, steps=enc_len // QB, follow=False,
        bias="blocks", causal=False, k=width, v=2 * width,
    )
    dec_cfg = dict(
        name="dec", heads=heads, bq=DEC_LEN, bk=DEC_LEN, steps=3, follow=True,
        bias="full", causal=True, k=width, v=2 * width,
    )
    cross_cfg = dict(
        name="cross", heads=heads, bq=DEC_LEN, bk=enc_len, steps=1, follow=False,
        bias=None, causal=False, k=0, v=width,
    )
    enc_idk = jnp.broadcast_to(ids_rel[:, None], (enc_len, QB))
    enc_idq = ids_rel.reshape(enc_len // QB, 1, QB)
    dec_idk = jnp.broadcast_to(dec_ids.astype(F32).reshape(-1, 1), (3 * DEC_LEN, DEC_LEN))
    dec_idq = dec_ids.astype(F32).reshape(3, 1, DEC_LEN)
    cross_idk = jnp.broadcast_to(ids_rel[:, None], (enc_len, DEC_LEN))

    x_f32 = x_own.astype(F32)
    norm1_all = rms_scale(x_all.astype(F32), gain1).astype(BF16)
    qkv = dot(norm1_all, w_qkv, NN).astype(BF16)

    def enc_attend(qkv):
        return attention_forward(enc_cfg, tp_arg, qkv, qkv, enc_idk, enc_idq, enc_bias)

    def dec_attend(qkv):
        ordered = rows.to_rows(qkv, enc_count)
        out, lse = attention_forward(dec_cfg, tp_arg, ordered, ordered, dec_idk, dec_idq, dec_bias)
        return rows.to_relative(out, enc_count), jnp.pad(
            lse.reshape(-1), (0, heads * enc_len - lse.size)
        ).reshape(enc_len // QB, heads, QB)

    att, lse1 = lax.cond(is_enc, enc_attend, dec_attend, after(qkv, held_gate, cot_all))
    x1 = x_f32 + reduce_tokens(dot(after(att, held_up), w_out, NT).astype(BF16))

    norm2_all = gather_tokens(after(rms_scale(x1, gain2).astype(BF16), held_down))
    feed_weights = (w_gate, w_up, after(w_down, held_cross))
    wide_units = w_gate.shape[1]
    width_all = x_own.shape[1]
    feed_out2, gate2, up2 = feed_call(
        "feed_forward", feed_kernel, 256, (norm2_all,), feed_weights,
        ((width_all, BF16), (wide_units, F32), (wide_units, F32)),
    )
    queries = {}

    def while_feed(anchor):
        dec_q_rel = dot(after(norm2_all, anchor), w_cq, NN).astype(BF16)
        dec_q = rows.to_rows(dec_q_rel, enc_count).reshape(3, DEC_LEN, width)
        dec_q = jnp.concatenate([dec_q, dec_ids.astype(BF16)[:, :, None]], axis=2)
        queries["sent"] = sum(groups.send(dec_q[r], 3, r) for r in range(3))
        return queries["sent"]

    def while_reduce(anchor):
        queries["hidden"] = dot(after(cot_all, anchor), feed_weights[2], NN)
        return queries["hidden"]

    x2 = x1 + reduce_tokens(feed_out2, while_reduce)
    memory = gather_tokens(rms_scale(x2, gain3).astype(BF16), while_feed)
    cross_idq = queries["sent"][:, width].astype(F32).reshape(1, 1, DEC_LEN)
    cross_q = queries["sent"][:, :width]

    cross_kv = dot(memory, w_cross, NN).astype(BF16)
    cross_o, lse2 = attention_forward(cross_cfg, tp_arg, cross_q, cross_kv, cross_idk, cross_idq)
    dec_o = jnp.concatenate([groups.send(cross_o, r, 3) for r in range(3)], axis=0)
    dec_o_rel = rows.to_relative(dec_o, dec_count)

    x2d = x1[:dec_count] + reduce_tokens(dot(dec_o_rel, w_co, NT).astype(BF16))
    norm3_all = gather_tokens(rms_scale(x2d, gain3).astype(BF16))
    grad_outs = ((width_all, BF16), (2 * wide_units, BF16), (wide_units, BF16))
    partial_n3, both3, hidden3 = feed_call(
        "feed_both", feed_both_kernel, 288, (norm3_all, queries["hidden"]), feed_weights[:2],
        grad_outs,
    )
    grad_n3 = reduce_tokens(partial_n3)
    grad_step, gain_d3 = norm_backward(x2d, gain3, grad_n3)
    grad_x2d = cot_own.astype(F32) + grad_step
    grad2_all = gather_tokens(grad_x2d.astype(BF16))
    grad_o_rel = dot(grad2_all, w_co, NN).astype(BF16)
    grad_o_rows = rows.to_rows(grad_o_rel, dec_count).reshape(3, DEC_LEN, width)
    cross_go = sum(groups.send(grad_o_rows[r], 3, r) for r in range(3))
    cross_gq, cross_gkv = attention_backward(
        cross_cfg, tp_arg, cross_q, cross_kv, cross_idk, cross_idq, lse2, cross_go
    )
    dec_gq = jnp.concatenate([groups.send(cross_gq, r, 3) for r in range(3)], axis=0)
    dec_gq_rel = rows.to_relative(dec_gq, enc_count)
    placed = {}

    def while_memory(anchor):
        left, right = after((memory, norm2_all), anchor)
        (product,) = token_product(
            groups,
            (2 * width,),
            (0, left, cross_gkv),
            (1, right, dec_gq_rel),
            (1, grad2_all, dec_o_rel),
        )
        placed["cross"] = groups.to_place(product)
        return product

    grad_memory = reduce_tokens(dot(cross_gkv, w_cross, NT).astype(BF16), while_memory)
    grad_memory = grad_memory.astype(BF16).astype(F32)
    grad_e2, gain_ef = norm_backward(x2, gain3, grad_memory)


    grad_e2_all = gather_tokens(grad_e2.astype(BF16))
    partial_n2, both2, hidden2 = feed_call(
        "feed_back", feed_back_kernel, 256, (gate2, up2, grad_e2_all), feed_weights, grad_outs
    )

    def input_product(index, anchor):
        tokens, others = after((norm2_all, norm3_all), anchor)
        (product,) = token_product(
            groups, (wide_units,), (0, tokens, both2, index), (1, others, both3, index)
        )
        placed[index] = groups.to_place(product)
        return product

    product = input_product(0, partial_n2)
    sums = {"cross": groups.to_owner(after(placed["cross"], product))}
    dec_partial = dot(after(dec_gq_rel, product), w_cq, NT).astype(BF16)
    partial_n2 = jnp.where(is_enc, partial_n2, dec_partial)

    def while_n2(anchor):
        grads, others = after((grad_e2_all, cot_all), input_product(1, anchor))
        (product,) = token_product(
            groups, (wide_units,), (0, grads, hidden2), (1, others, hidden3)
        )
        placed[2] = groups.to_place(product)
        placed["last"] = product
        return product

    grad_n2 = reduce_tokens(partial_n2, while_n2)
    grad_step, gain_2 = norm_backward(x1, gain2, grad_n2)
    grad_x1 = jnp.where(is_enc, grad_e2, pad_rows(grad_x2d, enc_count)) + grad_step
    sums[0] = groups.to_owner(after(placed[0], sums["cross"], placed["last"]))

    grad_x1_all = gather_tokens(after(grad_x1.astype(BF16), placed[0]))
    grad_att = dot(grad_x1_all, w_out, NN).astype(BF16)
    grad_att, sums[0] = lax.optimization_barrier((grad_att, sums[0]))
    def enc_attend_back(qkv, lse, grad_att):
        gq, gkv, gb = attention_backward(
            enc_cfg, tp_arg, qkv, qkv, enc_idk, enc_idq, lse, grad_att, enc_bias
        )
        return columns([gq, gkv]), gb.reshape(heads, -1)

    def dec_attend_back(qkv, lse, grad_att):
        ordered = rows.to_rows(qkv, enc_count)
        lse = lse.reshape(-1)[: 3 * heads * DEC_LEN].reshape(3, heads, DEC_LEN)
        gq, gkv, gb = attention_backward(
            dec_cfg, tp_arg, ordered, ordered, dec_idk, dec_idq, lse,
            rows.to_rows(grad_att, enc_count), dec_bias,
        )
        gb = gb.reshape(heads, -1)
        return (
            rows.to_relative(columns([gq, gkv]), enc_count),
            jnp.pad(gb, ((0, 0), (0, enc_hot.shape[1] - gb.shape[1]))),
        )

    grad_qkv, grad_bias = lax.cond(is_enc, enc_attend_back, dec_attend_back, qkv, lse1, grad_att)
    (product,) = token_product(
        groups,
        (4 * width,),
        (0, norm1_all, grad_qkv),
        (0, grad_x1_all, att),
        (1, norm1_all, grad_qkv),
        (1, grad_x1_all, att),
    )
    placed["first"] = groups.to_place(product)
    sums[1] = groups.to_owner(after(placed[1], sums[0]))
    partial_n1 = dot(after(grad_qkv, product), w_qkv, NT).astype(BF16)
    partial_n1, sums[1] = lax.optimization_barrier((partial_n1, sums[1]))

    def while_n1(anchor):
        tables["grad"] = lax.cond(
            is_enc,
            lambda gb: bucket_sums(enc_hot, gb),
            lambda gb: bucket_sums(dec_hot, gb[:, : dec_hot.shape[1]]),
            after(grad_bias, anchor),
        )
        feed_out3 = dot(after(hidden3, tables["grad"]), feed_weights[2], NT).astype(BF16)
        queries["out"] = x2d + reduce_tokens(feed_out3, None, dec_groups)
        return feed_out3

    tables = {}
    sums[2] = groups.to_owner(after(placed[2], sums[1]))
    grad_n1 = reduce_tokens(partial_n1, while_n1)
    grad_step, gain_1 = norm_backward(x_f32, gain1, grad_n1)
    grad_x = grad_x1 + grad_step
    enc_first, dec_first = groups.to_owner(after(placed["first"], sums[2]))
    enc_cross, dec_cross = sums["cross"]
    (enc_gate, dec_gate), (enc_up, dec_up), (enc_down, dec_down) = sums[0], sums[1], sums[2]

    gain_rows = jnp.stack([gain_1, gain_2, jnp.where(is_enc, gain_ef, gain_d3)])
    gain_rows = gain_rows + core_swap(gain_rows)
    gain_rows = gain_rows + pair_swap(gain_rows)
    small = jnp.concatenate([gain_rows.reshape(-1), tables["grad"].reshape(-1)])
    length = small.shape[0]
    small = jnp.pad(small, (0, -length % 1024)).reshape(-1, 128)
    enc_small, dec_small = groups.all_role_sums(after(small, sums[2]))

    def unpack(total):
        flat = total.reshape(-1)
        gain = flat[: gain_rows.size].reshape(gain_rows.shape)
        share = gain.shape[1] // groups.count
        mine = lax.dynamic_slice_in_dim(gain, groups.where * share, share, axis=1)
        return mine, flat[gain_rows.size : length].reshape(BUCKETS, heads)

    enc_gains, enc_table_grad = unpack(enc_small)
    dec_gains, dec_table_grad = unpack(dec_small)

    def part(value, index):
        return value[:, index * width : (index + 1) * width]

    zero_bf = jnp.zeros((), BF16)
    return (
        jnp.where(is_enc, zero_bf, queries["out"].astype(BF16))[None],
        jnp.where(is_enc, grad_x.astype(BF16), zero_bf)[None],
        jnp.where(is_enc, zero_bf, grad_x[:dec_count].astype(BF16))[None],
        enc_gains[0],
        part(enc_first, 0),
        part(enc_first, 1),
        part(enc_first, 2),
        part(enc_first, 3).T,
        enc_table_grad,
        enc_gains[1],
        enc_gate[:, :units],
        enc_up[:, :units],
        enc_down[:, :units].T,
        enc_gains[2],
        dec_gains[0],
        part(dec_first, 0),
        part(dec_first, 1),
        part(dec_first, 2),
        part(dec_first, 3).T,
        dec_table_grad,
        dec_gains[1],
        part(dec_cross, 0),
        part(enc_cross, 0),
        part(enc_cross, 1),
        part(dec_cross, 1).T,
        dec_gains[2],
        dec_gate[:, :units],
        dec_up[:, :units],
        dec_down[:, :units].T,
    )


def solution(mesh):
    vector, matrix, turned = P("grp"), P("grp", "tp"), P("tp", "grp")
    tokens, ids, table = P("grp", "tp", None), P("grp", None, None), P(None, "tp")
    enc = (vector, matrix, matrix, matrix, turned, table, vector, matrix, matrix, turned, vector)
    dec = (vector, matrix, matrix, matrix, turned, table, vector, matrix, matrix, matrix, turned)
    dec = dec + (vector, matrix, matrix, turned)
    return jax.shard_map(
        body,
        mesh=mesh,
        in_specs=(tokens, tokens, tokens, ids, ids) + enc + dec,
        out_specs=(tokens, tokens, tokens) + enc + dec,
        check_vma=False,
    )
```

```python
import math
from functools import partial

import jax
import jax.numpy as jnp
import numpy as np
from jax import lax
from jax.experimental import pallas as pl
from jax.experimental.pallas import tpu as pltpu
from jax.sharding import PartitionSpec as P

HEAD_DIM = 64
BUCKETS = 32
MAX_DIST = 128
DEC_LEN = 192
EPSILON = 1e-06
NEG_FILL = -1e30
QB = 128
F32 = jnp.float32
BF16 = jnp.bfloat16


def bucket_of(relative, two_sided):
    bucket_count = BUCKETS
    shifted = relative * 0
    if two_sided:
        bucket_count = bucket_count // 2
        shifted = shifted + (relative > 0) * bucket_count
        distance = np.abs(relative)
    else:
        distance = np.maximum(-relative, 0)
    exact_span = bucket_count // 2
    log_ratio = np.log(np.maximum(distance, 1) / exact_span) / np.log(MAX_DIST / exact_span)
    farther = np.minimum(
        exact_span + np.floor(log_ratio * (bucket_count - exact_span) + 1e-09).astype(np.int32),
        bucket_count - 1,
    )
    return (shifted + np.where(distance < exact_span, distance, farther)).astype(np.int32)


def one_hot_blocks(relative, two_sided):
    return np.eye(BUCKETS, dtype=np.float32)[:, bucket_of(relative, two_sided).reshape(-1)]


def enc_relative():
    return np.arange(-2 * QB, 3 * QB)[:, None] - np.arange(QB)[None, :]


def dec_relative():
    return np.arange(DEC_LEN)[:, None] - np.arange(DEC_LEN)[None, :]


def after(value, *others):
    return lax.optimization_barrier((value,) + others)[0]


def dot(left, right, dims):
    return lax.dot_general(left, right, (dims, ((), ())), preferred_element_type=F32)


NN = ((1,), (0,))
NT = ((1,), (1,))
TN = ((0,), (0,))


def block_of(place, tp):
    wide = place // 2
    swapped = (wide % 2) * 2 + wide // 2
    return (swapped ^ tp) * 2 + place % 2


def scores_t(head, cfg, keys, queries, bias_ref, same, place, tp):
    lanes = slice(head * HEAD_DIM, (head + 1) * HEAD_DIM)
    scores = dot(keys[:, lanes], queries[:, lanes], NT)
    if cfg["bias"] == "blocks":
        mine = block_of(place, tp)
        parts = []
        for kb in range(keys.shape[0] // QB):
            step = jnp.clip(block_of(kb, tp) - mine, -2, 2) + 2
            parts.append(bias_ref[head, step])
        scores = scores + jnp.concatenate(parts, axis=0)
    elif cfg["bias"] == "full":
        scores = scores + bias_ref[head]
    return jnp.where(same, scores, NEG_FILL)


def allowed_t(cfg, idk_ref, idq_ref):
    same = idk_ref[...] == idq_ref[0]
    if cfg["causal"]:
        key_pos = lax.broadcasted_iota(jnp.int32, same.shape, 0)
        query_pos = lax.broadcasted_iota(jnp.int32, same.shape, 1)
        same = same & (key_pos <= query_pos)
    return same


def forward_kernel(cfg, tp_ref, q_ref, kv_ref, idk_ref, idq_ref, *rest):
    if cfg["bias"]:
        bias_ref, out_ref, lse_ref, vt_ref = rest
    else:
        bias_ref, (out_ref, lse_ref, vt_ref) = None, rest
    heads = cfg["heads"]
    width = heads * HEAD_DIM
    place = pl.program_id(0)
    keys = kv_ref[:, cfg["k"] : cfg["k"] + width]

    def fill():
        vt_ref[...] = kv_ref[:, cfg["v"] : cfg["v"] + width].T

    if cfg["follow"]:
        fill()
    else:
        pl.when(place == 0)(fill)
    queries = q_ref[:, :width]
    same = allowed_t(cfg, idk_ref, idq_ref)
    outs = []
    for head in range(heads):
        scores = scores_t(head, cfg, keys, queries, bias_ref, same, place, tp_ref[0])
        peak = jnp.max(scores, axis=0, keepdims=True)
        exponent = jnp.exp(scores - peak)
        total = jnp.sum(exponent, axis=0, keepdims=True)
        weights = (exponent * (1.0 / total)).astype(BF16)
        outs.append(dot(vt_ref[head * HEAD_DIM : (head + 1) * HEAD_DIM, :], weights, NN))
        lse_ref[0, head : head + 1, :] = peak + jnp.log(total)
    out_ref[...] = jnp.concatenate(outs, axis=0).T.astype(BF16)


def backward_kernel(cfg, tp_ref, q_ref, kv_ref, idk_ref, idq_ref, *rest):
    if cfg["bias"]:
        bias_ref, lse_ref, go_ref, gq_ref, gkv_ref, gb_ref, kt_ref, acc_ref = rest
    else:
        bias_ref, gb_ref = None, None
        lse_ref, go_ref, gq_ref, gkv_ref, kt_ref, acc_ref = rest
    heads = cfg["heads"]
    width = heads * HEAD_DIM
    place = pl.program_id(0)
    keys = kv_ref[:, cfg["k"] : cfg["k"] + width]
    values = kv_ref[:, cfg["v"] : cfg["v"] + width]

    def clear():
        kt_ref[...] = kv_ref[:, cfg["k"] : cfg["k"] + width].T
        acc_ref[...] = jnp.zeros_like(acc_ref)

    def clear_bias():
        if gb_ref is not None:
            gb_ref[...] = jnp.zeros_like(gb_ref)

    pl.when(place == 0)(clear_bias)
    if cfg["follow"]:
        clear()
    else:
        pl.when(place == 0)(clear)
    queries = q_ref[:, :width]
    grad_out = go_ref[...]
    same = allowed_t(cfg, idk_ref, idq_ref)
    grads = []
    for head in range(heads):
        lanes = slice(head * HEAD_DIM, (head + 1) * HEAD_DIM)
        scores = scores_t(head, cfg, keys, queries, bias_ref, same, place, tp_ref[0])
        weights = jnp.exp(scores - lse_ref[0, head : head + 1, :])
        grad_weights = dot(values[:, lanes], grad_out[:, lanes], NT)
        delta = jnp.sum(grad_weights * weights, axis=0, keepdims=True)
        grad_scores = weights * (grad_weights - delta)
        if cfg["bias"] == "blocks":
            mine = block_of(place, tp_ref[0])
            for kb in range(keys.shape[0] // QB):
                step = jnp.clip(block_of(kb, tp_ref[0]) - mine, -2, 2) + 2
                gb_ref[head, step] += grad_scores[kb * QB : (kb + 1) * QB]
        elif cfg["bias"] == "full":
            gb_ref[head] += grad_scores
        scores_bf = grad_scores.astype(BF16)
        acc_ref[head] += dot(scores_bf, queries[:, lanes], NN)
        acc_ref[heads + head] += dot(weights.astype(BF16), grad_out[:, lanes], NN)
        grads.append(dot(kt_ref[lanes, :], scores_bf, NN))
    gq_ref[...] = jnp.concatenate(grads, axis=0).T.astype(BF16)

    def finish():
        gkv_ref[...] = jnp.concatenate(
            [acc_ref[k].astype(BF16) for k in range(2 * heads)], axis=1
        )

    if cfg["follow"]:
        finish()
    else:
        pl.when(place == pl.num_programs(0) - 1)(finish)


def attention_specs(cfg, q_cols, kv_cols, bias):
    bq, bk = cfg["bq"], cfg["bk"]
    follow = cfg["follow"]
    specs = [
        pl.BlockSpec((bq, q_cols), lambda i, s: (i, 0)),
        pl.BlockSpec((bk, kv_cols), (lambda i, s: (i, 0)) if follow else (lambda i, s: (0, 0))),
        pl.BlockSpec((bk, bq), (lambda i, s: (i, 0)) if follow else (lambda i, s: (0, 0))),
        pl.BlockSpec((1, 1, bq), lambda i, s: (i, 0, 0)),
    ]
    if bias is not None:
        rank = bias.ndim
        specs.append(pl.BlockSpec(bias.shape, lambda i, s: (0,) * rank))
    return specs


def attention_forward(cfg, tp, q, kv, idk, idq, bias=None):
    heads, bq, bk, steps = cfg["heads"], cfg["bq"], cfg["bk"], cfg["steps"]
    width = heads * HEAD_DIM
    extra = () if bias is None else (bias,)
    return pl.pallas_call(
        partial(forward_kernel, cfg),
        out_shape=(
            jax.ShapeDtypeStruct((steps * bq, width), BF16),
            jax.ShapeDtypeStruct((steps, heads, bq), F32),
        ),
        grid_spec=pltpu.PrefetchScalarGridSpec(
            num_scalar_prefetch=1,
            grid=(steps,),
            in_specs=attention_specs(cfg, q.shape[1], kv.shape[1], bias),
            out_specs=(
                pl.BlockSpec((bq, width), lambda i, s: (i, 0)),
                pl.BlockSpec((1, heads, bq), lambda i, s: (i, 0, 0)),
            ),
            scratch_shapes=[pltpu.VMEM((width, bk), BF16)],
        ),
        compiler_params=pltpu.CompilerParams(vmem_limit_bytes=40 << 20),
        name=cfg["name"] + "_forward",
    )(tp, q, kv, idk, idq, *extra)


def attention_backward(cfg, tp, q, kv, idk, idq, lse, grad_out, bias=None):
    heads, bq, bk, steps = cfg["heads"], cfg["bq"], cfg["bk"], cfg["steps"]
    width = heads * HEAD_DIM
    follow = cfg["follow"]
    extra = () if bias is None else (bias,)
    out_shape = [
        jax.ShapeDtypeStruct((steps * bq, width), BF16),
        jax.ShapeDtypeStruct((steps * bk if follow else bk, 2 * width), BF16),
    ]
    out_specs = [
        pl.BlockSpec((bq, width), lambda i, s: (i, 0)),
        pl.BlockSpec((bk, 2 * width), (lambda i, s: (i, 0)) if follow else (lambda i, s: (0, 0))),
    ]
    if bias is not None:
        rank = bias.ndim
        out_shape.append(jax.ShapeDtypeStruct(bias.shape, F32))
        out_specs.append(pl.BlockSpec(bias.shape, lambda i, s: (0,) * rank))
    return pl.pallas_call(
        partial(backward_kernel, cfg),
        out_shape=tuple(out_shape),
        grid_spec=pltpu.PrefetchScalarGridSpec(
            num_scalar_prefetch=1,
            grid=(steps,),
            in_specs=attention_specs(cfg, q.shape[1], kv.shape[1], bias)
            + [
                pl.BlockSpec((1, heads, bq), lambda i, s: (i, 0, 0)),
                pl.BlockSpec((bq, width), lambda i, s: (i, 0)),
            ],
            out_specs=tuple(out_specs),
            scratch_shapes=[pltpu.VMEM((width, bk), BF16), pltpu.VMEM((2 * heads, bk, HEAD_DIM), F32)],
        ),
        compiler_params=pltpu.CompilerParams(vmem_limit_bytes=48 << 20),
        name=cfg["name"] + "_backward",
    )(tp, q, kv, idk, idq, *extra, lse, grad_out)


def product_kernel(quarter, share, step, jobs, widths, role_ref, *refs):
    operands, out_refs = refs[: 2 * len(jobs)], refs[2 * len(jobs) :]
    starts = [sum(widths[:k]) for k in range(len(widths))]
    for index, (on_role, column) in enumerate(jobs):
        left_ref, right_ref = operands[2 * index], operands[2 * index + 1]

        @pl.when(role_ref[0] == on_role)
        def _():
            result = dot(left_ref[...], right_ref[...], TN).astype(BF16)
            rows_here, cols_here = result.shape
            first = pl.program_id(0) * (rows_here // step)
            for unit in range(rows_here // step):
                row = (first + unit) * step
                owner, offset = row // share, pl.multiple_of(row % share, step)
                for out_ref, start, cols in zip(out_refs, starts, widths):
                    low, high = max(start, column), min(start + cols, column + cols_here)
                    if low < high:
                        out_ref[
                            owner % quarter,
                            owner // quarter,
                            pl.ds(offset, step),
                            low - start : high - start,
                        ] = result[unit * step : (unit + 1) * step, low - column : high - column]


def token_product(groups, widths, *jobs):
    rows_count = jobs[0][1].shape[1]
    tile = 256
    share = rows_count // groups.count
    step = math.gcd(share, 64)
    offsets, described, operands, specs = {}, [], [], []
    for role, left, right, *block in jobs:
        count, cols = right.shape
        cols = sum(widths) if block else cols
        described.append((role, offsets.get(role, 0)))
        offsets[role] = offsets.get(role, 0) + cols

        def left_map(i, s, role=role):
            return (0, jnp.where(s[0] == role, i, 0))

        operands += [left, right]
        specs += [
            pl.BlockSpec((count, tile), left_map),
            pl.BlockSpec(
                (count, cols),
                lambda i, s, block=(block or [0])[0]: (0, block),
                pipeline_mode=pl.Buffered(1),
            ),
        ]
    shapes = [(groups.quarter, 4, share, cols) for cols in widths]
    role = jnp.where(groups.is_enc, 0, 1).astype(jnp.int32)[None]
    return pl.pallas_call(
        partial(product_kernel, groups.quarter, share, step, described, widths),
        out_shape=tuple(jax.ShapeDtypeStruct(dims, BF16) for dims in shapes),
        grid_spec=pltpu.PrefetchScalarGridSpec(
            num_scalar_prefetch=1,
            grid=(rows_count // tile,),
            in_specs=specs,
            out_specs=tuple(pl.BlockSpec(dims, lambda i, s: (0, 0, 0, 0)) for dims in shapes),
        ),
        compiler_params=pltpu.CompilerParams(vmem_limit_bytes=56 << 20),
        name="token_product",
    )(role, *operands)


def bucket_sums(hot, values):
    high = values.astype(BF16)
    low = (values - high.astype(F32)).astype(BF16)
    sums = dot(jnp.asarray(hot, BF16), jnp.concatenate([high, low], axis=0), NT)
    return sums[:, : values.shape[0]] + sums[:, values.shape[0] :]


def rms_scale(hidden, gain_vec):
    return (
        hidden * lax.rsqrt(jnp.mean(hidden * hidden, axis=-1, keepdims=True) + EPSILON) * gain_vec
    )


def norm_backward(hidden, gain_vec, grad_out):
    rate = lax.rsqrt(jnp.mean(hidden * hidden, axis=-1, keepdims=True) + EPSILON)
    scaled = gain_vec * grad_out
    inner = jnp.mean(hidden * scaled, axis=-1, keepdims=True)
    grad_in = rate * scaled - hidden * (rate * rate * rate * inner)
    return grad_in, jnp.sum(grad_out * hidden * rate, axis=0)


GELU_SCALE = float(np.sqrt(2.0 / np.pi))
GELU_CUBIC = 0.044715


def gelu_parts(value):
    square = value * value
    tanh = jnp.tanh(GELU_SCALE * (value + GELU_CUBIC * (value * square)))
    half = 0.5 * (1.0 + tanh)
    slope = half + 0.5 * value * (1.0 - tanh * tanh) * (
        GELU_SCALE * (1.0 + 3.0 * GELU_CUBIC * square)
    )
    return value * half, slope


def gelu(value):
    cubic = value + GELU_CUBIC * (value * value * value)
    return value * (0.5 * (1.0 + jnp.tanh(GELU_SCALE * cubic)))


def feed_kernel(tok_ref, wg_ref, wu_ref, wd_ref, out_ref, gate_ref, up_ref):
    tokens = tok_ref[...]
    gate = dot(tokens, wg_ref[...], NN)
    up = dot(tokens, wu_ref[...], NN)
    gate_ref[...] = gate
    up_ref[...] = up
    hidden = (gelu(gate) * up).astype(BF16)
    out_ref[...] = dot(hidden, wd_ref[...], NT).astype(BF16)


def feed_grads(gate, up, grad_hidden, wg_ref, wu_ref, gn_ref, both_ref, hid_ref):
    units = gate.shape[1]
    activated, slope = gelu_parts(gate)
    hid_ref[...] = (activated * up).astype(BF16)
    grad_gate = (grad_hidden * up * slope).astype(BF16)
    grad_up = (grad_hidden * activated).astype(BF16)
    both_ref[:, :units] = grad_gate
    both_ref[:, units:] = grad_up
    gn_ref[...] = (dot(grad_gate, wg_ref[...], NT) + dot(grad_up, wu_ref[...], NT)).astype(BF16)


def feed_back_kernel(gate_ref, up_ref, ga_ref, wg_ref, wu_ref, wd_ref, *outs):
    grad_hidden = dot(ga_ref[...], wd_ref[...], NN)
    feed_grads(gate_ref[...], up_ref[...], grad_hidden, wg_ref, wu_ref, *outs)


def feed_both_kernel(tok_ref, gh_ref, wg_ref, wu_ref, *outs):
    tokens = tok_ref[...]
    gate = dot(tokens, wg_ref[...], NN)
    up = dot(tokens, wu_ref[...], NN)
    feed_grads(gate, up, gh_ref[...], wg_ref, wu_ref, *outs)


def feed_call(name, kernel, tile, streamed, weights, outs):
    count = streamed[0].shape[0]
    return pl.pallas_call(
        kernel,
        out_shape=tuple(jax.ShapeDtypeStruct((count, cols), kind) for cols, kind in outs),
        grid=(count // tile,),
        in_specs=[pl.BlockSpec((tile, a.shape[1]), lambda i: (i, 0)) for a in streamed]
        + [
            pl.BlockSpec(w.shape, lambda i: (0, 0), pipeline_mode=pl.Buffered(1)) for w in weights
        ],
        out_specs=tuple(pl.BlockSpec((tile, cols), lambda i: (i, 0)) for cols, _ in outs),
        compiler_params=pltpu.CompilerParams(vmem_limit_bytes=50 << 20),
        name=name,
    )(*streamed, *weights)


SWAP_CORE = [(0, 1), (1, 0), (2, 3), (3, 2)]
SWAP_PAIR = [(0, 2), (2, 0), (1, 3), (3, 1)]


def tp_swap(value, pairs, groups=None):
    if groups is None:
        return lax.ppermute(value, "tp", pairs)
    size = lax.axis_size("tp")
    flat = [(g * size + source, g * size + target) for g in groups for source, target in pairs]
    return lax.ppermute(value, ("grp", "tp"), flat)


def core_swap(value, groups=None):
    return tp_swap(value, SWAP_CORE, groups)


def pair_swap(value, groups=None):
    return tp_swap(value, SWAP_PAIR, groups)


def gather_tokens(own, meanwhile=None, groups=None):
    far = pair_swap(own, groups)
    if meanwhile is not None:
        far = after(far, meanwhile(own))
    return jnp.concatenate([own, far, core_swap(own, groups), core_swap(far, groups)], axis=0)


def reduce_tokens(partial_bf, meanwhile=None, groups=None):
    count = partial_bf.shape[0] // 4
    other = core_swap(partial_bf[2 * count :], groups)
    away = (partial_bf[count : 2 * count].astype(F32) + other[count:].astype(F32)).astype(BF16)
    far = pair_swap(away, groups)
    if meanwhile is not None:
        far = after(far, meanwhile(away))
    return partial_bf[:count].astype(F32) + other[:count].astype(F32) + far.astype(F32)


class Groups:
    def __init__(self):
        self.count = lax.axis_size("grp")
        self.quarter = self.count // 4
        where = lax.axis_index("grp")
        self.where = where
        self.role = where // self.quarter
        self.place = where % self.quarter
        self.is_enc = self.role < 3
        self.peers = [
            [a * self.quarter + j for j in range(self.quarter)] for a in range(4)
        ]
        self.swap = [(i, i ^ 1) for i in range(self.count)]
        self.swapped = None
        self.roles = [
            [a * self.quarter + j for a in range(4)] for j in range(self.quarter)
        ]

    def shift(self, value, steps):
        hop = steps * self.quarter
        return lax.ppermute(
            value, "grp", [(i, (i + hop) % self.count) for i in range(self.count)]
        )

    def send(self, value, source, target):
        q = self.quarter
        return lax.ppermute(
            value, "grp", [(source * q + j, target * q + j) for j in range(q)]
        )

    def gather(self, chunks):
        fulls, last, brought = [], {}, []
        for enc, dec in chunks:
            rows, cols = enc.shape
            shards = [jnp.where(self.is_enc, enc, dec)]
            for step in (1, 2, 3):
                payload = jnp.where((self.role + step) % 4 < 3, enc, dec)
                if step in last:
                    payload = after(payload, last[step])
                last[step] = self.shift(payload, step)
                shards.append(last[step])
            brought.append(tuple(shards[1:]))
            full = jnp.zeros((4, self.quarter, rows, cols), enc.dtype)
            for step, shard in enumerate(shards):
                source = (self.role - step) % 4
                if self.quarter == 2:
                    other = lax.ppermute(shard, "grp", self.swap)
                    full = lax.dynamic_update_slice(
                        full, shard[None, None], (source, self.place, 0, 0)
                    )
                    full = lax.dynamic_update_slice(
                        full, other[None, None], (source, 1 - self.place, 0, 0)
                    )
                else:
                    group = lax.all_gather(shard, "grp", axis_index_groups=self.peers)
                    full = lax.dynamic_update_slice(full, group[None], (source, 0, 0, 0))
            fulls.append(full.reshape(-1, cols))
        return fulls, brought

    def gather_whole(self, enc, dec, pieces, *anchors):
        rows, cols = enc.shape
        payload = jnp.stack([enc, enc, enc, dec])
        held = self.to_quarters(after(payload, *anchors) if anchors else payload)
        if self.quarter == 2:
            full = jnp.zeros((4, 2, rows, cols), enc.dtype)
            full = lax.dynamic_update_slice(full, held[:, None], (0, self.place, 0, 0))
            for low in range(0, 4, 4 // pieces):
                piece = held[low : low + 4 // pieces]
                if self.swapped is not None:
                    piece = after(piece, self.swapped)
                self.swapped = lax.ppermute(piece, "grp", self.swap)
                full = lax.dynamic_update_slice(
                    full, self.swapped[:, None], (low, 1 - self.place, 0, 0)
                )
        else:
            full = lax.all_gather(held, "grp", axis=1, axis_index_groups=self.peers)
        return full.reshape(-1, cols), held

    def to_quarters(self, blocks):
        return lax.all_to_all(
            blocks, "grp", 0, 0, tiled=True, axis_index_groups=self.roles
        )

    def peer_sum(self, value):
        if self.quarter == 2:
            return value + lax.ppermute(value, "grp", self.swap)
        return lax.psum(value, "grp", axis_index_groups=self.peers)

    def role_sums(self, mine):
        enc_total, dec_total = 0.0, 0.0
        for step in range(4):
            target = (self.role + step) % 4
            block = lax.dynamic_index_in_dim(mine, target, 0, keepdims=False)
            if step:
                block = self.shift(block, step)
            block = block.astype(F32)
            source_enc = (self.role - step) % 4 < 3
            enc_total = enc_total + jnp.where(source_enc, block, 0.0)
            dec_total = dec_total + jnp.where(source_enc, 0.0, block)
        return enc_total, dec_total

    def to_place(self, product):
        return lax.psum_scatter(
            product, "grp", scatter_dimension=0, axis_index_groups=self.peers
        )

    def to_owner(self, mine):
        parts = self.to_quarters(mine).astype(F32)
        return parts[0] + parts[1] + parts[2], parts[3]

    def all_role_sums(self, value):
        value = self.peer_sum(value)
        return self.role_sums(jnp.broadcast_to(value[None], (4,) + value.shape))


def pad_rows(value, count):
    return jnp.pad(value, ((0, count - value.shape[0]), (0, 0)))


class DecoderRows:
    def __init__(self, tp, count, stride):
        self.count, self.stride, self.tp = count, stride, tp

    @staticmethod
    def flip(index):
        return (index % 2) * 2 + index // 2

    def to_rows(self, value, stride):
        return jnp.concatenate(
            [
                lax.dynamic_slice_in_dim(
                    value, self.flip(i ^ self.tp) * stride, self.count, axis=0
                )
                for i in range(4)
            ],
            axis=0,
        )

    def to_relative(self, value, stride):
        return jnp.concatenate(
            [
                pad_rows(
                    lax.dynamic_slice_in_dim(
                        value, (self.flip(b) ^ self.tp) * self.count, self.count, axis=0
                    ),
                    stride,
                )
                for b in range(4)
            ],
            axis=0,
        )


def body(
    enc_in,
    dec_in,
    dec_cot,
    enc_seg,
    dec_seg,
    enc_norm1,
    enc_wq,
    enc_wk,
    enc_wv,
    enc_wo,
    enc_table,
    enc_norm2,
    enc_wgate,
    enc_wup,
    enc_wdown,
    enc_normf,
    dec_norm1,
    dec_wq,
    dec_wk,
    dec_wv,
    dec_wo,
    dec_table,
    dec_norm2,
    cross_wq,
    cross_wk,
    cross_wv,
    cross_wo,
    dec_norm3,
    dec_wgate,
    dec_wup,
    dec_wdown,
):
    groups = Groups()
    is_enc = groups.is_enc
    tp = lax.axis_index("tp")
    tp_arg = tp.astype(jnp.int32)[None]
    heads = enc_table.shape[1]
    width = heads * HEAD_DIM
    enc_count = enc_in.shape[1]
    dec_count = dec_in.shape[1]
    enc_len = enc_seg.shape[-1]
    rows = DecoderRows(tp, dec_count, enc_count)

    def columns(parts):
        return jnp.concatenate(parts, axis=1)

    x_own = jnp.where(is_enc, enc_in[0], pad_rows(dec_in[0], enc_count))
    x_all = gather_tokens(x_own)
    units = enc_wgate.shape[1]
    padded = -units % 128

    def first_chunk(weights, gains, w_out):
        gains = jnp.pad(jnp.stack(gains, axis=1), ((0, 0), (0, -len(gains) % 64)))
        parts = columns(list(weights) + [gains, w_out])
        return jnp.pad(parts, ((0, 0), (0, -parts.shape[1] % 128)))

    def wide(weight):
        return jnp.pad(weight, ((0, 0), (0, padded)))

    (first,), brought = groups.gather(
        [
            (
                first_chunk(
                    [enc_wq, enc_wk, enc_wv], [enc_norm1, enc_norm2, enc_normf], enc_wo.T
                ),
                first_chunk(
                    [dec_wq, dec_wk, dec_wv], [dec_norm1, dec_norm2, dec_norm3], dec_wo.T
                ),
            ),
        ]
    )
    w_gate, held_gate = groups.gather_whole(
        wide(enc_wgate), wide(dec_wgate), 1, brought[0][0]
    )
    w_up, held_up = groups.gather_whole(wide(enc_wup), wide(dec_wup), 2, held_gate)
    w_down, held_down = groups.gather_whole(wide(enc_wdown.T), wide(dec_wdown.T), 1, held_up)
    w_cross, held_cross = groups.gather_whole(
        columns([cross_wk, cross_wv]), columns([cross_wq, cross_wo.T]), 1, held_down
    )
    w_qkv = first[:, : 3 * width]
    gains = first[:, 3 * width : 3 * width + 3].astype(F32).T
    gains = after(gains, held_gate)
    gain1, gain2, gain3 = gains[0:1], gains[1:2], gains[2:3]
    w_out = first[:, 3 * width + 64 : 4 * width + 64]
    w_cq, w_co = w_cross[:, :width], w_cross[:, width:]
    cot_own = dec_cot[0]
    dec_groups = range(3 * groups.quarter, groups.count)
    cot_all = gather_tokens(cot_own, None, dec_groups)
    enc_table, dec_table = after((enc_table, dec_table), brought[0])

    enc_ids = enc_seg[0, 0].astype(F32)
    ids_rel = jnp.concatenate(
        [
            lax.dynamic_slice_in_dim(enc_ids, (DecoderRows.flip(b) ^ tp) * enc_count, enc_count)
            for b in range(4)
        ]
    )
    dec_ids = dec_seg[0]
    enc_hot = one_hot_blocks(enc_relative(), True)
    dec_hot = one_hot_blocks(dec_relative(), False)
    enc_bias = dot(enc_table, jnp.asarray(enc_hot, BF16), TN).reshape(heads, 5, QB, QB)
    dec_bias = dot(dec_table, jnp.asarray(dec_hot, BF16), TN).reshape(heads, DEC_LEN, DEC_LEN)

    enc_cfg = dict(
        name="enc", heads=heads, bq=QB, bk=enc_len, steps=enc_len // QB, follow=False,
        bias="blocks", causal=False, k=width, v=2 * width,
    )
    dec_cfg = dict(
        name="dec", heads=heads, bq=DEC_LEN, bk=DEC_LEN, steps=3, follow=True,
        bias="full", causal=True, k=width, v=2 * width,
    )
    cross_cfg = dict(
        name="cross", heads=heads, bq=DEC_LEN, bk=enc_len, steps=1, follow=False,
        bias=None, causal=False, k=0, v=width,
    )
    enc_idk = jnp.broadcast_to(ids_rel[:, None], (enc_len, QB))
    enc_idq = ids_rel.reshape(enc_len // QB, 1, QB)
    dec_idk = jnp.broadcast_to(dec_ids.astype(F32).reshape(-1, 1), (3 * DEC_LEN, DEC_LEN))
    dec_idq = dec_ids.astype(F32).reshape(3, 1, DEC_LEN)
    cross_idk = jnp.broadcast_to(ids_rel[:, None], (enc_len, DEC_LEN))

    x_f32 = x_own.astype(F32)
    norm1_all = rms_scale(x_all.astype(F32), gain1).astype(BF16)
    qkv = dot(norm1_all, w_qkv, NN).astype(BF16)

    def enc_attend(qkv):
        return attention_forward(enc_cfg, tp_arg, qkv, qkv, enc_idk, enc_idq, enc_bias)

    def dec_attend(qkv):
        ordered = rows.to_rows(qkv, enc_count)
        out, lse = attention_forward(dec_cfg, tp_arg, ordered, ordered, dec_idk, dec_idq, dec_bias)
        return rows.to_relative(out, enc_count), jnp.pad(
            lse.reshape(-1), (0, heads * enc_len - lse.size)
        ).reshape(enc_len // QB, heads, QB)

    att, lse1 = lax.cond(is_enc, enc_attend, dec_attend, after(qkv, held_gate, cot_all))
    x1 = x_f32 + reduce_tokens(dot(after(att, held_up), w_out, NT).astype(BF16))

    norm2_all = gather_tokens(after(rms_scale(x1, gain2).astype(BF16), held_down))
    feed_weights = (w_gate, w_up, after(w_down, held_cross))
    wide_units = w_gate.shape[1]
    width_all = x_own.shape[1]
    feed_out2, gate2, up2 = feed_call(
        "feed_forward", feed_kernel, 256, (norm2_all,), feed_weights,
        ((width_all, BF16), (wide_units, F32), (wide_units, F32)),
    )
    queries = {}

    def while_feed(anchor):
        dec_q_rel = dot(after(norm2_all, anchor), w_cq, NN).astype(BF16)
        dec_q = rows.to_rows(dec_q_rel, enc_count).reshape(3, DEC_LEN, width)
        dec_q = jnp.concatenate([dec_q, dec_ids.astype(BF16)[:, :, None]], axis=2)
        queries["sent"] = sum(groups.send(dec_q[r], 3, r) for r in range(3))
        return queries["sent"]

    def while_reduce(anchor):
        queries["hidden"] = dot(after(cot_all, anchor), feed_weights[2], NN)
        return queries["hidden"]

    x2 = x1 + reduce_tokens(feed_out2, while_reduce)
    memory = gather_tokens(rms_scale(x2, gain3).astype(BF16), while_feed)
    cross_idq = queries["sent"][:, width].astype(F32).reshape(1, 1, DEC_LEN)
    cross_q = queries["sent"][:, :width]

    cross_kv = dot(memory, w_cross, NN).astype(BF16)
    cross_o, lse2 = attention_forward(cross_cfg, tp_arg, cross_q, cross_kv, cross_idk, cross_idq)
    dec_o = jnp.concatenate([groups.send(cross_o, r, 3) for r in range(3)], axis=0)
    dec_o_rel = rows.to_relative(dec_o, dec_count)

    x2d = x1[:dec_count] + reduce_tokens(dot(dec_o_rel, w_co, NT).astype(BF16))
    norm3_all = gather_tokens(rms_scale(x2d, gain3).astype(BF16))
    grad_outs = ((width_all, BF16), (2 * wide_units, BF16), (wide_units, BF16))
    partial_n3, both3, hidden3 = feed_call(
        "feed_both", feed_both_kernel, 288, (norm3_all, queries["hidden"]), feed_weights[:2],
        grad_outs,
    )
    grad_n3 = reduce_tokens(partial_n3)
    grad_step, gain_d3 = norm_backward(x2d, gain3, grad_n3)
    grad_x2d = cot_own.astype(F32) + grad_step
    grad2_all = gather_tokens(grad_x2d.astype(BF16))
    grad_o_rel = dot(grad2_all, w_co, NN).astype(BF16)
    grad_o_rows = rows.to_rows(grad_o_rel, dec_count).reshape(3, DEC_LEN, width)
    cross_go = sum(groups.send(grad_o_rows[r], 3, r) for r in range(3))
    cross_gq, cross_gkv = attention_backward(
        cross_cfg, tp_arg, cross_q, cross_kv, cross_idk, cross_idq, lse2, cross_go
    )
    dec_gq = jnp.concatenate([groups.send(cross_gq, r, 3) for r in range(3)], axis=0)
    dec_gq_rel = rows.to_relative(dec_gq, enc_count)
    placed = {}

    def while_memory(anchor):
        left, right = after((memory, norm2_all), anchor)
        (product,) = token_product(
            groups,
            (2 * width,),
            (0, left, cross_gkv),
            (1, right, dec_gq_rel),
            (1, grad2_all, dec_o_rel),
        )
        placed["cross"] = groups.to_place(product)
        return product

    grad_memory = reduce_tokens(dot(cross_gkv, w_cross, NT).astype(BF16), while_memory)
    grad_memory = grad_memory.astype(BF16).astype(F32)
    grad_e2, gain_ef = norm_backward(x2, gain3, grad_memory)


    grad_e2_all = gather_tokens(grad_e2.astype(BF16))
    partial_n2, both2, hidden2 = feed_call(
        "feed_back", feed_back_kernel, 256, (gate2, up2, grad_e2_all), feed_weights, grad_outs
    )

    def input_product(index, anchor):
        tokens, others = after((norm2_all, norm3_all), anchor)
        (product,) = token_product(
            groups, (wide_units,), (0, tokens, both2, index), (1, others, both3, index)
        )
        placed[index] = groups.to_place(product)
        return product

    product = input_product(0, partial_n2)
    sums = {}
    dec_partial = dot(after(dec_gq_rel, product), w_cq, NT).astype(BF16)
    partial_n2 = jnp.where(is_enc, partial_n2, dec_partial)

    def while_n2(anchor):
        grads, others = after((grad_e2_all, cot_all), input_product(1, anchor))
        (product,) = token_product(
            groups, (wide_units,), (0, grads, hidden2), (1, others, hidden3)
        )
        placed[2] = groups.to_place(product)
        sums["cross"] = groups.to_owner(after(placed["cross"], product))
        return product

    grad_n2 = reduce_tokens(partial_n2, while_n2)
    grad_step, gain_2 = norm_backward(x1, gain2, grad_n2)
    grad_x1 = jnp.where(is_enc, grad_e2, pad_rows(grad_x2d, enc_count)) + grad_step
    sums[0] = groups.to_owner(after(placed[0], sums["cross"]))

    grad_x1_all = gather_tokens(after(grad_x1.astype(BF16), placed[0]))
    grad_att = dot(grad_x1_all, w_out, NN).astype(BF16)
    grad_att, sums[0] = lax.optimization_barrier((grad_att, sums[0]))
    def enc_attend_back(qkv, lse, grad_att):
        gq, gkv, gb = attention_backward(
            enc_cfg, tp_arg, qkv, qkv, enc_idk, enc_idq, lse, grad_att, enc_bias
        )
        return columns([gq, gkv]), gb.reshape(heads, -1)

    def dec_attend_back(qkv, lse, grad_att):
        ordered = rows.to_rows(qkv, enc_count)
        lse = lse.reshape(-1)[: 3 * heads * DEC_LEN].reshape(3, heads, DEC_LEN)
        gq, gkv, gb = attention_backward(
            dec_cfg, tp_arg, ordered, ordered, dec_idk, dec_idq, lse,
            rows.to_rows(grad_att, enc_count), dec_bias,
        )
        gb = gb.reshape(heads, -1)
        return (
            rows.to_relative(columns([gq, gkv]), enc_count),
            jnp.pad(gb, ((0, 0), (0, enc_hot.shape[1] - gb.shape[1]))),
        )

    grad_qkv, grad_bias = lax.cond(is_enc, enc_attend_back, dec_attend_back, qkv, lse1, grad_att)
    (product,) = token_product(
        groups,
        (4 * width,),
        (0, norm1_all, grad_qkv),
        (0, grad_x1_all, att),
        (1, norm1_all, grad_qkv),
        (1, grad_x1_all, att),
    )
    placed["first"] = groups.to_place(product)
    sums[1] = groups.to_owner(after(placed[1], sums[0]))
    partial_n1 = dot(after(grad_qkv, product), w_qkv, NT).astype(BF16)
    partial_n1, sums[1] = lax.optimization_barrier((partial_n1, sums[1]))

    def while_n1(anchor):
        tables["grad"] = lax.cond(
            is_enc,
            lambda gb: bucket_sums(enc_hot, gb),
            lambda gb: bucket_sums(dec_hot, gb[:, : dec_hot.shape[1]]),
            after(grad_bias, anchor),
        )
        feed_out3 = dot(after(hidden3, tables["grad"]), feed_weights[2], NT).astype(BF16)
        queries["out"] = x2d + reduce_tokens(feed_out3, None, dec_groups)
        return feed_out3

    tables = {}
    sums[2] = groups.to_owner(after(placed[2], sums[1]))
    grad_n1 = reduce_tokens(partial_n1, while_n1)
    grad_step, gain_1 = norm_backward(x_f32, gain1, grad_n1)
    grad_x = grad_x1 + grad_step
    enc_first, dec_first = groups.to_owner(after(placed["first"], sums[2]))
    enc_cross, dec_cross = sums["cross"]
    (enc_gate, dec_gate), (enc_up, dec_up), (enc_down, dec_down) = sums[0], sums[1], sums[2]

    gain_rows = jnp.stack([gain_1, gain_2, jnp.where(is_enc, gain_ef, gain_d3)])
    gain_rows = gain_rows + core_swap(gain_rows)
    gain_rows = gain_rows + pair_swap(gain_rows)
    small = jnp.concatenate([gain_rows.reshape(-1), tables["grad"].reshape(-1)])
    length = small.shape[0]
    small = jnp.pad(small, (0, -length % 1024)).reshape(-1, 128)
    enc_small, dec_small = groups.all_role_sums(after(small, sums[2]))

    def unpack(total):
        flat = total.reshape(-1)
        gain = flat[: gain_rows.size].reshape(gain_rows.shape)
        share = gain.shape[1] // groups.count
        mine = lax.dynamic_slice_in_dim(gain, groups.where * share, share, axis=1)
        return mine, flat[gain_rows.size : length].reshape(BUCKETS, heads)

    enc_gains, enc_table_grad = unpack(enc_small)
    dec_gains, dec_table_grad = unpack(dec_small)

    def part(value, index):
        return value[:, index * width : (index + 1) * width]

    zero_bf = jnp.zeros((), BF16)
    return (
        jnp.where(is_enc, zero_bf, queries["out"].astype(BF16))[None],
        jnp.where(is_enc, grad_x.astype(BF16), zero_bf)[None],
        jnp.where(is_enc, zero_bf, grad_x[:dec_count].astype(BF16))[None],
        enc_gains[0],
        part(enc_first, 0),
        part(enc_first, 1),
        part(enc_first, 2),
        part(enc_first, 3).T,
        enc_table_grad,
        enc_gains[1],
        enc_gate[:, :units],
        enc_up[:, :units],
        enc_down[:, :units].T,
        enc_gains[2],
        dec_gains[0],
        part(dec_first, 0),
        part(dec_first, 1),
        part(dec_first, 2),
        part(dec_first, 3).T,
        dec_table_grad,
        dec_gains[1],
        part(dec_cross, 0),
        part(enc_cross, 0),
        part(enc_cross, 1),
        part(dec_cross, 1).T,
        dec_gains[2],
        dec_gate[:, :units],
        dec_up[:, :units],
        dec_down[:, :units].T,
    )


def solution(mesh):
    vector, matrix, turned = P("grp"), P("grp", "tp"), P("tp", "grp")
    tokens, ids, table = P("grp", "tp", None), P("grp", None, None), P(None, "tp")
    enc = (vector, matrix, matrix, matrix, turned, table, vector, matrix, matrix, turned, vector)
    dec = (vector, matrix, matrix, matrix, turned, table, vector, matrix, matrix, matrix, turned)
    dec = dec + (vector, matrix, matrix, turned)
    return jax.shard_map(
        body,
        mesh=mesh,
        in_specs=(tokens, tokens, tokens, ids, ids) + enc + dec,
        out_specs=(tokens, tokens, tokens) + enc + dec,
        check_vma=False,
    )
```

```python
import math
from functools import partial

import jax
import jax.numpy as jnp
import numpy as np
from jax import lax
from jax.experimental import pallas as pl
from jax.experimental.pallas import tpu as pltpu
from jax.sharding import PartitionSpec as P

HEAD_DIM = 64
BUCKETS = 32
MAX_DIST = 128
DEC_LEN = 192
EPSILON = 1e-06
NEG_FILL = -1e30
QB = 128
F32 = jnp.float32
BF16 = jnp.bfloat16


def bucket_of(relative, two_sided):
    bucket_count = BUCKETS
    shifted = relative * 0
    if two_sided:
        bucket_count = bucket_count // 2
        shifted = shifted + (relative > 0) * bucket_count
        distance = np.abs(relative)
    else:
        distance = np.maximum(-relative, 0)
    exact_span = bucket_count // 2
    log_ratio = np.log(np.maximum(distance, 1) / exact_span) / np.log(MAX_DIST / exact_span)
    farther = np.minimum(
        exact_span + np.floor(log_ratio * (bucket_count - exact_span) + 1e-09).astype(np.int32),
        bucket_count - 1,
    )
    return (shifted + np.where(distance < exact_span, distance, farther)).astype(np.int32)


def one_hot_blocks(relative, two_sided):
    return np.eye(BUCKETS, dtype=np.float32)[:, bucket_of(relative, two_sided).reshape(-1)]


def enc_relative():
    return np.arange(-2 * QB, 3 * QB)[:, None] - np.arange(QB)[None, :]


def dec_relative():
    return np.arange(DEC_LEN)[:, None] - np.arange(DEC_LEN)[None, :]


def after(value, *others):
    return lax.optimization_barrier((value,) + others)[0]


def dot(left, right, dims):
    return lax.dot_general(left, right, (dims, ((), ())), preferred_element_type=F32)


NN = ((1,), (0,))
NT = ((1,), (1,))
TN = ((0,), (0,))


def block_of(place, tp):
    wide = place // 2
    swapped = (wide % 2) * 2 + wide // 2
    return (swapped ^ tp) * 2 + place % 2


def scores_t(head, cfg, keys, queries, bias_ref, same, place, tp):
    lanes = slice(head * HEAD_DIM, (head + 1) * HEAD_DIM)
    scores = dot(keys[:, lanes], queries[:, lanes], NT)
    if cfg["bias"] == "blocks":
        mine = block_of(place, tp)
        parts = []
        for kb in range(keys.shape[0] // QB):
            step = jnp.clip(block_of(kb, tp) - mine, -2, 2) + 2
            parts.append(bias_ref[head, step])
        scores = scores + jnp.concatenate(parts, axis=0)
    elif cfg["bias"] == "full":
        scores = scores + bias_ref[head]
    return jnp.where(same, scores, NEG_FILL)


def allowed_t(cfg, idk_ref, idq_ref):
    same = idk_ref[...] == idq_ref[0]
    if cfg["causal"]:
        key_pos = lax.broadcasted_iota(jnp.int32, same.shape, 0)
        query_pos = lax.broadcasted_iota(jnp.int32, same.shape, 1)
        same = same & (key_pos <= query_pos)
    return same


def forward_kernel(cfg, tp_ref, q_ref, kv_ref, idk_ref, idq_ref, *rest):
    if cfg["bias"]:
        bias_ref, out_ref, lse_ref, vt_ref = rest
    else:
        bias_ref, (out_ref, lse_ref, vt_ref) = None, rest
    heads = cfg["heads"]
    width = heads * HEAD_DIM
    place = pl.program_id(0)
    keys = kv_ref[:, cfg["k"] : cfg["k"] + width]

    def fill():
        vt_ref[...] = kv_ref[:, cfg["v"] : cfg["v"] + width].T

    if cfg["follow"]:
        fill()
    else:
        pl.when(place == 0)(fill)
    queries = q_ref[:, :width]
    same = allowed_t(cfg, idk_ref, idq_ref)
    outs = []
    for head in range(heads):
        scores = scores_t(head, cfg, keys, queries, bias_ref, same, place, tp_ref[0])
        peak = jnp.max(scores, axis=0, keepdims=True)
        exponent = jnp.exp(scores - peak)
        total = jnp.sum(exponent, axis=0, keepdims=True)
        weights = (exponent * (1.0 / total)).astype(BF16)
        outs.append(dot(vt_ref[head * HEAD_DIM : (head + 1) * HEAD_DIM, :], weights, NN))
        lse_ref[0, head : head + 1, :] = peak + jnp.log(total)
    out_ref[...] = jnp.concatenate(outs, axis=0).T.astype(BF16)


def backward_kernel(cfg, tp_ref, q_ref, kv_ref, idk_ref, idq_ref, *rest):
    if cfg["bias"]:
        bias_ref, lse_ref, go_ref, gq_ref, gkv_ref, gb_ref, kt_ref, acc_ref = rest
    else:
        bias_ref, gb_ref = None, None
        lse_ref, go_ref, gq_ref, gkv_ref, kt_ref, acc_ref = rest
    heads = cfg["heads"]
    width = heads * HEAD_DIM
    place = pl.program_id(0)
    keys = kv_ref[:, cfg["k"] : cfg["k"] + width]
    values = kv_ref[:, cfg["v"] : cfg["v"] + width]

    def clear():
        kt_ref[...] = kv_ref[:, cfg["k"] : cfg["k"] + width].T
        acc_ref[...] = jnp.zeros_like(acc_ref)

    def clear_bias():
        if gb_ref is not None:
            gb_ref[...] = jnp.zeros_like(gb_ref)

    pl.when(place == 0)(clear_bias)
    if cfg["follow"]:
        clear()
    else:
        pl.when(place == 0)(clear)
    queries = q_ref[:, :width]
    grad_out = go_ref[...]
    same = allowed_t(cfg, idk_ref, idq_ref)
    grads = []
    for head in range(heads):
        lanes = slice(head * HEAD_DIM, (head + 1) * HEAD_DIM)
        scores = scores_t(head, cfg, keys, queries, bias_ref, same, place, tp_ref[0])
        weights = jnp.exp(scores - lse_ref[0, head : head + 1, :])
        grad_weights = dot(values[:, lanes], grad_out[:, lanes], NT)
        delta = jnp.sum(grad_weights * weights, axis=0, keepdims=True)
        grad_scores = weights * (grad_weights - delta)
        if cfg["bias"] == "blocks":
            mine = block_of(place, tp_ref[0])
            for kb in range(keys.shape[0] // QB):
                step = jnp.clip(block_of(kb, tp_ref[0]) - mine, -2, 2) + 2
                gb_ref[head, step] += grad_scores[kb * QB : (kb + 1) * QB]
        elif cfg["bias"] == "full":
            gb_ref[head] += grad_scores
        scores_bf = grad_scores.astype(BF16)
        acc_ref[head] += dot(scores_bf, queries[:, lanes], NN)
        acc_ref[heads + head] += dot(weights.astype(BF16), grad_out[:, lanes], NN)
        grads.append(dot(kt_ref[lanes, :], scores_bf, NN))
    gq_ref[...] = jnp.concatenate(grads, axis=0).T.astype(BF16)

    def finish():
        gkv_ref[...] = jnp.concatenate(
            [acc_ref[k].astype(BF16) for k in range(2 * heads)], axis=1
        )

    if cfg["follow"]:
        finish()
    else:
        pl.when(place == pl.num_programs(0) - 1)(finish)


def attention_specs(cfg, q_cols, kv_cols, bias):
    bq, bk = cfg["bq"], cfg["bk"]
    follow = cfg["follow"]
    specs = [
        pl.BlockSpec((bq, q_cols), lambda i, s: (i, 0)),
        pl.BlockSpec((bk, kv_cols), (lambda i, s: (i, 0)) if follow else (lambda i, s: (0, 0))),
        pl.BlockSpec((bk, bq), (lambda i, s: (i, 0)) if follow else (lambda i, s: (0, 0))),
        pl.BlockSpec((1, 1, bq), lambda i, s: (i, 0, 0)),
    ]
    if bias is not None:
        rank = bias.ndim
        specs.append(pl.BlockSpec(bias.shape, lambda i, s: (0,) * rank))
    return specs


def attention_forward(cfg, tp, q, kv, idk, idq, bias=None):
    heads, bq, bk, steps = cfg["heads"], cfg["bq"], cfg["bk"], cfg["steps"]
    width = heads * HEAD_DIM
    extra = () if bias is None else (bias,)
    return pl.pallas_call(
        partial(forward_kernel, cfg),
        out_shape=(
            jax.ShapeDtypeStruct((steps * bq, width), BF16),
            jax.ShapeDtypeStruct((steps, heads, bq), F32),
        ),
        grid_spec=pltpu.PrefetchScalarGridSpec(
            num_scalar_prefetch=1,
            grid=(steps,),
            in_specs=attention_specs(cfg, q.shape[1], kv.shape[1], bias),
            out_specs=(
                pl.BlockSpec((bq, width), lambda i, s: (i, 0)),
                pl.BlockSpec((1, heads, bq), lambda i, s: (i, 0, 0)),
            ),
            scratch_shapes=[pltpu.VMEM((width, bk), BF16)],
        ),
        compiler_params=pltpu.CompilerParams(vmem_limit_bytes=40 << 20),
        name=cfg["name"] + "_forward",
    )(tp, q, kv, idk, idq, *extra)


def attention_backward(cfg, tp, q, kv, idk, idq, lse, grad_out, bias=None):
    heads, bq, bk, steps = cfg["heads"], cfg["bq"], cfg["bk"], cfg["steps"]
    width = heads * HEAD_DIM
    follow = cfg["follow"]
    extra = () if bias is None else (bias,)
    out_shape = [
        jax.ShapeDtypeStruct((steps * bq, width), BF16),
        jax.ShapeDtypeStruct((steps * bk if follow else bk, 2 * width), BF16),
    ]
    out_specs = [
        pl.BlockSpec((bq, width), lambda i, s: (i, 0)),
        pl.BlockSpec((bk, 2 * width), (lambda i, s: (i, 0)) if follow else (lambda i, s: (0, 0))),
    ]
    if bias is not None:
        rank = bias.ndim
        out_shape.append(jax.ShapeDtypeStruct(bias.shape, F32))
        out_specs.append(pl.BlockSpec(bias.shape, lambda i, s: (0,) * rank))
    return pl.pallas_call(
        partial(backward_kernel, cfg),
        out_shape=tuple(out_shape),
        grid_spec=pltpu.PrefetchScalarGridSpec(
            num_scalar_prefetch=1,
            grid=(steps,),
            in_specs=attention_specs(cfg, q.shape[1], kv.shape[1], bias)
            + [
                pl.BlockSpec((1, heads, bq), lambda i, s: (i, 0, 0)),
                pl.BlockSpec((bq, width), lambda i, s: (i, 0)),
            ],
            out_specs=tuple(out_specs),
            scratch_shapes=[pltpu.VMEM((width, bk), BF16), pltpu.VMEM((2 * heads, bk, HEAD_DIM), F32)],
        ),
        compiler_params=pltpu.CompilerParams(vmem_limit_bytes=48 << 20),
        name=cfg["name"] + "_backward",
    )(tp, q, kv, idk, idq, *extra, lse, grad_out)


def product_kernel(quarter, share, step, jobs, widths, role_ref, *refs):
    operands, out_refs = refs[: 2 * len(jobs)], refs[2 * len(jobs) :]
    starts = [sum(widths[:k]) for k in range(len(widths))]
    for index, (on_role, column) in enumerate(jobs):
        left_ref, right_ref = operands[2 * index], operands[2 * index + 1]

        @pl.when(role_ref[0] == on_role)
        def _():
            result = dot(left_ref[...], right_ref[...], TN).astype(BF16)
            rows_here, cols_here = result.shape
            first = pl.program_id(0) * (rows_here // step)
            for unit in range(rows_here // step):
                row = (first + unit) * step
                owner, offset = row // share, pl.multiple_of(row % share, step)
                for out_ref, start, cols in zip(out_refs, starts, widths):
                    low, high = max(start, column), min(start + cols, column + cols_here)
                    if low < high:
                        out_ref[
                            owner % quarter,
                            owner // quarter,
                            pl.ds(offset, step),
                            low - start : high - start,
                        ] = result[unit * step : (unit + 1) * step, low - column : high - column]


def token_product(groups, widths, *jobs):
    rows_count = jobs[0][1].shape[1]
    tile = 512
    share = rows_count // groups.count
    step = math.gcd(share, 64)
    offsets, described, operands, specs = {}, [], [], []
    for role, left, right, *block in jobs:
        count, cols = right.shape
        cols = sum(widths) if block else cols
        described.append((role, offsets.get(role, 0)))
        offsets[role] = offsets.get(role, 0) + cols

        def left_map(i, s, role=role):
            return (0, jnp.where(s[0] == role, i, 0))

        operands += [left, right]
        specs += [
            pl.BlockSpec((count, tile), left_map),
            pl.BlockSpec(
                (count, cols),
                lambda i, s, block=(block or [0])[0]: (0, block),
                pipeline_mode=pl.Buffered(1),
            ),
        ]
    shapes = [(groups.quarter, 4, share, cols) for cols in widths]
    role = jnp.where(groups.is_enc, 0, 1).astype(jnp.int32)[None]
    return pl.pallas_call(
        partial(product_kernel, groups.quarter, share, step, described, widths),
        out_shape=tuple(jax.ShapeDtypeStruct(dims, BF16) for dims in shapes),
        grid_spec=pltpu.PrefetchScalarGridSpec(
            num_scalar_prefetch=1,
            grid=(rows_count // tile,),
            in_specs=specs,
            out_specs=tuple(pl.BlockSpec(dims, lambda i, s: (0, 0, 0, 0)) for dims in shapes),
        ),
        compiler_params=pltpu.CompilerParams(vmem_limit_bytes=56 << 20),
        name="token_product",
    )(role, *operands)


def bucket_sums(hot, values):
    high = values.astype(BF16)
    low = (values - high.astype(F32)).astype(BF16)
    sums = dot(jnp.asarray(hot, BF16), jnp.concatenate([high, low], axis=0), NT)
    return sums[:, : values.shape[0]] + sums[:, values.shape[0] :]


def rms_scale(hidden, gain_vec):
    return (
        hidden * lax.rsqrt(jnp.mean(hidden * hidden, axis=-1, keepdims=True) + EPSILON) * gain_vec
    )


def norm_backward(hidden, gain_vec, grad_out):
    rate = lax.rsqrt(jnp.mean(hidden * hidden, axis=-1, keepdims=True) + EPSILON)
    scaled = gain_vec * grad_out
    inner = jnp.mean(hidden * scaled, axis=-1, keepdims=True)
    grad_in = rate * scaled - hidden * (rate * rate * rate * inner)
    return grad_in, jnp.sum(grad_out * hidden * rate, axis=0)


GELU_SCALE = float(np.sqrt(2.0 / np.pi))
GELU_CUBIC = 0.044715


def gelu_parts(value):
    square = value * value
    tanh = jnp.tanh(GELU_SCALE * (value + GELU_CUBIC * (value * square)))
    half = 0.5 * (1.0 + tanh)
    slope = half + 0.5 * value * (1.0 - tanh * tanh) * (
        GELU_SCALE * (1.0 + 3.0 * GELU_CUBIC * square)
    )
    return value * half, slope


def gelu(value):
    cubic = value + GELU_CUBIC * (value * value * value)
    return value * (0.5 * (1.0 + jnp.tanh(GELU_SCALE * cubic)))


def feed_kernel(tok_ref, wg_ref, wu_ref, wd_ref, out_ref, gate_ref, up_ref):
    tokens = tok_ref[...]
    gate = dot(tokens, wg_ref[...], NN)
    up = dot(tokens, wu_ref[...], NN)
    gate_ref[...] = gate
    up_ref[...] = up
    hidden = (gelu(gate) * up).astype(BF16)
    out_ref[...] = dot(hidden, wd_ref[...], NT).astype(BF16)


def feed_grads(gate, up, grad_hidden, wg_ref, wu_ref, gn_ref, both_ref, hid_ref):
    units = gate.shape[1]
    activated, slope = gelu_parts(gate)
    hid_ref[...] = (activated * up).astype(BF16)
    grad_gate = (grad_hidden * up * slope).astype(BF16)
    grad_up = (grad_hidden * activated).astype(BF16)
    both_ref[:, :units] = grad_gate
    both_ref[:, units:] = grad_up
    gn_ref[...] = (dot(grad_gate, wg_ref[...], NT) + dot(grad_up, wu_ref[...], NT)).astype(BF16)


def feed_back_kernel(gate_ref, up_ref, ga_ref, wg_ref, wu_ref, wd_ref, *outs):
    grad_hidden = dot(ga_ref[...], wd_ref[...], NN)
    feed_grads(gate_ref[...], up_ref[...], grad_hidden, wg_ref, wu_ref, *outs)


def feed_both_kernel(tok_ref, gh_ref, wg_ref, wu_ref, *outs):
    tokens = tok_ref[...]
    gate = dot(tokens, wg_ref[...], NN)
    up = dot(tokens, wu_ref[...], NN)
    feed_grads(gate, up, gh_ref[...], wg_ref, wu_ref, *outs)


def feed_call(name, kernel, tile, streamed, weights, outs):
    count = streamed[0].shape[0]
    return pl.pallas_call(
        kernel,
        out_shape=tuple(jax.ShapeDtypeStruct((count, cols), kind) for cols, kind in outs),
        grid=(count // tile,),
        in_specs=[pl.BlockSpec((tile, a.shape[1]), lambda i: (i, 0)) for a in streamed]
        + [
            pl.BlockSpec(w.shape, lambda i: (0, 0), pipeline_mode=pl.Buffered(1)) for w in weights
        ],
        out_specs=tuple(pl.BlockSpec((tile, cols), lambda i: (i, 0)) for cols, _ in outs),
        compiler_params=pltpu.CompilerParams(vmem_limit_bytes=50 << 20),
        name=name,
    )(*streamed, *weights)


SWAP_CORE = [(0, 1), (1, 0), (2, 3), (3, 2)]
SWAP_PAIR = [(0, 2), (2, 0), (1, 3), (3, 1)]


def tp_swap(value, pairs, groups=None):
    if groups is None:
        return lax.ppermute(value, "tp", pairs)
    size = lax.axis_size("tp")
    flat = [(g * size + source, g * size + target) for g in groups for source, target in pairs]
    return lax.ppermute(value, ("grp", "tp"), flat)


def core_swap(value, groups=None):
    return tp_swap(value, SWAP_CORE, groups)


def pair_swap(value, groups=None):
    return tp_swap(value, SWAP_PAIR, groups)


def gather_tokens(own, meanwhile=None, groups=None):
    far = pair_swap(own, groups)
    if meanwhile is not None:
        far = after(far, meanwhile(own))
    return jnp.concatenate([own, far, core_swap(own, groups), core_swap(far, groups)], axis=0)


def reduce_tokens(partial_bf, meanwhile=None, groups=None):
    count = partial_bf.shape[0] // 4
    other = core_swap(partial_bf[2 * count :], groups)
    away = (partial_bf[count : 2 * count].astype(F32) + other[count:].astype(F32)).astype(BF16)
    far = pair_swap(away, groups)
    if meanwhile is not None:
        far = after(far, meanwhile(away))
    return partial_bf[:count].astype(F32) + other[:count].astype(F32) + far.astype(F32)


class Groups:
    def __init__(self):
        self.count = lax.axis_size("grp")
        self.quarter = self.count // 4
        where = lax.axis_index("grp")
        self.where = where
        self.role = where // self.quarter
        self.place = where % self.quarter
        self.is_enc = self.role < 3
        self.peers = [
            [a * self.quarter + j for j in range(self.quarter)] for a in range(4)
        ]
        self.swap = [(i, i ^ 1) for i in range(self.count)]
        self.swapped = None
        self.roles = [
            [a * self.quarter + j for a in range(4)] for j in range(self.quarter)
        ]

    def shift(self, value, steps):
        hop = steps * self.quarter
        return lax.ppermute(
            value, "grp", [(i, (i + hop) % self.count) for i in range(self.count)]
        )

    def send(self, value, source, target):
        q = self.quarter
        return lax.ppermute(
            value, "grp", [(source * q + j, target * q + j) for j in range(q)]
        )

    def gather(self, chunks):
        fulls, last, brought = [], {}, []
        for enc, dec in chunks:
            rows, cols = enc.shape
            shards = [jnp.where(self.is_enc, enc, dec)]
            for step in (1, 2, 3):
                payload = jnp.where((self.role + step) % 4 < 3, enc, dec)
                if step in last:
                    payload = after(payload, last[step])
                last[step] = self.shift(payload, step)
                shards.append(last[step])
            brought.append(tuple(shards[1:]))
            full = jnp.zeros((4, self.quarter, rows, cols), enc.dtype)
            for step, shard in enumerate(shards):
                source = (self.role - step) % 4
                if self.quarter == 2:
                    other = lax.ppermute(shard, "grp", self.swap)
                    full = lax.dynamic_update_slice(
                        full, shard[None, None], (source, self.place, 0, 0)
                    )
                    full = lax.dynamic_update_slice(
                        full, other[None, None], (source, 1 - self.place, 0, 0)
                    )
                else:
                    group = lax.all_gather(shard, "grp", axis_index_groups=self.peers)
                    full = lax.dynamic_update_slice(full, group[None], (source, 0, 0, 0))
            fulls.append(full.reshape(-1, cols))
        return fulls, brought

    def gather_whole(self, enc, dec, pieces, *anchors):
        rows, cols = enc.shape
        payload = jnp.stack([enc, enc, enc, dec])
        held = self.to_quarters(after(payload, *anchors) if anchors else payload)
        if self.quarter == 2:
            full = jnp.zeros((4, 2, rows, cols), enc.dtype)
            full = lax.dynamic_update_slice(full, held[:, None], (0, self.place, 0, 0))
            for low in range(0, 4, 4 // pieces):
                piece = held[low : low + 4 // pieces]
                if self.swapped is not None:
                    piece = after(piece, self.swapped)
                self.swapped = lax.ppermute(piece, "grp", self.swap)
                full = lax.dynamic_update_slice(
                    full, self.swapped[:, None], (low, 1 - self.place, 0, 0)
                )
        else:
            full = lax.all_gather(held, "grp", axis=1, axis_index_groups=self.peers)
        return full.reshape(-1, cols), held

    def to_quarters(self, blocks):
        return lax.all_to_all(
            blocks, "grp", 0, 0, tiled=True, axis_index_groups=self.roles
        )

    def peer_sum(self, value):
        if self.quarter == 2:
            return value + lax.ppermute(value, "grp", self.swap)
        return lax.psum(value, "grp", axis_index_groups=self.peers)

    def role_sums(self, mine):
        enc_total, dec_total = 0.0, 0.0
        for step in range(4):
            target = (self.role + step) % 4
            block = lax.dynamic_index_in_dim(mine, target, 0, keepdims=False)
            if step:
                block = self.shift(block, step)
            block = block.astype(F32)
            source_enc = (self.role - step) % 4 < 3
            enc_total = enc_total + jnp.where(source_enc, block, 0.0)
            dec_total = dec_total + jnp.where(source_enc, 0.0, block)
        return enc_total, dec_total

    def to_place(self, product):
        return lax.psum_scatter(
            product, "grp", scatter_dimension=0, axis_index_groups=self.peers
        )

    def to_owner(self, mine):
        parts = self.to_quarters(mine).astype(F32)
        return parts[0] + parts[1] + parts[2], parts[3]

    def all_role_sums(self, value):
        value = self.peer_sum(value)
        return self.role_sums(jnp.broadcast_to(value[None], (4,) + value.shape))


def pad_rows(value, count):
    return jnp.pad(value, ((0, count - value.shape[0]), (0, 0)))


class DecoderRows:
    def __init__(self, tp, count, stride):
        self.count, self.stride, self.tp = count, stride, tp

    @staticmethod
    def flip(index):
        return (index % 2) * 2 + index // 2

    def to_rows(self, value, stride):
        return jnp.concatenate(
            [
                lax.dynamic_slice_in_dim(
                    value, self.flip(i ^ self.tp) * stride, self.count, axis=0
                )
                for i in range(4)
            ],
            axis=0,
        )

    def to_relative(self, value, stride):
        return jnp.concatenate(
            [
                pad_rows(
                    lax.dynamic_slice_in_dim(
                        value, (self.flip(b) ^ self.tp) * self.count, self.count, axis=0
                    ),
                    stride,
                )
                for b in range(4)
            ],
            axis=0,
        )


def body(
    enc_in,
    dec_in,
    dec_cot,
    enc_seg,
    dec_seg,
    enc_norm1,
    enc_wq,
    enc_wk,
    enc_wv,
    enc_wo,
    enc_table,
    enc_norm2,
    enc_wgate,
    enc_wup,
    enc_wdown,
    enc_normf,
    dec_norm1,
    dec_wq,
    dec_wk,
    dec_wv,
    dec_wo,
    dec_table,
    dec_norm2,
    cross_wq,
    cross_wk,
    cross_wv,
    cross_wo,
    dec_norm3,
    dec_wgate,
    dec_wup,
    dec_wdown,
):
    groups = Groups()
    is_enc = groups.is_enc
    tp = lax.axis_index("tp")
    tp_arg = tp.astype(jnp.int32)[None]
    heads = enc_table.shape[1]
    width = heads * HEAD_DIM
    enc_count = enc_in.shape[1]
    dec_count = dec_in.shape[1]
    enc_len = enc_seg.shape[-1]
    rows = DecoderRows(tp, dec_count, enc_count)

    def columns(parts):
        return jnp.concatenate(parts, axis=1)

    x_own = jnp.where(is_enc, enc_in[0], pad_rows(dec_in[0], enc_count))
    x_all = gather_tokens(x_own)
    units = enc_wgate.shape[1]
    padded = -units % 128

    def first_chunk(weights, gains, w_out):
        gains = jnp.pad(jnp.stack(gains, axis=1), ((0, 0), (0, -len(gains) % 64)))
        parts = columns(list(weights) + [gains, w_out])
        return jnp.pad(parts, ((0, 0), (0, -parts.shape[1] % 128)))

    def wide(weight):
        return jnp.pad(weight, ((0, 0), (0, padded)))

    (first,), brought = groups.gather(
        [
            (
                first_chunk(
                    [enc_wq, enc_wk, enc_wv], [enc_norm1, enc_norm2, enc_normf], enc_wo.T
                ),
                first_chunk(
                    [dec_wq, dec_wk, dec_wv], [dec_norm1, dec_norm2, dec_norm3], dec_wo.T
                ),
            ),
        ]
    )
    w_gate, held_gate = groups.gather_whole(
        wide(enc_wgate), wide(dec_wgate), 1, brought[0][0]
    )
    w_up, held_up = groups.gather_whole(wide(enc_wup), wide(dec_wup), 2, held_gate)
    w_down, held_down = groups.gather_whole(wide(enc_wdown.T), wide(dec_wdown.T), 1, held_up)
    w_cross, held_cross = groups.gather_whole(
        columns([cross_wk, cross_wv]), columns([cross_wq, cross_wo.T]), 1, held_down
    )
    w_qkv = first[:, : 3 * width]
    gains = first[:, 3 * width : 3 * width + 3].astype(F32).T
    gains = after(gains, held_gate)
    gain1, gain2, gain3 = gains[0:1], gains[1:2], gains[2:3]
    w_out = first[:, 3 * width + 64 : 4 * width + 64]
    w_cq, w_co = w_cross[:, :width], w_cross[:, width:]
    cot_own = dec_cot[0]
    dec_groups = range(3 * groups.quarter, groups.count)
    cot_all = gather_tokens(cot_own, None, dec_groups)
    enc_table, dec_table = after((enc_table, dec_table), brought[0])

    enc_ids = enc_seg[0, 0].astype(F32)
    ids_rel = jnp.concatenate(
        [
            lax.dynamic_slice_in_dim(enc_ids, (DecoderRows.flip(b) ^ tp) * enc_count, enc_count)
            for b in range(4)
        ]
    )
    dec_ids = dec_seg[0]
    enc_hot = one_hot_blocks(enc_relative(), True)
    dec_hot = one_hot_blocks(dec_relative(), False)
    enc_bias = dot(enc_table, jnp.asarray(enc_hot, BF16), TN).reshape(heads, 5, QB, QB)
    dec_bias = dot(dec_table, jnp.asarray(dec_hot, BF16), TN).reshape(heads, DEC_LEN, DEC_LEN)

    enc_cfg = dict(
        name="enc", heads=heads, bq=QB, bk=enc_len, steps=enc_len // QB, follow=False,
        bias="blocks", causal=False, k=width, v=2 * width,
    )
    dec_cfg = dict(
        name="dec", heads=heads, bq=DEC_LEN, bk=DEC_LEN, steps=3, follow=True,
        bias="full", causal=True, k=width, v=2 * width,
    )
    cross_cfg = dict(
        name="cross", heads=heads, bq=DEC_LEN, bk=enc_len, steps=1, follow=False,
        bias=None, causal=False, k=0, v=width,
    )
    enc_idk = jnp.broadcast_to(ids_rel[:, None], (enc_len, QB))
    enc_idq = ids_rel.reshape(enc_len // QB, 1, QB)
    dec_idk = jnp.broadcast_to(dec_ids.astype(F32).reshape(-1, 1), (3 * DEC_LEN, DEC_LEN))
    dec_idq = dec_ids.astype(F32).reshape(3, 1, DEC_LEN)
    cross_idk = jnp.broadcast_to(ids_rel[:, None], (enc_len, DEC_LEN))

    x_f32 = x_own.astype(F32)
    norm1_all = rms_scale(x_all.astype(F32), gain1).astype(BF16)
    qkv = dot(norm1_all, w_qkv, NN).astype(BF16)

    def enc_attend(qkv):
        return attention_forward(enc_cfg, tp_arg, qkv, qkv, enc_idk, enc_idq, enc_bias)

    def dec_attend(qkv):
        ordered = rows.to_rows(qkv, enc_count)
        out, lse = attention_forward(dec_cfg, tp_arg, ordered, ordered, dec_idk, dec_idq, dec_bias)
        return rows.to_relative(out, enc_count), jnp.pad(
            lse.reshape(-1), (0, heads * enc_len - lse.size)
        ).reshape(enc_len // QB, heads, QB)

    att, lse1 = lax.cond(is_enc, enc_attend, dec_attend, after(qkv, held_gate, cot_all))
    x1 = x_f32 + reduce_tokens(dot(after(att, held_up), w_out, NT).astype(BF16))

    norm2_all = gather_tokens(after(rms_scale(x1, gain2).astype(BF16), held_down))
    feed_weights = (w_gate, w_up, after(w_down, held_cross))
    wide_units = w_gate.shape[1]
    width_all = x_own.shape[1]
    feed_out2, gate2, up2 = feed_call(
        "feed_forward", feed_kernel, 512, (norm2_all,), feed_weights,
        ((width_all, BF16), (wide_units, F32), (wide_units, F32)),
    )
    queries = {}

    def while_feed(anchor):
        dec_q_rel = dot(after(norm2_all, anchor), w_cq, NN).astype(BF16)
        dec_q = rows.to_rows(dec_q_rel, enc_count).reshape(3, DEC_LEN, width)
        dec_q = jnp.concatenate([dec_q, dec_ids.astype(BF16)[:, :, None]], axis=2)
        queries["sent"] = sum(groups.send(dec_q[r], 3, r) for r in range(3))
        return queries["sent"]

    def while_reduce(anchor):
        queries["hidden"] = dot(after(cot_all, anchor), feed_weights[2], NN)
        return queries["hidden"]

    x2 = x1 + reduce_tokens(feed_out2, while_reduce)
    memory = gather_tokens(rms_scale(x2, gain3).astype(BF16), while_feed)
    cross_idq = queries["sent"][:, width].astype(F32).reshape(1, 1, DEC_LEN)
    cross_q = queries["sent"][:, :width]

    cross_kv = dot(memory, w_cross, NN).astype(BF16)
    cross_o, lse2 = attention_forward(cross_cfg, tp_arg, cross_q, cross_kv, cross_idk, cross_idq)
    dec_o = jnp.concatenate([groups.send(cross_o, r, 3) for r in range(3)], axis=0)
    dec_o_rel = rows.to_relative(dec_o, dec_count)

    x2d = x1[:dec_count] + reduce_tokens(dot(dec_o_rel, w_co, NT).astype(BF16))
    norm3_all = gather_tokens(rms_scale(x2d, gain3).astype(BF16))
    grad_outs = ((width_all, BF16), (2 * wide_units, BF16), (wide_units, BF16))
    partial_n3, both3, hidden3 = feed_call(
        "feed_both", feed_both_kernel, 288, (norm3_all, queries["hidden"]), feed_weights[:2],
        grad_outs,
    )
    grad_n3 = reduce_tokens(partial_n3)
    grad_step, gain_d3 = norm_backward(x2d, gain3, grad_n3)
    grad_x2d = cot_own.astype(F32) + grad_step
    grad2_all = gather_tokens(grad_x2d.astype(BF16))
    grad_o_rel = dot(grad2_all, w_co, NN).astype(BF16)
    grad_o_rows = rows.to_rows(grad_o_rel, dec_count).reshape(3, DEC_LEN, width)
    cross_go = sum(groups.send(grad_o_rows[r], 3, r) for r in range(3))
    cross_gq, cross_gkv = attention_backward(
        cross_cfg, tp_arg, cross_q, cross_kv, cross_idk, cross_idq, lse2, cross_go
    )
    dec_gq = jnp.concatenate([groups.send(cross_gq, r, 3) for r in range(3)], axis=0)
    dec_gq_rel = rows.to_relative(dec_gq, enc_count)
    placed = {}

    def while_memory(anchor):
        left, right = after((memory, norm2_all), anchor)
        (product,) = token_product(
            groups,
            (2 * width,),
            (0, left, cross_gkv),
            (1, right, dec_gq_rel),
            (1, grad2_all, dec_o_rel),
        )
        placed["cross"] = groups.to_place(product)
        return product

    grad_memory = reduce_tokens(dot(cross_gkv, w_cross, NT).astype(BF16), while_memory)
    grad_memory = grad_memory.astype(BF16).astype(F32)
    grad_e2, gain_ef = norm_backward(x2, gain3, grad_memory)


    grad_e2_all = gather_tokens(grad_e2.astype(BF16))
    partial_n2, both2, hidden2 = feed_call(
        "feed_back", feed_back_kernel, 256, (gate2, up2, grad_e2_all), feed_weights, grad_outs
    )

    def input_product(index, anchor):
        tokens, others = after((norm2_all, norm3_all), anchor)
        (product,) = token_product(
            groups, (wide_units,), (0, tokens, both2, index), (1, others, both3, index)
        )
        placed[index] = groups.to_place(product)
        return product

    product = input_product(0, partial_n2)
    sums = {}
    dec_partial = dot(after(dec_gq_rel, product), w_cq, NT).astype(BF16)
    partial_n2 = jnp.where(is_enc, partial_n2, dec_partial)

    def while_n2(anchor):
        grads, others = after((grad_e2_all, cot_all), input_product(1, anchor))
        (product,) = token_product(
            groups, (wide_units,), (0, grads, hidden2), (1, others, hidden3)
        )
        placed[2] = groups.to_place(product)
        sums["cross"] = groups.to_owner(after(placed["cross"], product))
        return product

    grad_n2 = reduce_tokens(partial_n2, while_n2)
    grad_step, gain_2 = norm_backward(x1, gain2, grad_n2)
    grad_x1 = jnp.where(is_enc, grad_e2, pad_rows(grad_x2d, enc_count)) + grad_step
    sums[0] = groups.to_owner(after(placed[0], sums["cross"]))

    grad_x1_all = gather_tokens(after(grad_x1.astype(BF16), placed[0]))
    grad_att = dot(grad_x1_all, w_out, NN).astype(BF16)
    grad_att, sums[0] = lax.optimization_barrier((grad_att, sums[0]))
    def enc_attend_back(qkv, lse, grad_att):
        gq, gkv, gb = attention_backward(
            enc_cfg, tp_arg, qkv, qkv, enc_idk, enc_idq, lse, grad_att, enc_bias
        )
        return columns([gq, gkv]), gb.reshape(heads, -1)

    def dec_attend_back(qkv, lse, grad_att):
        ordered = rows.to_rows(qkv, enc_count)
        lse = lse.reshape(-1)[: 3 * heads * DEC_LEN].reshape(3, heads, DEC_LEN)
        gq, gkv, gb = attention_backward(
            dec_cfg, tp_arg, ordered, ordered, dec_idk, dec_idq, lse,
            rows.to_rows(grad_att, enc_count), dec_bias,
        )
        gb = gb.reshape(heads, -1)
        return (
            rows.to_relative(columns([gq, gkv]), enc_count),
            jnp.pad(gb, ((0, 0), (0, enc_hot.shape[1] - gb.shape[1]))),
        )

    grad_qkv, grad_bias = lax.cond(is_enc, enc_attend_back, dec_attend_back, qkv, lse1, grad_att)
    (product,) = token_product(
        groups,
        (4 * width,),
        (0, norm1_all, grad_qkv),
        (0, grad_x1_all, att),
        (1, norm1_all, grad_qkv),
        (1, grad_x1_all, att),
    )
    placed["first"] = groups.to_place(product)
    sums[1] = groups.to_owner(after(placed[1], sums[0]))
    partial_n1 = dot(after(grad_qkv, product), w_qkv, NT).astype(BF16)
    partial_n1, sums[1] = lax.optimization_barrier((partial_n1, sums[1]))

    def while_n1(anchor):
        tables["grad"] = lax.cond(
            is_enc,
            lambda gb: bucket_sums(enc_hot, gb),
            lambda gb: bucket_sums(dec_hot, gb[:, : dec_hot.shape[1]]),
            after(grad_bias, anchor),
        )
        feed_out3 = dot(after(hidden3, tables["grad"]), feed_weights[2], NT).astype(BF16)
        queries["out"] = x2d + reduce_tokens(feed_out3, None, dec_groups)
        return feed_out3

    tables = {}
    sums[2] = groups.to_owner(after(placed[2], sums[1]))
    grad_n1 = reduce_tokens(partial_n1, while_n1)
    grad_step, gain_1 = norm_backward(x_f32, gain1, grad_n1)
    grad_x = grad_x1 + grad_step
    enc_first, dec_first = groups.to_owner(after(placed["first"], sums[2]))
    enc_cross, dec_cross = sums["cross"]
    (enc_gate, dec_gate), (enc_up, dec_up), (enc_down, dec_down) = sums[0], sums[1], sums[2]

    gain_rows = jnp.stack([gain_1, gain_2, jnp.where(is_enc, gain_ef, gain_d3)])
    gain_rows = gain_rows + core_swap(gain_rows)
    gain_rows = gain_rows + pair_swap(gain_rows)
    small = jnp.concatenate([gain_rows.reshape(-1), tables["grad"].reshape(-1)])
    length = small.shape[0]
    small = jnp.pad(small, (0, -length % 1024)).reshape(-1, 128)
    enc_small, dec_small = groups.all_role_sums(after(small, sums[2]))

    def unpack(total):
        flat = total.reshape(-1)
        gain = flat[: gain_rows.size].reshape(gain_rows.shape)
        share = gain.shape[1] // groups.count
        mine = lax.dynamic_slice_in_dim(gain, groups.where * share, share, axis=1)
        return mine, flat[gain_rows.size : length].reshape(BUCKETS, heads)

    enc_gains, enc_table_grad = unpack(enc_small)
    dec_gains, dec_table_grad = unpack(dec_small)

    def part(value, index):
        return value[:, index * width : (index + 1) * width]

    zero_bf = jnp.zeros((), BF16)
    return (
        jnp.where(is_enc, zero_bf, queries["out"].astype(BF16))[None],
        jnp.where(is_enc, grad_x.astype(BF16), zero_bf)[None],
        jnp.where(is_enc, zero_bf, grad_x[:dec_count].astype(BF16))[None],
        enc_gains[0],
        part(enc_first, 0),
        part(enc_first, 1),
        part(enc_first, 2),
        part(enc_first, 3).T,
        enc_table_grad,
        enc_gains[1],
        enc_gate[:, :units],
        enc_up[:, :units],
        enc_down[:, :units].T,
        enc_gains[2],
        dec_gains[0],
        part(dec_first, 0),
        part(dec_first, 1),
        part(dec_first, 2),
        part(dec_first, 3).T,
        dec_table_grad,
        dec_gains[1],
        part(dec_cross, 0),
        part(enc_cross, 0),
        part(enc_cross, 1),
        part(dec_cross, 1).T,
        dec_gains[2],
        dec_gate[:, :units],
        dec_up[:, :units],
        dec_down[:, :units].T,
    )


def solution(mesh):
    vector, matrix, turned = P("grp"), P("grp", "tp"), P("tp", "grp")
    tokens, ids, table = P("grp", "tp", None), P("grp", None, None), P(None, "tp")
    enc = (vector, matrix, matrix, matrix, turned, table, vector, matrix, matrix, turned, vector)
    dec = (vector, matrix, matrix, matrix, turned, table, vector, matrix, matrix, matrix, turned)
    dec = dec + (vector, matrix, matrix, turned)
    return jax.shard_map(
        body,
        mesh=mesh,
        in_specs=(tokens, tokens, tokens, ids, ids) + enc + dec,
        out_specs=(tokens, tokens, tokens) + enc + dec,
        check_vma=False,
    )
```
